32 devices in a mesh: dp: 8 (over y, x, core), tensor: 4 (over z).
Axes of the slice: x: 2, y: 2, z: 4, core: 2. Of those that a mesh axis runs over, the one named last changes fastest.
Arguments:
- activations: bfloat16 [4096, 8192], P('dp', 'tensor'), may hold values from -6 to 6
- out_grads: bfloat16 [4096, 28672], P('dp', 'tensor'), may hold values from -6 to 6
- input_proj: bfloat16 [8192, 64], P('tensor'), may hold values from -0.0625 to 0.0625
- grad_proj: bfloat16 [28672, 64], P('tensor'), may hold values from -4 to 4, as said below
- example_count: int32 [8], P('dp'), may hold values from 1 to 4, as said below
- child_order: int32 [8], replicated, may hold values 0 or 1
- prior_sketch: float32 [2048, 4096], P('dp', 'tensor'), may hold values from -6 to 6
- fold_map: float32 [256, 4], replicated, may hold values from -3 to 3
- merge_mix: float32 [256, 512], replicated, may hold values from -0.25 to 0.25
Outputs:
- merged_sketch: float32 [256, 4096], P(None, 'tensor')
- preconditioned: float32 [32, 4096], P('dp', 'tensor')
The draws below stay inside these ranges and needn't reach their ends.
Inputs may be any that keep to these rules, and one draw needn't show every extreme that they name: `example_count`: some data rank has exactly 4 live examples. `grad_proj`: entries within 26 / sqrt(28672) of zero.
All inputs are finite; a program needn't handle non-finite values.
Results may differ from the reference program's by a relative error of at most 0.0003.
Values sent between devices are 32-bit elements; how exact they have to be, the bound alone decides.
A program may use at most 64 MiB of HBM per device.

```python
import jax
import jax.numpy as jnp
import numpy as np
from jax import lax

D = 8192
FF = 28672
RANK = 64
PROJ = 4096
SKETCH = 256
SEQ = 128
EX_DEV = 4
EXAMPLES = 32
TOKENS = 4096
LEVELS = 3
N_DP = 8


def draw_grad_proj(key, part):
    key_base, key_jitter = jax.random.split(key, 2)
    base = jnp.clip(jax.random.normal(key_base, (FF, RANK), jnp.float32), -6.0, 6.0)
    rising = jnp.exp(jnp.log(3.0) * jnp.arange(RANK, dtype=jnp.float32) / (RANK - 1))
    jitter = jax.random.uniform(key_jitter, (RANK,), jnp.float32, 0.7, 1.4)
    return (base * rising * jitter / jnp.sqrt(jnp.float32(FF))).astype(jnp.bfloat16)


def draw_example_count(key, part):
    key_counts, key_pick = jax.random.split(jax.random.fold_in(key, 11), 2)
    counts = jax.random.randint(key_counts, (N_DP,), 1, EX_DEV + 1, dtype=jnp.int32)
    chosen = jax.random.randint(key_pick, (), 0, N_DP, dtype=jnp.int32)
    positions = jnp.arange(N_DP, dtype=jnp.int32)
    return jnp.where(positions == chosen, EX_DEV, counts).astype(jnp.int32)


def touch_ends(values, key, least, top_value):
    index_at = [jax.random.randint(jax.random.fold_in(key, axis), (), 0, length) for axis, length in enumerate(values.shape)]
    widest = values.shape.index(max(values.shape))
    next_to = index_at[:widest] + [(index_at[widest] + 1) % values.shape[widest]] + index_at[widest + 1:]
    return values.at[tuple(index_at)].set(least).at[tuple(next_to)].set(top_value)


def block_scale(rng, extent, shards, low, top_value):
    factor_of, own = 1.0, jax.random.fold_in(rng, 6)
    for axis_at, parts in shards:
        heights = jnp.exp(jax.random.uniform(jax.random.fold_in(own, axis_at), (parts,), jnp.float32, low / len(shards), top_value / len(shards)))
        factor_of = factor_of * jnp.repeat(heights, extent[axis_at] // parts).reshape([-1 if axis == axis_at else 1 for axis in range(len(extent))])
    return factor_of


def bell_draw(own_key, shape, width, bound, cuts=(), kind=jnp.bfloat16):
    result = width * jax.random.normal(own_key, shape, jnp.float32)
    if cuts:
        result = result * block_scale(own_key, shape, cuts, -0.22, 0.18)
    return jnp.clip(result, -bound, bound).astype(kind)


def setup_inputs(seed: int = 0) -> dict:
    key_of = jax.random.split(jax.random.key(seed), 10)
    return {
        "activations": bell_draw(key_of[0], (TOKENS, D), 1.0, 6.0, ((0, 8), (1, 4))),
        "out_grads": bell_draw(key_of[1], (TOKENS, FF), 1.0, 6.0, ((0, 8), (1, 4))),
        "input_proj": bell_draw(key_of[2], (D, RANK), D ** -0.5, 0.0625, ((0, 4),)),
        "grad_proj": draw_grad_proj(jax.random.fold_in(key_of[9], 71), 0),
        "example_count": draw_example_count(jax.random.fold_in(key_of[9], 71), 0),
        "child_order": touch_ends((jax.random.randint(key_of[5], (N_DP,), 0, 2) < 1).astype(jnp.int32), jax.random.fold_in(key_of[5], 1), 0, 1),
        "prior_sketch": bell_draw(key_of[6], (N_DP * SKETCH, PROJ), 1.0, 6.0, ((0, 8), (1, 4)), jnp.float32),
        "fold_map": bell_draw(key_of[7], (SKETCH, EX_DEV), EX_DEV ** -0.5, 3.0, (), jnp.float32),
        "merge_mix": bell_draw(key_of[8], (SKETCH, 2 * SKETCH), (2 * SKETCH) ** -0.5, 0.25, (), jnp.float32),
    }


def reference(activations, out_grads, input_proj, grad_proj, example_count, child_order, prior_sketch, fold_map, merge_mix):
    input_side = jnp.dot(activations.astype(jnp.float32), input_proj.astype(jnp.float32), preferred_element_type=jnp.float32)
    grad_side = jnp.dot(out_grads.astype(jnp.float32), grad_proj.astype(jnp.float32), preferred_element_type=jnp.float32)
    grad_blocks = grad_side.reshape(EXAMPLES, SEQ, RANK)
    input_blocks = input_side.reshape(EXAMPLES, SEQ, RANK)
    example_grad = jnp.einsum('eta,etb->eab', grad_blocks, input_blocks, precision=lax.Precision.HIGHEST)
    example_grad = example_grad.reshape(EXAMPLES, PROJ) / jnp.sqrt(jnp.float32(SEQ))
    slot_index = jnp.arange(EXAMPLES, dtype=jnp.int32)
    live = slot_index % EX_DEV < example_count[slot_index // EX_DEV]
    example_grad = jnp.where(live[:, None], example_grad, jnp.zeros_like(example_grad))
    grouped = example_grad.reshape(N_DP, EX_DEV, PROJ)
    nodes = prior_sketch.reshape(N_DP, SKETCH, PROJ) + jnp.einsum('sk,nkp->nsp', fold_map, grouped, precision=lax.Precision.HIGHEST)
    masses = lax.optimization_barrier(jnp.sum(nodes * nodes, axis=(1, 2)))
    mix_first = merge_mix[:, :SKETCH]
    mix_second = merge_mix[:, SKETCH:]
    for level_index in range(LEVELS):
        count_pairs = nodes.shape[0] // 2
        flag_index = np.arange(count_pairs) * 2 ** (level_index + 1) + 2 ** level_index - 1
        flips = child_order[flag_index] == 1
        lower_nodes = nodes[0::2]
        upper_nodes = nodes[1::2]
        first = jnp.where(flips[:, None, None], upper_nodes, lower_nodes)
        second = jnp.where(flips[:, None, None], lower_nodes, upper_nodes)
        first_mass = jnp.where(flips, masses[1::2], masses[0::2])
        second_mass = jnp.where(flips, masses[0::2], masses[1::2])
        mixture = jnp.einsum('sk,nkp->nsp', mix_first, first, precision=lax.Precision.HIGHEST) + jnp.einsum('sk,nkp->nsp', mix_second, second, precision=lax.Precision.HIGHEST)
        mix_total = lax.optimization_barrier(jnp.sum(mixture * mixture, axis=(1, 2)))
        masses = first_mass + second_mass
        nodes = mixture * jnp.sqrt(masses / (mix_total + 1e-06))[:, None, None]
    merged_sketch = nodes[0]
    gram = jnp.dot(merged_sketch, merged_sketch.T, precision=lax.Precision.HIGHEST)
    damping = jnp.trace(gram) / SKETCH
    system = gram + damping * jnp.eye(SKETCH, dtype=jnp.float32)
    sketch_grad = jnp.dot(merged_sketch, example_grad.T, precision=lax.Precision.HIGHEST)
    solved = jnp.linalg.solve(system, sketch_grad)
    preconditioned = example_grad - jnp.dot(solved.T, merged_sketch, precision=lax.Precision.HIGHEST)
    return (merged_sketch, preconditioned)
```

```python
import functools

import jax
import jax.numpy as jnp
from jax import lax
from jax.experimental import pallas as pl
from jax.experimental.pallas import tpu as pltpu
from jax.sharding import PartitionSpec as P

RANK = 64
SEQ = 128
LANES = 128
HIGHEST = lax.Precision.HIGHEST
MESH = pl.DeviceIdType.MESH


def newton_plan(rows):
    low, high = 0.999, (rows + 1) * 1.001
    first = 2.0 / (low + high)
    reach, scales = first * low, []
    while 1.0 - reach > 1e-3:
        grown = reach * (2.0 - reach)
        scale = 2.0 / (1.0 + grown)
        scales.append(scale)
        reach = grown * scale
    return first, scales


def dot_high(left, right):
    return jnp.dot(left, right, precision=HIGHEST, preferred_element_type=jnp.float32)


def dot_flip(left, right):
    return lax.dot_general(left, right, (((1,), (1,)), ((), ())), preferred_element_type=jnp.float32)


def dot_rows(left, right):
    return lax.dot_general(
        left, right, (((1,), (1,)), ((), ())), precision=HIGHEST, preferred_element_type=jnp.float32
    )


def halves(value):
    high = value.astype(jnp.bfloat16)
    return high, (value - high.astype(jnp.float32)).astype(jnp.bfloat16)


def dot_halves(left, right):
    (a, b), (c, d) = left, right
    out = jnp.dot(a, c, preferred_element_type=jnp.float32)
    out = out + jnp.dot(a, d, preferred_element_type=jnp.float32)
    return out + jnp.dot(b, c, preferred_element_type=jnp.float32)


def dot_mid(left, right):
    return dot_halves(halves(left), halves(right))


def dot_flip_halves(left, right):
    (a, b), (c, d) = left, right
    return dot_flip(jnp.concatenate([a, a, b], axis=1), jnp.concatenate([c, d, c], axis=1))


def dot_split(left, right):
    (a, b), (c, d) = left, right
    half = a.shape[1] // 2
    first = jnp.dot(
        jnp.concatenate([a, b[:, :half]], axis=1),
        jnp.concatenate([c, c[:half]], axis=0),
        preferred_element_type=jnp.float32,
    )
    second = jnp.dot(
        jnp.concatenate([a, b[:, half:]], axis=1),
        jnp.concatenate([d, c[half:]], axis=0),
        preferred_element_type=jnp.float32,
    )
    return first + second


def stacked(value, order):
    high = value.astype(jnp.bfloat16).astype(jnp.float32)
    both = (high, value - high)
    return jnp.concatenate([both[i] for i in order], axis=0)


def solve(gram, target):
    rows = gram.shape[0]
    eye = lax.broadcasted_iota(jnp.int32, gram.shape, 0) == lax.broadcasted_iota(jnp.int32, gram.shape, 1)
    trace = jnp.sum(
        jnp.sum(jnp.where(eye, gram, 0.0), axis=0, keepdims=True), axis=1, keepdims=True
    )
    unit = 1.0 / (trace / rows)
    system = gram * unit + jnp.where(eye, 1.0, 0.0)
    target = target * unit
    first, scales = newton_plan(rows)
    state, solved, path = first * system, first * target, None
    for index, scale in enumerate(scales):
        factor = jnp.where(eye, 2.0 * scale, 0.0) - scale * state
        factor_halves = halves(factor)
        solved = dot_split(halves(solved), factor_halves)
        if index < len(scales) - 1:
            state = dot_split(halves(state), factor_halves)
            if path is None:
                path = factor_halves[0]
            else:
                path = jnp.dot(path, factor_halves[0], preferred_element_type=jnp.float32)
                path = path.astype(jnp.bfloat16)
    high, low = halves(first * (target - dot_high(solved, system)))
    step = jnp.dot(high, path, preferred_element_type=jnp.float32)
    step = step + jnp.dot(low, path, preferred_element_type=jnp.float32)
    return solved + dot_split(halves(step), factor_halves)


def fused_kernel(
    n_dp,
    n_tp,
    act_hbm,
    out_hbm,
    wi_hbm,
    wo_hbm,
    count_ref,
    order_ref,
    prior_hbm,
    fold_hbm,
    mix_hbm,
    root_out,
    solved_out,
    grads_out,
    act,
    outg,
    wi,
    wo,
    prior,
    fold_ref,
    mix_ref,
    pair_in,
    node_send,
    node_recv,
    zsend,
    zrecv,
    full,
    grads,
    grads_rows,
    grads_all,
    sums_all,
    root,
    gram_part,
    gram_rs,
    gram_z,
    gram_all,
    load_sem,
    pair_sems,
    node_sems,
    root_sems,
    z_send,
    z_recv,
    p_send,
    p_recv,
    a_send,
    a_recv,
    out_sem,
    ready_sem,
):
    f32 = jnp.float32
    me, z = lax.axis_index("dp"), lax.axis_index("tensor")
    rows = prior.shape[0]
    part_rows = gram_z.shape[1]
    levels = n_dp.bit_length() - 1

    def dp_of(k):
        return lax.rem(me + k, n_dp)

    def tp_of(k):
        return lax.rem(z + k, n_tp)

    order = sorted(range(1, n_tp), key=lambda k: -min(k, n_tp - k)) + [0]
    loads = []

    def load(source, target):
        copy = pltpu.make_async_copy(source, target, load_sem.at[len(loads)])
        copy.start()
        loads.append(copy)
        return copy

    def load_chunk(index):
        span = pl.ds(pl.multiple_of(tp_of(order[index]) * SEQ, SEQ), SEQ)
        return load(act_hbm.at[span], act.at[index]), load(out_hbm.at[span], outg.at[index])

    weight_loads = [load(wi_hbm, wi), load(wo_hbm, wo)]
    chunk_loads = [load_chunk(0)]
    own_prior = load(prior_hbm, prior)
    mix_load = load(mix_hbm, mix_ref)
    chunk_loads += [load_chunk(index) for index in range(1, n_tp)]
    fold_load = load(fold_hbm, fold_ref)

    def tile_of(owner):
        return pl.ds(pl.multiple_of(owner * LANES, LANES), LANES)

    barrier = pltpu.get_barrier_semaphore()
    for k in range(1, n_tp):
        pl.semaphore_signal(barrier, inc=1, device_id={"tensor": tp_of(k)}, device_id_type=MESH)
    for k in range(1, n_dp):
        pl.semaphore_signal(barrier, inc=1, device_id={"dp": dp_of(k)}, device_id_type=MESH)
    pl.semaphore_wait(barrier, n_dp + n_tp - 2)
    for k in range(1, n_dp):
        pl.semaphore_signal(ready_sem, inc=1, device_id={"dp": dp_of(k)}, device_id_type=MESH)

    half = n_dp // 2
    core, chip = lax.rem(me, 2), me // 2
    partner = me + 1 - 2 * core
    chip_x = chip + 1 - 2 * lax.rem(chip, 2)
    chip_y = chip + 2 - 4 * (chip // 2)
    chip_d = half - 1 - chip

    def push(source, target, device, sems, index):
        copy = pltpu.make_async_remote_copy(
            src_ref=source,
            dst_ref=target,
            send_sem=sems.at[0, index],
            recv_sem=sems.at[1, index],
            device_id={"dp": device},
            device_id_type=MESH,
        )
        copy.start()
        return copy

    pair_copies = [
        push(prior_hbm.at[:, tile_of(2 * q + 1 - core)], pair_in.at[q], partner, pair_sems, q)
        for q in range(half)
    ]

    def exchange(axis, phase, source, target):
        size, other = (n_tp, tp_of) if axis == "tensor" else (n_dp, dp_of)
        send, recv = (z_send, z_recv) if axis == "tensor" else (p_send, p_recv)
        copies = []
        for k in range(1, size):
            copies.append(
                pltpu.make_async_remote_copy(
                    src_ref=source(other(k)),
                    dst_ref=target,
                    send_sem=send.at[phase, k],
                    recv_sem=recv.at[phase, k],
                    device_id={axis: other(k)},
                    device_id_type=MESH,
                )
            )
            copies[-1].start()
        return copies

    def exchange_all(phase, source, target):
        copies = []
        for j in sorted(range(n_tp), key=lambda j: -min(j, n_tp - j)):
            for k in range(n_dp):
                if j == 0 and k == 0:
                    continue
                copies.append(
                    pltpu.make_async_remote_copy(
                        src_ref=source(dp_of(k), tp_of(j)),
                        dst_ref=target,
                        send_sem=a_send.at[phase, j * n_dp + k],
                        recv_sem=a_recv.at[phase, j * n_dp + k],
                        device_id={"dp": dp_of(k), "tensor": tp_of(j)},
                        device_id_type=MESH,
                    )
                )
                copies[-1].start()
        return copies

    side_copies = []

    def do_chunk(index):
        k = order[index]
        for copy in chunk_loads[index]:
            copy.wait()
        mid = SEQ // 2
        right = [dot_flip(outg[index, h * mid : (h + 1) * mid], wo[...]) for h in range(2)]
        left = [dot_flip(act[index, h * mid : (h + 1) * mid], wi[...]) for h in range(2)]
        both = jnp.concatenate([jnp.concatenate(pair, axis=1) for pair in zip(left, right)], axis=0)
        if k == 0:
            zrecv[z] = both
            return
        zsend[index] = both
        copy = pltpu.make_async_remote_copy(
            src_ref=zsend.at[index],
            dst_ref=zrecv.at[z],
            send_sem=z_send.at[0, k],
            recv_sem=z_recv.at[0, k],
            device_id={"tensor": tp_of(k)},
            device_id_type=MESH,
        )
        copy.start()
        side_copies.append(copy)

    for copy in weight_loads:
        copy.wait()
    do_chunk(0)

    own_prior.wait()
    mix_load.wait()
    for copy in pair_copies:
        copy.wait()
    first_mix, second_mix = mix_ref[:, :rows], mix_ref[:, rows:]
    own_first = order_ref[2 * chip] == core
    own_half = [prior[:, tile_of(2 * q + core)] for q in range(half)]
    firsts = [jnp.where(own_first, own_half[q], pair_in[q]) for q in range(half)]
    seconds = [jnp.where(own_first, pair_in[q], own_half[q]) for q in range(half)]
    first_halves, second_halves = halves(first_mix), halves(second_mix)
    mixed = dot_halves(first_halves, halves(jnp.concatenate(firsts, axis=1)))
    mixed = mixed + dot_halves(second_halves, halves(jnp.concatenate(seconds, axis=1)))
    for q in range(half):
        node_send[q] = mixed[:, q * LANES : (q + 1) * LANES]
    node_copies = [
        push(node_send.at[other], node_recv.at[chip], 2 * other + core, node_sems, index)
        for index, other in enumerate((chip_x, chip_y, chip_d))
    ]
    node_recv[chip] = node_send[chip]
    for index in range(1, n_tp):
        do_chunk(index)

    fold_load.wait()
    fold_rows = fold_ref[...]
    paths = [[jnp.concatenate([dot_rows(fold_rows, first_mix), dot_rows(fold_rows, second_mix)], axis=0)]]
    for level in range(1, levels):
        paths.append(
            [dot_rows(p, first_mix) for p in paths[-1]] + [dot_rows(p, second_mix) for p in paths[-1]]
        )
    paths = [[stacked(p, (0, 0, 1)).T.astype(jnp.bfloat16) for p in level] for level in paths]
    fold = fold_rows.T

    for copy in side_copies:
        copy.wait()
    sides = zrecv[0]
    for index in range(1, n_tp):
        sides = sides + zrecv[index]
    lane = lax.broadcasted_iota(jnp.int32, sides.shape, 1)
    doubled = jnp.where(lane < RANK, sides, pltpu.roll(sides, RANK, 1))
    product = dot_mid(sides.T, doubled) / jnp.sqrt(f32(SEQ))
    product = jnp.where(z < count_ref[0], product, jnp.zeros_like(product))
    full[...] = product[RANK:]
    even = full[pl.ds(0, RANK // 2, stride=2), :]
    odd = full[pl.ds(1, RANK // 2, stride=2), :]
    lane = lax.broadcasted_iota(jnp.int32, even.shape, 1)
    mine = jnp.where(lane < RANK, even, odd)
    for row in range(n_tp * n_dp):
        grads_rows[row] = mine[row : row + 1]
    for index in range(n_tp):
        zsend[n_tp + index, 0:n_dp, :] = mine[index * n_dp : (index + 1) * n_dp]
    grads[z] = zsend[n_tp + z, 0:n_dp, :]
    slot = me * n_tp + z
    grads_all[slot] = grads_rows[z * n_dp + me]
    pl.semaphore_wait(ready_sem, n_dp - 1)
    grad_copies = exchange("tensor", 1, lambda t: zsend.at[n_tp + t, 0:n_dp, :], grads.at[z])
    row_copies = exchange_all(0, lambda d, t: grads_rows.at[t * n_dp + d], grads_all.at[slot])

    flags = [
        [order_ref[j * 2 ** (level + 1) + 2**level - 1] == 1 for j in range(n_dp >> (level + 1))]
        for level in range(levels)
    ]

    def pick(flip, lower, upper):
        first = [jnp.where(flip, b, a) for a, b in zip(lower, upper)]
        return first, [jnp.where(flip, a, b) for a, b in zip(lower, upper)]

    def total(value):
        return jnp.sum(jnp.sum(value, axis=0, keepdims=True), axis=1, keepdims=True)

    for copy in node_copies:
        copy.wait()
    mixtures = [[[node_recv[j]] for j in range(half)]]
    for level in range(1, levels):
        below = mixtures[-1]
        sides_of = [pick(flags[level][j], below[2 * j], below[2 * j + 1]) for j in range(len(below) // 2)]
        count = len(below[0])
        left = dot_halves(first_halves, halves(jnp.concatenate([v for f, _ in sides_of for v in f], axis=1)))
        right = dot_halves(second_halves, halves(jnp.concatenate([v for _, g in sides_of for v in g], axis=1)))
        mixtures.append(
            [
                [
                    side[:, (j * count + i) * LANES : (j * count + i + 1) * LANES]
                    for side in (left, right)
                    for i in range(count)
                ]
                for j in range(len(sides_of))
            ]
        )

    for copy in grad_copies:
        copy.wait()
    leaf_square = jnp.zeros((rows, LANES), f32)
    for tile in range(n_dp):
        leaf = prior[:, tile * LANES : (tile + 1) * LANES]
        for e in range(n_tp):
            step = grads[e, tile : tile + 1, :]
            grads_out[e : e + 1, tile * LANES : (tile + 1) * LANES] = step
            leaf = leaf + fold[:, e : e + 1] * step
        leaf_square = leaf_square + leaf * leaf
    own_mass = total(leaf_square)

    for copy in row_copies:
        copy.wait()
    steps_of = [
        [jnp.concatenate([grads_all[r * n_tp + e] for e in range(n_tp)], axis=0)] for r in range(n_dp)
    ]
    every = jnp.concatenate([step[0] for step in steps_of], axis=0)
    every_halves = halves(every)
    sums, products, nodes = [], [], []
    for level in range(levels):
        level_products, level_nodes, merged_steps = [], [], []
        for j in range(len(steps_of) // 2):
            first, second = pick(flags[level][j], steps_of[2 * j], steps_of[2 * j + 1])
            if level == 0:
                merged_steps.append([jnp.concatenate([first[0], second[0]], axis=0)])
            else:
                merged_steps.append(first + second)
        updates = [
            jnp.dot(
                path,
                jnp.concatenate([stacked(g[i], (0, 1, 0)) for g in merged_steps], axis=1).astype(jnp.bfloat16),
                preferred_element_type=f32,
            )
            for i, path in enumerate(paths[level])
        ]
        for j in range(len(merged_steps)):
            parts = [
                v + update[:, j * LANES : (j + 1) * LANES]
                for v, update in zip(mixtures[level][j], updates)
            ]
            index_of = {}
            for a in range(len(parts)):
                for b in range(a + 1):
                    index_of[a, b] = n_dp + len(sums)
                    sums.append(total(parts[a] * parts[b]))
            level_products.append(index_of)
            level_nodes.append(parts)
        steps_of = merged_steps
        products.append(level_products)
        nodes = level_nodes
    lane = lax.broadcasted_iota(jnp.int32, (1, LANES), 1)
    packed = jnp.where(lane == me, own_mass, jnp.zeros((1, LANES), f32))
    for index, value in enumerate(sums):
        packed = jnp.where(lane == n_dp + index, value, packed)
    sums_all[slot] = packed
    for copy in exchange_all(1, lambda d, t: sums_all.at[slot], sums_all.at[slot]):
        copy.wait()
    parts_of = [sums_all[index] for index in range(n_tp * n_dp)]
    while len(parts_of) > 1:
        parts_of = [a + b for a, b in zip(parts_of[0::2], parts_of[1::2])]
    packed = parts_of[0]

    def summed(index):
        return jnp.sum(jnp.where(lane == index, packed, 0.0), axis=1, keepdims=True)

    masses = [summed(index) for index in range(n_dp)]
    scales = [[jnp.ones((1, 1), f32)] for _ in range(n_dp)]
    for level in range(levels):
        new_masses, new_scales = [], []
        for j, products_of in enumerate(products[level]):
            flip = flags[level][j]
            lower, upper = scales[2 * j], scales[2 * j + 1]
            if level == 0:
                coefs = [jnp.ones((1, 1), f32)]
            else:
                coefs = [jnp.where(flip, b, a) for a, b in zip(lower, upper)]
                coefs += [jnp.where(flip, a, b) for a, b in zip(lower, upper)]
            square = jnp.zeros((1, 1), f32)
            for (a, b), index in products_of.items():
                term = coefs[a] * (coefs[b] * summed(index))
                square = square + (term if a == b else 2.0 * term)
            mass = masses[2 * j] + masses[2 * j + 1]
            scale = jnp.sqrt(mass / (jnp.maximum(square, 0.0) + 1e-06))
            new_masses.append(mass)
            new_scales.append([scale * c for c in coefs])
        masses, scales = new_masses, new_scales
    chunk = scales[0][0] * nodes[0][0]
    for c, part in zip(scales[0][1:], nodes[0][1:]):
        chunk = chunk + c * part
    root[:, tile_of(me)] = chunk

    chunk_halves = halves(chunk)
    upper_halves, lower_halves = [[v[s] for v in chunk_halves] for s in (slice(0, LANES), slice(LANES, rows))]
    targets = dot_flip_halves(every_halves, chunk_halves)
    triangle = jnp.concatenate(
        [
            dot_flip_halves(chunk_halves, upper_halves),
            dot_flip_halves(lower_halves, lower_halves),
            targets[:, :LANES],
            targets[:, LANES:],
        ],
        axis=0,
    )
    for r in range(n_dp):
        gram_part[r] = triangle[r * part_rows : (r + 1) * part_rows]
    gram_rs[me] = gram_part[me]
    gram_copies = exchange("dp", 0, lambda t: gram_part.at[t], gram_rs.at[me])
    dev_x, dev_y, dev_d = (2 * other + core for other in (chip_x, chip_y, chip_d))
    upper, lower = pl.ds(0, rows // 2), pl.ds(rows // 2, rows // 2)

    def relay(index, owner, device, span=slice(None)):
        block_of = root.at[span, tile_of(owner)]
        return push(block_of, block_of, device, root_sems, index)

    relays = [relay(0, me, dev_x), relay(1, me, dev_y), relay(2, me, partner)]
    for copy in gram_copies:
        copy.wait()
    part = gram_rs[0]
    for index in range(1, n_dp):
        part = part + gram_rs[index]
    gram_z[z] = part
    z_copies = exchange("tensor", 2, lambda t: gram_z.at[z], gram_z.at[z])
    relays[0].wait_recv()
    relays.append(relay(3, dev_x, dev_y, upper))
    relays.append(relay(4, dev_x, partner))
    relays[1].wait_recv()
    relays.append(relay(5, dev_y, dev_x, lower))
    relays.append(relay(6, dev_y, partner))
    for copy in z_copies:
        copy.wait()
    part = gram_z[0]
    for index in range(1, n_tp):
        part = part + gram_z[index]
    gram_all[me] = part
    gram_copies = exchange("dp", 1, lambda t: gram_all.at[me], gram_all.at[me])
    relays[3].wait_recv()
    relays[5].wait_recv()
    relays.append(relay(7, dev_d, partner))
    for copy in gram_copies:
        copy.wait()
    triangle = jnp.concatenate([gram_all[r] for r in range(n_dp)], axis=0)
    corner = triangle[LANES:rows]
    gram = jnp.concatenate(
        [
            jnp.concatenate([triangle[:LANES], corner.T], axis=1),
            jnp.concatenate([corner, triangle[rows : rows + LANES]], axis=1),
        ],
        axis=0,
    )
    targets = triangle[rows + LANES :]
    target = jnp.zeros((n_tp, rows), f32)
    for r in range(n_dp):
        span = slice(r * n_tp, (r + 1) * n_tp)
        both = [targets[: n_dp * n_tp][span], targets[n_dp * n_tp :][span]]
        target = jnp.where(me == r, jnp.concatenate(both, axis=1), target)
    solved_out[...] = solve(gram, target)
    for index, copy in enumerate(relays):
        copy.wait_send()
        if index not in (0, 1, 3, 5):
            copy.wait_recv()
    root_write = pltpu.make_async_copy(root, root_out, out_sem.at[0])
    root_write.start()
    root_write.wait()


def last_kernel(root_ref, solved_ref, grads_ref, root_out, pre_out, sem):
    write = pltpu.make_async_copy(root_ref, root_out, sem.at[0])
    write.start()
    pre_out[...] = grads_ref[...] - dot_mid(solved_ref[...], root_ref[...])
    write.wait()


def fused_body(
    activations,
    out_grads,
    input_proj,
    grad_proj,
    example_count,
    child_order,
    prior_sketch,
    fold_map,
    merge_mix,
):
    n_dp, n_tp = lax.axis_size("dp"), lax.axis_size("tensor")
    rows, columns = prior_sketch.shape
    slots = activations.shape[0] // SEQ
    f32, bf16 = jnp.float32, jnp.bfloat16
    width, hidden = activations.shape[1], out_grads.shape[1]
    hbm = pl.BlockSpec(memory_space=pltpu.HBM)
    anywhere = pl.BlockSpec(memory_space=pl.ANY)
    vmem = pl.BlockSpec(memory_space=pltpu.VMEM)
    smem = pl.BlockSpec(memory_space=pltpu.SMEM)
    devices = n_dp * n_tp
    part_rows = (3 * LANES + 2 * n_dp * slots) // n_dp
    pin = functools.partial(pltpu.with_memory_space_constraint, memory_space=pltpu.HBM)
    root, solved, grads = pl.pallas_call(
        functools.partial(fused_kernel, n_dp, n_tp),
        out_shape=(
            jax.ShapeDtypeStruct((rows, columns), f32),
            jax.ShapeDtypeStruct((slots, rows), f32),
            jax.ShapeDtypeStruct((slots, columns), f32),
        ),
        in_specs=[hbm, hbm, hbm, hbm, smem, smem, hbm, hbm, hbm],
        out_specs=(anywhere, vmem, vmem),
        scratch_shapes=[
            pltpu.VMEM((slots, SEQ, width), bf16),
            pltpu.VMEM((slots, SEQ, hidden), bf16),
            pltpu.VMEM((RANK, width), bf16),
            pltpu.VMEM((RANK, hidden), bf16),
            pltpu.VMEM((rows, columns), f32),
            pltpu.VMEM((slots, rows), f32),
            pltpu.VMEM((rows, 2 * rows), f32),
            pltpu.VMEM((n_dp // 2, rows, LANES), f32),
            pltpu.VMEM((n_dp // 2, rows, LANES), f32),
            pltpu.VMEM((n_dp // 2, rows, LANES), f32),
            pltpu.VMEM((2 * n_tp, SEQ, LANES), f32),
            pltpu.VMEM((n_tp, SEQ, LANES), f32),
            pltpu.VMEM((RANK, LANES), f32),
            pltpu.VMEM((n_tp, n_dp, LANES), f32),
            pltpu.VMEM((devices, 1, LANES), f32),
            pltpu.VMEM((devices, 1, LANES), f32),
            pltpu.VMEM((devices, 1, LANES), f32),
            pltpu.VMEM((rows, columns), f32),
            pltpu.VMEM((n_dp, part_rows, LANES), f32),
            pltpu.VMEM((n_dp, part_rows, LANES), f32),
            pltpu.VMEM((n_tp, part_rows, LANES), f32),
            pltpu.VMEM((n_dp, part_rows, LANES), f32),
            pltpu.SemaphoreType.DMA((5 + 2 * n_tp,)),
            pltpu.SemaphoreType.DMA((2, n_dp // 2)),
            pltpu.SemaphoreType.DMA((2, 3)),
            pltpu.SemaphoreType.DMA((2, 8)),
            pltpu.SemaphoreType.DMA((3, n_tp)),
            pltpu.SemaphoreType.DMA((3, n_tp)),
            pltpu.SemaphoreType.DMA((2, n_dp)),
            pltpu.SemaphoreType.DMA((2, n_dp)),
            pltpu.SemaphoreType.DMA((2, devices)),
            pltpu.SemaphoreType.DMA((2, devices)),
            pltpu.SemaphoreType.DMA((1,)),
            pltpu.SemaphoreType.REGULAR,
        ],
        compiler_params=pltpu.CompilerParams(
            collective_id=0, has_side_effects=True, vmem_limit_bytes=32 * 2**20
        ),
    )(
        pin(activations),
        pin(out_grads),
        pin(input_proj.T),
        pin(grad_proj.T),
        example_count,
        child_order,
        pin(prior_sketch),
        pin(fold_map.T),
        pin(merge_mix),
    )
    return pl.pallas_call(
        last_kernel,
        out_shape=(
            jax.ShapeDtypeStruct((rows, columns), f32),
            jax.ShapeDtypeStruct((slots, columns), f32),
        ),
        in_specs=[vmem] * 3,
        out_specs=(anywhere, vmem),
        scratch_shapes=[pltpu.SemaphoreType.DMA((1,))],
        compiler_params=pltpu.CompilerParams(vmem_limit_bytes=16 * 2**20),
    )(root, solved, grads)


def from_partner(value, axis, stride):
    mask = 2**stride
    pairs = [(source, source ^ mask) for source in range(lax.axis_size(axis))]
    return lax.ppermute(value, axis, pairs)


def body(
    activations,
    out_grads,
    input_proj,
    grad_proj,
    example_count,
    child_order,
    prior_sketch,
    fold_map,
    merge_mix,
):
    tensor_count = lax.axis_size("tensor")
    own_rank = RANK // tensor_count
    example_slots = activations.shape[0] // SEQ
    sketch_rows = prior_sketch.shape[0]
    input_part = jnp.dot(activations, input_proj, preferred_element_type=jnp.float32)
    grad_part = jnp.dot(out_grads, grad_proj, preferred_element_type=jnp.float32)
    input_side, grad_side = lax.psum((input_part, grad_part), "tensor")
    grad_own = lax.dynamic_slice_in_dim(grad_side, lax.axis_index("tensor") * own_rank, own_rank, 1)
    grad_blocks = grad_own.reshape(example_slots, SEQ, own_rank)
    input_blocks = input_side.reshape(example_slots, SEQ, RANK)
    example_grad = jnp.einsum(
        "eta,etb->eab", grad_blocks, input_blocks, precision=lax.Precision.HIGHEST
    )
    example_grad = example_grad.reshape(example_slots, own_rank * RANK) / jnp.sqrt(jnp.float32(SEQ))
    live = jnp.arange(example_slots, dtype=jnp.int32) < example_count[0]
    example_grad = jnp.where(live[:, None], example_grad, jnp.zeros_like(example_grad))
    leaf_node = prior_sketch + jnp.dot(fold_map, example_grad, precision=lax.Precision.HIGHEST)
    leaf_weight = lax.psum(jnp.sum(leaf_node * leaf_node), "tensor")
    mix_first = merge_mix[:, :sketch_rows]
    mix_second = merge_mix[:, sketch_rows:]
    depth_count = lax.axis_size("dp").bit_length() - 1
    rank_index = lax.axis_index("dp")
    sketch_node = leaf_node
    sketch_weight = leaf_weight
    for level_index in range(depth_count):
        sibling_node, sibling_weight = from_partner((sketch_node, sketch_weight), "dp", level_index)
        upper_half = rank_index >> level_index & 1
        block_start = rank_index >> level_index + 1 << level_index + 1
        flip_order = child_order[block_start + (1 << level_index) - 1]
        own_first = upper_half == flip_order
        first = jnp.where(own_first, sketch_node, sibling_node)
        second = jnp.where(own_first, sibling_node, sketch_node)
        first_weight = jnp.where(own_first, sketch_weight, sibling_weight)
        second_weight = jnp.where(own_first, sibling_weight, sketch_weight)
        mixture = jnp.dot(mix_first, first, precision=lax.Precision.HIGHEST) + jnp.dot(
            mix_second, second, precision=lax.Precision.HIGHEST
        )
        mix_total = lax.psum(jnp.sum(mixture * mixture), "tensor")
        sketch_weight = first_weight + second_weight
        sketch_node = mixture * jnp.sqrt(sketch_weight / (mix_total + 1e-06))
    gram_part = jnp.dot(sketch_node, sketch_node.T, precision=lax.Precision.HIGHEST)
    product_part = jnp.dot(sketch_node, example_grad.T, precision=lax.Precision.HIGHEST)
    gram, sketch_grad = lax.psum((gram_part, product_part), "tensor")
    damping = jnp.trace(gram) / sketch_rows
    system = gram + damping * jnp.eye(sketch_rows, dtype=jnp.float32)
    factor = jnp.linalg.cholesky(system)
    solved = jax.scipy.linalg.cho_solve((factor, True), sketch_grad)
    preconditioned = example_grad - jnp.dot(solved.T, sketch_node, precision=lax.Precision.HIGHEST)
    return (sketch_node, preconditioned)


def fits_fused(rows, columns, slots, n_dp, n_tp):
    return (
        columns == n_dp * LANES
        and slots == n_tp
        and 2 * RANK == LANES
        and n_dp == 8
        and rows == 2 * LANES
        and (3 * LANES + 2 * n_dp * slots) % (8 * n_dp) == 0
    )


def step(*args):
    n_dp, n_tp = lax.axis_size("dp"), lax.axis_size("tensor")
    slots = args[0].shape[0] // SEQ
    rows, columns = args[6].shape
    if fits_fused(rows, columns, slots, n_dp, n_tp):
        return fused_body(*args)
    return body(*args)


def solution(mesh):
    in_specs = (
        P("dp", "tensor"),
        P("dp", "tensor"),
        P("tensor", None),
        P("tensor", None),
        P("dp"),
        P(),
        P("dp", "tensor"),
        P(),
        P(),
    )
    out_specs = (P(None, "tensor"), P("dp", "tensor"))
    return jax.shard_map(step, mesh=mesh, in_specs=in_specs, out_specs=out_specs, check_vma=False)
```

```python
import functools

import jax
import jax.numpy as jnp
from jax import lax
from jax.experimental import pallas as pl
from jax.experimental.pallas import tpu as pltpu
from jax.sharding import PartitionSpec as P

RANK = 64
SEQ = 128
LANES = 128
HIGHEST = lax.Precision.HIGHEST
MESH = pl.DeviceIdType.MESH


def newton_plan(rows):
    low, high = 0.999, (rows + 1) * 1.001
    first = 2.0 / (low + high)
    reach, scales = first * low, []
    while 1.0 - reach > 1e-3:
        grown = reach * (2.0 - reach)
        scale = 2.0 / (1.0 + grown)
        scales.append(scale)
        reach = grown * scale
    return first, scales


def dot_high(left, right):
    return jnp.dot(left, right, precision=HIGHEST, preferred_element_type=jnp.float32)


def dot_flip(left, right):
    return lax.dot_general(left, right, (((1,), (1,)), ((), ())), preferred_element_type=jnp.float32)


def dot_rows(left, right):
    return lax.dot_general(
        left, right, (((1,), (1,)), ((), ())), precision=HIGHEST, preferred_element_type=jnp.float32
    )


def halves(value):
    high = value.astype(jnp.bfloat16)
    return high, (value - high.astype(jnp.float32)).astype(jnp.bfloat16)


def dot_halves(left, right):
    (a, b), (c, d) = left, right
    out = jnp.dot(a, c, preferred_element_type=jnp.float32)
    out = out + jnp.dot(a, d, preferred_element_type=jnp.float32)
    return out + jnp.dot(b, c, preferred_element_type=jnp.float32)


def dot_mid(left, right):
    return dot_halves(halves(left), halves(right))


def dot_flip_halves(left, right):
    (a, b), (c, d) = left, right
    return dot_flip(jnp.concatenate([a, a, b], axis=1), jnp.concatenate([c, d, c], axis=1))


def dot_split(left, right):
    (a, b), (c, d) = left, right
    half = a.shape[1] // 2
    first = jnp.dot(
        jnp.concatenate([a, b[:, :half]], axis=1),
        jnp.concatenate([c, c[:half]], axis=0),
        preferred_element_type=jnp.float32,
    )
    second = jnp.dot(
        jnp.concatenate([a, b[:, half:]], axis=1),
        jnp.concatenate([d, c[half:]], axis=0),
        preferred_element_type=jnp.float32,
    )
    return first + second


def stacked(value, order):
    high = value.astype(jnp.bfloat16).astype(jnp.float32)
    both = (high, value - high)
    return jnp.concatenate([both[i] for i in order], axis=0)


def solve(gram, target):
    rows = gram.shape[0]
    eye = lax.broadcasted_iota(jnp.int32, gram.shape, 0) == lax.broadcasted_iota(jnp.int32, gram.shape, 1)
    trace = jnp.sum(
        jnp.sum(jnp.where(eye, gram, 0.0), axis=0, keepdims=True), axis=1, keepdims=True
    )
    unit = 1.0 / (trace / rows)
    system = gram * unit + jnp.where(eye, 1.0, 0.0)
    target = target * unit
    first, scales = newton_plan(rows)
    state, solved, path = first * system, first * target, None
    for index, scale in enumerate(scales):
        factor = jnp.where(eye, 2.0 * scale, 0.0) - scale * state
        factor_halves = halves(factor)
        solved = dot_split(halves(solved), factor_halves)
        if index < len(scales) - 1:
            state = dot_split(halves(state), factor_halves)
            if path is None:
                path = factor_halves[0]
            else:
                path = jnp.dot(path, factor_halves[0], preferred_element_type=jnp.float32)
                path = path.astype(jnp.bfloat16)
    high, low = halves(first * (target - dot_high(solved, system)))
    step = jnp.dot(high, path, preferred_element_type=jnp.float32)
    step = step + jnp.dot(low, path, preferred_element_type=jnp.float32)
    return solved + dot_split(halves(step), factor_halves)


def fused_kernel(
    n_dp,
    n_tp,
    act_hbm,
    out_hbm,
    wi_hbm,
    wo_hbm,
    count_ref,
    order_hbm,
    prior_hbm,
    fold_hbm,
    mix_hbm,
    root_out,
    gram_out,
    target_out,
    grads_out,
    tokens,
    weights,
    order_ref,
    prior,
    fold_ref,
    mix_ref,
    pair_in,
    node_send,
    node_recv,
    zsend,
    zmid,
    zrecv,
    full,
    slices_send,
    grads,
    grads_rows,
    grads_all,
    sums_all,
    root,
    gram_part,
    gram_rs,
    gram_z,
    gram_all,
    load_sem,
    sems,
    root_sems,
    out_sem,
    ready_sem,
):
    f32 = jnp.float32
    me, z = lax.axis_index("dp"), lax.axis_index("tensor")
    rows = prior.shape[0]
    part_rows = gram_z.shape[1]
    levels = n_dp.bit_length() - 1

    def dp_of(k):
        return lax.rem(me + k, n_dp)

    def tp_of(k):
        return lax.rem(z + k, n_tp)

    width = act_hbm.shape[1]
    near = z + 1 - 2 * lax.rem(z, 2)
    far = z + 2 - 4 * (z // 2)
    diagonal = near + 2 - 4 * (near // 2)
    order = (diagonal, far, near, z)
    used = []

    def load(*pairs):
        for source, target in pairs:
            pltpu.make_async_copy(source, target, load_sem.at[len(used)]).start()
        used.append(None)
        return len(used) - 1

    def drain(ref, sem):
        pltpu.make_async_copy(ref, ref, sem).wait()

    def load_chunk(index):
        span = pl.ds(pl.multiple_of(order[index] * SEQ, SEQ), SEQ)
        into = tokens.at[index]
        return load((act_hbm.at[span], into.at[:, :width]), (out_hbm.at[span], into.at[:, width:]))

    order_load = load((order_hbm, order_ref))
    weight_load = load((wi_hbm, weights.at[:, :width]), (wo_hbm, weights.at[:, width:]))
    chunk_loads = [load_chunk(0)]
    prior_load = load((prior_hbm, prior))
    mix_load = load((mix_hbm, mix_ref))
    chunk_loads += [load_chunk(index) for index in range(1, n_tp)]
    fold_load = load((fold_hbm, fold_ref))

    def tile_of(owner):
        return pl.ds(pl.multiple_of(owner * LANES, LANES), LANES)

    barrier = pltpu.get_barrier_semaphore()
    for k in range(1, n_tp):
        pl.semaphore_signal(barrier, inc=1, device_id={"tensor": tp_of(k)}, device_id_type=MESH)
    for k in range(1, n_dp):
        pl.semaphore_signal(barrier, inc=1, device_id={"dp": dp_of(k)}, device_id_type=MESH)
    pl.semaphore_wait(barrier, n_dp + n_tp - 2)
    for k in range(1, n_dp):
        pl.semaphore_signal(ready_sem, inc=1, device_id={"dp": dp_of(k)}, device_id_type=MESH)

    half = n_dp // 2
    core, chip = lax.rem(me, 2), me // 2
    partner = me + 1 - 2 * core
    chip_x = chip + 1 - 2 * lax.rem(chip, 2)
    chip_y = chip + 2 - 4 * (chip // 2)
    chip_d = half - 1 - chip

    PAIR, NODE, MID, SIDE, SLICE, ROW, SUM, SCATTER, ALONG, GATHER = range(10)

    def push(phase, source, target, **device):
        pltpu.make_async_remote_copy(
            src_ref=source,
            dst_ref=target,
            send_sem=sems.at[0, phase],
            recv_sem=sems.at[1, phase],
            device_id=device,
            device_id_type=MESH,
        ).start()

    def received(phase, ref):
        drain(ref, sems.at[1, phase])

    for q in range(half):
        push(PAIR, prior_hbm.at[:, tile_of(2 * q + 1 - core)], pair_in.at[q], dp=partner)

    def exchange(axis, phase, source, target):
        size, other = (n_tp, tp_of) if axis == "tensor" else (n_dp, dp_of)
        for k in range(1, size):
            push(phase, source(other(k)), target, **{axis: other(k)})

    def exchange_all(phase, source, target):
        for j in sorted(range(n_tp), key=lambda j: -min(j, n_tp - j)):
            for k in range(n_dp):
                if (j, k) != (0, 0):
                    push(phase, source(dp_of(k), tp_of(j)), target, dp=dp_of(k), tensor=tp_of(j))

    def sides_of_chunk(index):
        drain(tokens.at[index], load_sem.at[chunk_loads[index]])
        mid = SEQ // 2
        spans = [slice(h * mid, (h + 1) * mid) for h in range(2)]
        right = [dot_flip(tokens[index, span, width:], weights[:, width:]) for span in spans]
        left = [dot_flip(tokens[index, span, :width], weights[:, :width]) for span in spans]
        return jnp.concatenate([jnp.concatenate(pair, axis=1) for pair in zip(left, right)], axis=0)

    drain(weights, load_sem.at[weight_load])
    zsend[0] = sides_of_chunk(0)
    push(MID, zsend.at[0], zmid, tensor=near)

    drain(order_ref, load_sem.at[order_load])
    drain(prior, load_sem.at[prior_load])
    drain(mix_ref, load_sem.at[mix_load])
    received(PAIR, pair_in)
    first_mix, second_mix = mix_ref[:, :rows], mix_ref[:, rows:]
    own_first = order_ref[0, 2 * chip] == core
    own_half = [prior[:, tile_of(2 * q + core)] for q in range(half)]
    firsts = [jnp.where(own_first, own_half[q], pair_in[q]) for q in range(half)]
    seconds = [jnp.where(own_first, pair_in[q], own_half[q]) for q in range(half)]
    first_halves, second_halves = halves(first_mix), halves(second_mix)
    mixed = dot_halves(first_halves, halves(jnp.concatenate(firsts, axis=1)))
    mixed = mixed + dot_halves(second_halves, halves(jnp.concatenate(seconds, axis=1)))
    for q in range(half):
        node_send[q] = mixed[:, q * LANES : (q + 1) * LANES]
    for other in (chip_x, chip_y, chip_d):
        push(NODE, node_send.at[other], node_recv.at[chip], dp=2 * other + core)
    node_recv[chip] = node_send[chip]
    far_sides = sides_of_chunk(1)
    zsend[2] = sides_of_chunk(2)
    received(MID, zmid)
    zsend[1] = far_sides + zmid[...]
    push(SIDE, zsend.at[1], zrecv.at[1], tensor=far)
    push(SIDE, zsend.at[2], zrecv.at[0], tensor=near)
    own_sides = sides_of_chunk(3)

    drain(fold_ref, load_sem.at[fold_load])
    fold_rows = fold_ref[...]
    paths = [[jnp.concatenate([dot_rows(fold_rows, first_mix), dot_rows(fold_rows, second_mix)], axis=0)]]
    for level in range(1, levels):
        paths.append(
            [dot_rows(p, first_mix) for p in paths[-1]] + [dot_rows(p, second_mix) for p in paths[-1]]
        )
    paths = [[stacked(p, (0, 0, 1)).T.astype(jnp.bfloat16) for p in level] for level in paths]
    fold = fold_rows.T

    received(SIDE, zrecv)
    sides = (own_sides + zrecv[0]) + zrecv[1]
    lane = lax.broadcasted_iota(jnp.int32, sides.shape, 1)
    doubled = jnp.where(lane < RANK, sides, pltpu.roll(sides, RANK, 1))
    product = dot_mid(sides.T, doubled) / jnp.sqrt(f32(SEQ))
    product = jnp.where(z < count_ref[0], product, jnp.zeros_like(product))
    full[...] = product[RANK:]
    even = full[pl.ds(0, RANK // 2, stride=2), :]
    odd = full[pl.ds(1, RANK // 2, stride=2), :]
    lane = lax.broadcasted_iota(jnp.int32, even.shape, 1)
    mine = jnp.where(lane < RANK, even, odd)
    for row in range(n_tp * n_dp):
        grads_rows[row] = mine[row : row + 1]
    for index in range(n_tp):
        slices_send[index] = mine[index * n_dp : (index + 1) * n_dp]
    grads[z] = slices_send[z]
    slot = me * n_tp + z
    grads_all[slot] = grads_rows[z * n_dp + me]
    pl.semaphore_wait(ready_sem, n_dp - 1)
    exchange("tensor", SLICE, lambda t: slices_send.at[t], grads.at[z])
    exchange_all(ROW, lambda d, t: grads_rows.at[t * n_dp + d], grads_all.at[slot])

    flags = [
        [order_ref[0, j * 2 ** (level + 1) + 2**level - 1] == 1 for j in range(n_dp >> (level + 1))]
        for level in range(levels)
    ]

    def pick(flip, lower, upper):
        first = [jnp.where(flip, b, a) for a, b in zip(lower, upper)]
        return first, [jnp.where(flip, a, b) for a, b in zip(lower, upper)]

    def total(value):
        return jnp.sum(jnp.sum(value, axis=0, keepdims=True), axis=1, keepdims=True)

    received(NODE, node_recv.at[: half - 1])
    mixtures = [[[node_recv[j]] for j in range(half)]]
    for level in range(1, levels):
        below = mixtures[-1]
        sides_of = [pick(flags[level][j], below[2 * j], below[2 * j + 1]) for j in range(len(below) // 2)]
        count = len(below[0])
        left = dot_halves(first_halves, halves(jnp.concatenate([v for f, _ in sides_of for v in f], axis=1)))
        right = dot_halves(second_halves, halves(jnp.concatenate([v for _, g in sides_of for v in g], axis=1)))
        mixtures.append(
            [
                [
                    side[:, (j * count + i) * LANES : (j * count + i + 1) * LANES]
                    for side in (left, right)
                    for i in range(count)
                ]
                for j in range(len(sides_of))
            ]
        )

    received(SLICE, grads.at[: n_tp - 1])
    leaf_square = jnp.zeros((rows, LANES), f32)
    for tile in range(n_dp):
        leaf = prior[:, tile * LANES : (tile + 1) * LANES]
        for e in range(n_tp):
            step = grads[e, tile : tile + 1, :]
            grads_out[e : e + 1, tile * LANES : (tile + 1) * LANES] = step
            leaf = leaf + fold[:, e : e + 1] * step
        leaf_square = leaf_square + leaf * leaf
    own_mass = total(leaf_square)

    received(ROW, grads_all.at[: n_tp * n_dp - 1])
    steps_of = [
        [jnp.concatenate([grads_all[r * n_tp + e] for e in range(n_tp)], axis=0)] for r in range(n_dp)
    ]
    every = jnp.concatenate([step[0] for step in steps_of], axis=0)
    every_halves = halves(every)
    sums, products, nodes = [], [], []
    for level in range(levels):
        level_products, level_nodes, merged_steps = [], [], []
        for j in range(len(steps_of) // 2):
            first, second = pick(flags[level][j], steps_of[2 * j], steps_of[2 * j + 1])
            if level == 0:
                merged_steps.append([jnp.concatenate([first[0], second[0]], axis=0)])
            else:
                merged_steps.append(first + second)
        updates = [
            jnp.dot(
                path,
                jnp.concatenate([stacked(g[i], (0, 1, 0)) for g in merged_steps], axis=1).astype(jnp.bfloat16),
                preferred_element_type=f32,
            )
            for i, path in enumerate(paths[level])
        ]
        for j in range(len(merged_steps)):
            parts = [
                v + update[:, j * LANES : (j + 1) * LANES]
                for v, update in zip(mixtures[level][j], updates)
            ]
            index_of = {}
            for a in range(len(parts)):
                for b in range(a + 1):
                    index_of[a, b] = n_dp + len(sums)
                    sums.append(total(parts[a] * parts[b]))
            level_products.append(index_of)
            level_nodes.append(parts)
        steps_of = merged_steps
        products.append(level_products)
        nodes = level_nodes
    lane = lax.broadcasted_iota(jnp.int32, (1, LANES), 1)
    packed = jnp.where(lane == me, own_mass, jnp.zeros((1, LANES), f32))
    for index, value in enumerate(sums):
        packed = jnp.where(lane == n_dp + index, value, packed)
    sums_all[slot] = packed
    exchange_all(SUM, lambda d, t: sums_all.at[slot], sums_all.at[slot])
    received(SUM, sums_all.at[: n_tp * n_dp - 1])
    parts_of = [sums_all[index] for index in range(n_tp * n_dp)]
    while len(parts_of) > 1:
        parts_of = [a + b for a, b in zip(parts_of[0::2], parts_of[1::2])]
    packed = parts_of[0]

    def summed(index):
        return jnp.sum(jnp.where(lane == index, packed, 0.0), axis=1, keepdims=True)

    masses = [summed(index) for index in range(n_dp)]
    scales = [[jnp.ones((1, 1), f32)] for _ in range(n_dp)]
    for level in range(levels):
        new_masses, new_scales = [], []
        for j, products_of in enumerate(products[level]):
            flip = flags[level][j]
            lower, upper = scales[2 * j], scales[2 * j + 1]
            if level == 0:
                coefs = [jnp.ones((1, 1), f32)]
            else:
                coefs = [jnp.where(flip, b, a) for a, b in zip(lower, upper)]
                coefs += [jnp.where(flip, a, b) for a, b in zip(lower, upper)]
            square = jnp.zeros((1, 1), f32)
            for (a, b), index in products_of.items():
                term = coefs[a] * (coefs[b] * summed(index))
                square = square + (term if a == b else 2.0 * term)
            mass = masses[2 * j] + masses[2 * j + 1]
            scale = jnp.sqrt(mass / (jnp.maximum(square, 0.0) + 1e-06))
            new_masses.append(mass)
            new_scales.append([scale * c for c in coefs])
        masses, scales = new_masses, new_scales
    chunk = scales[0][0] * nodes[0][0]
    for c, part in zip(scales[0][1:], nodes[0][1:]):
        chunk = chunk + c * part
    root[:, tile_of(me)] = chunk

    chunk_halves = halves(chunk)
    upper_halves, lower_halves = [[v[s] for v in chunk_halves] for s in (slice(0, LANES), slice(LANES, rows))]
    targets = dot_flip_halves(every_halves, chunk_halves)
    triangle = jnp.concatenate(
        [
            dot_flip_halves(chunk_halves, upper_halves),
            dot_flip_halves(lower_halves, lower_halves),
            targets[:, :LANES],
            targets[:, LANES:],
        ],
        axis=0,
    )
    for r in range(n_dp):
        gram_part[r] = triangle[r * part_rows : (r + 1) * part_rows]
    gram_rs[me] = gram_part[me]
    exchange("dp", SCATTER, lambda t: gram_part.at[t], gram_rs.at[me])
    dev_x, dev_y, dev_d = (2 * other + core for other in (chip_x, chip_y, chip_d))
    upper, lower = pl.ds(0, rows // 2), pl.ds(rows // 2, rows // 2)

    def relay(index, owner, device, span=slice(None)):
        block_of = root.at[span, tile_of(owner)]
        pltpu.make_async_remote_copy(
            src_ref=block_of,
            dst_ref=block_of,
            send_sem=root_sems.at[5],
            recv_sem=root_sems.at[index],
            device_id={"dp": device},
            device_id_type=MESH,
        ).start()

    def relayed(index, count):
        drain(root.at[:, : count * LANES] if count else root.at[upper, :LANES], root_sems.at[index])

    relay(0, me, dev_x)
    relay(1, me, dev_y)
    relay(4, me, partner)
    received(SCATTER, gram_rs.at[: n_dp - 1])
    part = gram_rs[0]
    for index in range(1, n_dp):
        part = part + gram_rs[index]
    gram_z[z] = part
    exchange("tensor", ALONG, lambda t: gram_z.at[z], gram_z.at[z])
    relayed(0, 1)
    relay(2, dev_x, dev_y, upper)
    relay(4, dev_x, partner)
    relayed(1, 1)
    relay(3, dev_y, dev_x, lower)
    relay(4, dev_y, partner)
    received(ALONG, gram_z.at[: n_tp - 1])
    part = gram_z[0]
    for index in range(1, n_tp):
        part = part + gram_z[index]
    gram_all[me] = part
    exchange("dp", GATHER, lambda t: gram_all.at[me], gram_all.at[me])
    relayed(2, 0)
    relayed(3, 0)
    relay(4, dev_d, partner)
    relayed(4, half)
    root_write = pltpu.make_async_copy(root, root_out, out_sem.at[0])
    root_write.start()
    for phase, ref in (
        (PAIR, pair_in),
        (NODE, node_recv.at[: half - 1]),
        (MID, zmid),
        (SIDE, zrecv),
        (SLICE, grads.at[: n_tp - 1]),
        (ROW, grads_all.at[: n_tp * n_dp - 1]),
        (SUM, sums_all.at[: n_tp * n_dp - 1]),
        (SCATTER, gram_rs.at[: n_dp - 1]),
        (ALONG, gram_z.at[: n_tp - 1]),
    ):
        drain(ref, sems.at[0, phase])
    received(GATHER, gram_all.at[: n_dp - 1])
    triangle = jnp.concatenate([gram_all[r] for r in range(n_dp)], axis=0)
    gram_out[...] = triangle[: rows + LANES]
    targets = triangle[rows + LANES :]
    target = jnp.zeros((n_tp, rows), f32)
    for r in range(n_dp):
        span = slice(r * n_tp, (r + 1) * n_tp)
        both = [targets[: n_dp * n_tp][span], targets[n_dp * n_tp :][span]]
        target = jnp.where(me == r, jnp.concatenate(both, axis=1), target)
    target_out[...] = target
    drain(gram_all.at[: n_dp - 1], sems.at[0, GATHER])
    drain(root.at[:, : (n_dp - 1) * LANES], root_sems.at[5])
    root_write.wait()


def last_kernel(root_ref, gram_ref, target_ref, grads_ref, root_out, pre_out, pre, sem):
    write = pltpu.make_async_copy(root_ref, root_out, sem.at[0])
    write.start()
    rows = root_ref.shape[0]
    corner = gram_ref[LANES:rows]
    gram = jnp.concatenate(
        [
            jnp.concatenate([gram_ref[:LANES], corner.T], axis=1),
            jnp.concatenate([corner, gram_ref[rows:]], axis=1),
        ],
        axis=0,
    )
    solved = solve(gram, target_ref[...])
    pre[...] = grads_ref[...] - dot_mid(solved, root_ref[...])
    pre_write = pltpu.make_async_copy(pre, pre_out, sem.at[1])
    pre_write.start()
    write.wait()
    pre_write.wait()


def fused_body(
    activations,
    out_grads,
    input_proj,
    grad_proj,
    example_count,
    child_order,
    prior_sketch,
    fold_map,
    merge_mix,
):
    n_dp, n_tp = lax.axis_size("dp"), lax.axis_size("tensor")
    rows, columns = prior_sketch.shape
    slots = activations.shape[0] // SEQ
    f32, bf16 = jnp.float32, jnp.bfloat16
    width, hidden = activations.shape[1], out_grads.shape[1]
    hbm = pl.BlockSpec(memory_space=pltpu.HBM)
    anywhere = pl.BlockSpec(memory_space=pl.ANY)
    vmem = pl.BlockSpec(memory_space=pltpu.VMEM)
    smem = pl.BlockSpec(memory_space=pltpu.SMEM)
    devices = n_dp * n_tp
    part_rows = (3 * LANES + 2 * n_dp * slots) // n_dp
    pin = functools.partial(pltpu.with_memory_space_constraint, memory_space=pltpu.HBM)
    root, gram, target, grads = pl.pallas_call(
        functools.partial(fused_kernel, n_dp, n_tp),
        out_shape=(
            jax.ShapeDtypeStruct((rows, columns), f32),
            jax.ShapeDtypeStruct((3 * LANES, LANES), f32),
            jax.ShapeDtypeStruct((slots, rows), f32),
            jax.ShapeDtypeStruct((slots, columns), f32),
        ),
        in_specs=[hbm, hbm, hbm, hbm, smem, hbm, hbm, hbm, hbm],
        out_specs=(anywhere, vmem, vmem, vmem),
        scratch_shapes=[
            pltpu.VMEM((slots, SEQ, width + hidden), bf16),
            pltpu.VMEM((RANK, width + hidden), bf16),
            pltpu.SMEM((1, n_dp), jnp.int32),
            pltpu.VMEM((rows, columns), f32),
            pltpu.VMEM((slots, rows), f32),
            pltpu.VMEM((rows, 2 * rows), f32),
            pltpu.VMEM((n_dp // 2, rows, LANES), f32),
            pltpu.VMEM((n_dp // 2, rows, LANES), f32),
            pltpu.VMEM((n_dp // 2, rows, LANES), f32),
            pltpu.VMEM((3, SEQ, LANES), f32),
            pltpu.VMEM((SEQ, LANES), f32),
            pltpu.VMEM((2, SEQ, LANES), f32),
            pltpu.VMEM((RANK, LANES), f32),
            pltpu.VMEM((n_tp, n_dp, LANES), f32),
            pltpu.VMEM((n_tp, n_dp, LANES), f32),
            pltpu.VMEM((devices, 1, LANES), f32),
            pltpu.VMEM((devices, 1, LANES), f32),
            pltpu.VMEM((devices, 1, LANES), f32),
            pltpu.VMEM((rows, columns), f32),
            pltpu.VMEM((n_dp, part_rows, LANES), f32),
            pltpu.VMEM((n_dp, part_rows, LANES), f32),
            pltpu.VMEM((n_tp, part_rows, LANES), f32),
            pltpu.VMEM((n_dp, part_rows, LANES), f32),
            pltpu.SemaphoreType.DMA((9,)),
            pltpu.SemaphoreType.DMA((2, 10)),
            pltpu.SemaphoreType.DMA((6,)),
            pltpu.SemaphoreType.DMA((1,)),
            pltpu.SemaphoreType.REGULAR,
        ],
        compiler_params=pltpu.CompilerParams(
            collective_id=0, has_side_effects=True, vmem_limit_bytes=32 * 2**20
        ),
    )(
        pin(activations),
        pin(out_grads),
        pin(input_proj.T),
        pin(grad_proj.T),
        example_count,
        pin(child_order.reshape(1, n_dp)),
        pin(prior_sketch),
        pin(fold_map.T),
        pin(merge_mix),
    )
    return pl.pallas_call(
        last_kernel,
        out_shape=(
            jax.ShapeDtypeStruct((rows, columns), f32),
            jax.ShapeDtypeStruct((slots, columns), f32),
        ),
        in_specs=[vmem] * 4,
        out_specs=(anywhere, anywhere),
        scratch_shapes=[pltpu.VMEM((slots, columns), f32), pltpu.SemaphoreType.DMA((2,))],
        compiler_params=pltpu.CompilerParams(vmem_limit_bytes=16 * 2**20),
    )(root, gram, target, grads)


def from_partner(value, axis, stride):
    mask = 2**stride
    pairs = [(source, source ^ mask) for source in range(lax.axis_size(axis))]
    return lax.ppermute(value, axis, pairs)


def body(
    activations,
    out_grads,
    input_proj,
    grad_proj,
    example_count,
    child_order,
    prior_sketch,
    fold_map,
    merge_mix,
):
    tensor_count = lax.axis_size("tensor")
    own_rank = RANK // tensor_count
    example_slots = activations.shape[0] // SEQ
    sketch_rows = prior_sketch.shape[0]
    input_part = jnp.dot(activations, input_proj, preferred_element_type=jnp.float32)
    grad_part = jnp.dot(out_grads, grad_proj, preferred_element_type=jnp.float32)
    input_side, grad_side = lax.psum((input_part, grad_part), "tensor")
    grad_own = lax.dynamic_slice_in_dim(grad_side, lax.axis_index("tensor") * own_rank, own_rank, 1)
    grad_blocks = grad_own.reshape(example_slots, SEQ, own_rank)
    input_blocks = input_side.reshape(example_slots, SEQ, RANK)
    example_grad = jnp.einsum(
        "eta,etb->eab", grad_blocks, input_blocks, precision=lax.Precision.HIGHEST
    )
    example_grad = example_grad.reshape(example_slots, own_rank * RANK) / jnp.sqrt(jnp.float32(SEQ))
    live = jnp.arange(example_slots, dtype=jnp.int32) < example_count[0]
    example_grad = jnp.where(live[:, None], example_grad, jnp.zeros_like(example_grad))
    leaf_node = prior_sketch + jnp.dot(fold_map, example_grad, precision=lax.Precision.HIGHEST)
    leaf_weight = lax.psum(jnp.sum(leaf_node * leaf_node), "tensor")
    mix_first = merge_mix[:, :sketch_rows]
    mix_second = merge_mix[:, sketch_rows:]
    depth_count = lax.axis_size("dp").bit_length() - 1
    rank_index = lax.axis_index("dp")
    sketch_node = leaf_node
    sketch_weight = leaf_weight
    for level_index in range(depth_count):
        sibling_node, sibling_weight = from_partner((sketch_node, sketch_weight), "dp", level_index)
        upper_half = rank_index >> level_index & 1
        block_start = rank_index >> level_index + 1 << level_index + 1
        flip_order = child_order[block_start + (1 << level_index) - 1]
        own_first = upper_half == flip_order
        first = jnp.where(own_first, sketch_node, sibling_node)
        second = jnp.where(own_first, sibling_node, sketch_node)
        first_weight = jnp.where(own_first, sketch_weight, sibling_weight)
        second_weight = jnp.where(own_first, sibling_weight, sketch_weight)
        mixture = jnp.dot(mix_first, first, precision=lax.Precision.HIGHEST) + jnp.dot(
            mix_second, second, precision=lax.Precision.HIGHEST
        )
        mix_total = lax.psum(jnp.sum(mixture * mixture), "tensor")
        sketch_weight = first_weight + second_weight
        sketch_node = mixture * jnp.sqrt(sketch_weight / (mix_total + 1e-06))
    gram_part = jnp.dot(sketch_node, sketch_node.T, precision=lax.Precision.HIGHEST)
    product_part = jnp.dot(sketch_node, example_grad.T, precision=lax.Precision.HIGHEST)
    gram, sketch_grad = lax.psum((gram_part, product_part), "tensor")
    damping = jnp.trace(gram) / sketch_rows
    system = gram + damping * jnp.eye(sketch_rows, dtype=jnp.float32)
    factor = jnp.linalg.cholesky(system)
    solved = jax.scipy.linalg.cho_solve((factor, True), sketch_grad)
    preconditioned = example_grad - jnp.dot(solved.T, sketch_node, precision=lax.Precision.HIGHEST)
    return (sketch_node, preconditioned)


def fits_fused(rows, columns, slots, n_dp, n_tp):
    return (
        columns == n_dp * LANES
        and slots == n_tp
        and 2 * RANK == LANES
        and n_dp == 8
        and n_tp == 4
        and rows == 2 * LANES
        and (3 * LANES + 2 * n_dp * slots) % (8 * n_dp) == 0
    )


def step(*args):
    n_dp, n_tp = lax.axis_size("dp"), lax.axis_size("tensor")
    slots = args[0].shape[0] // SEQ
    rows, columns = args[6].shape
    if fits_fused(rows, columns, slots, n_dp, n_tp):
        return fused_body(*args)
    return body(*args)


def solution(mesh):
    in_specs = (
        P("dp", "tensor"),
        P("dp", "tensor"),
        P("tensor", None),
        P("tensor", None),
        P("dp"),
        P(),
        P("dp", "tensor"),
        P(),
        P(),
    )
    out_specs = (P(None, "tensor"), P("dp", "tensor"))
    return jax.shard_map(step, mesh=mesh, in_specs=in_specs, out_specs=out_specs, check_vma=False)
```

```python
import functools

import jax
import jax.numpy as jnp
from jax import lax
from jax.experimental import pallas as pl
from jax.experimental.pallas import tpu as pltpu
from jax.sharding import PartitionSpec as P

RANK = 64
SEQ = 128
LANES = 128
HIGHEST = lax.Precision.HIGHEST
MESH = pl.DeviceIdType.MESH


def newton_plan(rows):
    low, high = 0.999, (rows + 1) * 1.001
    first = 2.0 / (low + high)
    reach, scales = first * low, []
    while 1.0 - reach > 1e-3:
        grown = reach * (2.0 - reach)
        scale = 2.0 / (1.0 + grown)
        scales.append(scale)
        reach = grown * scale
    return first, scales


def dot_high(left, right):
    return jnp.dot(left, right, precision=HIGHEST, preferred_element_type=jnp.float32)


def dot_flip(left, right):
    return lax.dot_general(left, right, (((1,), (1,)), ((), ())), preferred_element_type=jnp.float32)


def dot_rows(left, right):
    return lax.dot_general(
        left, right, (((1,), (1,)), ((), ())), precision=HIGHEST, preferred_element_type=jnp.float32
    )


def halves(value):
    high = value.astype(jnp.bfloat16)
    return high, (value - high.astype(jnp.float32)).astype(jnp.bfloat16)


def dot_halves(left, right):
    (a, b), (c, d) = left, right
    out = jnp.dot(a, c, preferred_element_type=jnp.float32)
    out = out + jnp.dot(a, d, preferred_element_type=jnp.float32)
    return out + jnp.dot(b, c, preferred_element_type=jnp.float32)


def dot_mid(left, right):
    return dot_halves(halves(left), halves(right))


def dot_flip_halves(left, right):
    (a, b), (c, d) = left, right
    return dot_flip(jnp.concatenate([a, a, b], axis=1), jnp.concatenate([c, d, c], axis=1))


def dot_split(left, right):
    (a, b), (c, d) = left, right
    half = a.shape[1] // 2
    first = jnp.dot(
        jnp.concatenate([a, b[:, :half]], axis=1),
        jnp.concatenate([c, c[:half]], axis=0),
        preferred_element_type=jnp.float32,
    )
    second = jnp.dot(
        jnp.concatenate([a, b[:, half:]], axis=1),
        jnp.concatenate([d, c[half:]], axis=0),
        preferred_element_type=jnp.float32,
    )
    return first + second


def stacked(value, order):
    high = value.astype(jnp.bfloat16).astype(jnp.float32)
    both = (high, value - high)
    return jnp.concatenate([both[i] for i in order], axis=0)


def solve(gram, target):
    rows = gram.shape[0]
    eye = lax.broadcasted_iota(jnp.int32, gram.shape, 0) == lax.broadcasted_iota(jnp.int32, gram.shape, 1)
    trace = jnp.sum(
        jnp.sum(jnp.where(eye, gram, 0.0), axis=0, keepdims=True), axis=1, keepdims=True
    )
    unit = 1.0 / (trace / rows)
    system = gram * unit + jnp.where(eye, 1.0, 0.0)
    target = target * unit
    first, scales = newton_plan(rows)
    state, solved, path = first * system, first * target, None
    for index, scale in enumerate(scales):
        factor = jnp.where(eye, 2.0 * scale, 0.0) - scale * state
        factor_halves = halves(factor)
        solved = dot_split(halves(solved), factor_halves)
        if index < len(scales) - 1:
            state = dot_split(halves(state), factor_halves)
            if path is None:
                path = factor_halves[0]
            else:
                path = jnp.dot(path, factor_halves[0], preferred_element_type=jnp.float32)
                path = path.astype(jnp.bfloat16)
    high, low = halves(first * (target - dot_high(solved, system)))
    step = jnp.dot(high, path, preferred_element_type=jnp.float32)
    step = step + jnp.dot(low, path, preferred_element_type=jnp.float32)
    return solved + dot_split(halves(step), factor_halves)


def fused_kernel(
    n_dp,
    n_tp,
    act_hbm,
    out_hbm,
    wi_hbm,
    wo_hbm,
    count_ref,
    order_hbm,
    prior_hbm,
    fold_hbm,
    mix_hbm,
    root_out,
    gram_out,
    target_out,
    grads_out,
    tokens,
    weights,
    order_ref,
    prior,
    fold_ref,
    mix_ref,
    pair_in,
    node_send,
    node_recv,
    zsend,
    zmid,
    zrecv,
    full,
    slices_send,
    grads,
    grads_rows,
    grads_all,
    peer_all,
    mix_send,
    mix_recv,
    sums_all,
    root,
    gram_part,
    gram_rs,
    gram_z,
    gram_all,
    load_sem,
    sems,
    root_sems,
    out_sem,
    ready_sem,
):
    f32 = jnp.float32
    me, z = lax.axis_index("dp"), lax.axis_index("tensor")
    rows = prior.shape[0]
    part_rows = gram_z.shape[1]
    levels = n_dp.bit_length() - 1

    def dp_of(k):
        return lax.rem(me + k, n_dp)

    def tp_of(k):
        return lax.rem(z + k, n_tp)

    width = act_hbm.shape[1]
    near = z + 1 - 2 * lax.rem(z, 2)
    far = z + 2 - 4 * (z // 2)
    diagonal = near + 2 - 4 * (near // 2)
    order = (diagonal, near, far, z)
    used = []

    def load(*pairs):
        for source, target in pairs:
            pltpu.make_async_copy(source, target, load_sem.at[len(used)]).start()
        used.append(None)
        return len(used) - 1

    def drain(ref, sem):
        pltpu.make_async_copy(ref, ref, sem).wait()

    def load_chunk(index):
        span = pl.ds(pl.multiple_of(order[index] * SEQ, SEQ), SEQ)
        into = tokens.at[index]
        return load((act_hbm.at[span], into.at[:, :width]), (out_hbm.at[span], into.at[:, width:]))

    order_load = load((order_hbm, order_ref))
    weight_load = load((wi_hbm, weights.at[:, :width]), (wo_hbm, weights.at[:, width:]))
    chunk_loads = [load_chunk(0)]
    prior_load = load((prior_hbm, prior))
    mix_load = load((mix_hbm, mix_ref))
    chunk_loads += [load_chunk(index) for index in range(1, n_tp)]
    fold_load = load((fold_hbm, fold_ref))

    def tile_of(owner):
        return pl.ds(pl.multiple_of(owner * LANES, LANES), LANES)

    barrier = pltpu.get_barrier_semaphore()
    for k in range(1, n_tp):
        pl.semaphore_signal(barrier, inc=1, device_id={"tensor": tp_of(k)}, device_id_type=MESH)
    for k in range(1, n_dp):
        pl.semaphore_signal(barrier, inc=1, device_id={"dp": dp_of(k)}, device_id_type=MESH)
    pl.semaphore_wait(barrier, n_dp + n_tp - 2)
    for k in range(1, n_dp):
        pl.semaphore_signal(ready_sem, inc=1, device_id={"dp": dp_of(k)}, device_id_type=MESH)

    half = n_dp // 2
    core, chip = lax.rem(me, 2), me // 2
    partner = me + 1 - 2 * core
    chip_x = chip + 1 - 2 * lax.rem(chip, 2)
    chip_y = chip + 2 - 4 * (chip // 2)
    chip_d = half - 1 - chip

    PAIR, NODE, MID, SIDE, SLICE, ROW, PEER, SUM, SCATTER, ALONG, GATHER, MIX = range(12)

    def push(phase, source, target, **device):
        pltpu.make_async_remote_copy(
            src_ref=source,
            dst_ref=target,
            send_sem=sems.at[0, phase],
            recv_sem=sems.at[1, phase],
            device_id=device,
            device_id_type=MESH,
        ).start()

    def received(phase, ref):
        drain(ref, sems.at[1, phase])

    for q in range(half):
        push(PAIR, prior_hbm.at[:, tile_of(2 * q + 1 - core)], pair_in.at[q], dp=partner)

    def exchange(axis, phase, source, target):
        size, other = (n_tp, tp_of) if axis == "tensor" else (n_dp, dp_of)
        for k in range(1, size):
            push(phase, source(other(k)), target, **{axis: other(k)})

    def exchange_all(phase, source, target):
        for j in sorted(range(n_tp), key=lambda j: -min(j, n_tp - j)):
            for k in range(n_dp):
                if (j, k) != (0, 0):
                    push(phase, source(dp_of(k), tp_of(j)), target, dp=dp_of(k), tensor=tp_of(j))

    def sides_of_chunk(index):
        drain(tokens.at[index], load_sem.at[chunk_loads[index]])
        mid = SEQ // 2
        spans = [slice(h * mid, (h + 1) * mid) for h in range(2)]
        right = [dot_flip(tokens[index, span, width:], weights[:, width:]) for span in spans]
        left = [dot_flip(tokens[index, span, :width], weights[:, :width]) for span in spans]
        return jnp.concatenate([jnp.concatenate(pair, axis=1) for pair in zip(left, right)], axis=0)

    drain(weights, load_sem.at[weight_load])
    zsend[0] = sides_of_chunk(0)
    push(MID, zsend.at[0], zmid, tensor=near)

    drain(order_ref, load_sem.at[order_load])
    drain(prior, load_sem.at[prior_load])
    drain(mix_ref, load_sem.at[mix_load])
    received(PAIR, pair_in)
    first_mix, second_mix = mix_ref[:, :rows], mix_ref[:, rows:]
    own_first = order_ref[0, 2 * chip] == core
    own_half = [prior[:, tile_of(2 * q + core)] for q in range(half)]
    firsts = [jnp.where(own_first, own_half[q], pair_in[q]) for q in range(half)]
    seconds = [jnp.where(own_first, pair_in[q], own_half[q]) for q in range(half)]
    first_halves, second_halves = halves(first_mix), halves(second_mix)
    mixed = dot_halves(first_halves, halves(jnp.concatenate(firsts, axis=1)))
    mixed = mixed + dot_halves(second_halves, halves(jnp.concatenate(seconds, axis=1)))
    for q in range(half):
        node_send[q] = mixed[:, q * LANES : (q + 1) * LANES]
    for other in (chip_x, chip_y, chip_d):
        push(NODE, node_send.at[other], node_recv.at[chip], dp=2 * other + core)
    node_recv[chip] = node_send[chip]
    zsend[1] = sides_of_chunk(1)
    push(SIDE, zsend.at[1], zrecv.at[0], tensor=near)
    far_sides = sides_of_chunk(2)
    received(MID, zmid)
    zsend[2] = far_sides + zmid[...]
    push(SIDE, zsend.at[2], zrecv.at[1], tensor=far)
    own_sides = sides_of_chunk(3)

    drain(fold_ref, load_sem.at[fold_load])
    fold_rows = fold_ref[...]
    paths = [[jnp.concatenate([dot_rows(fold_rows, first_mix), dot_rows(fold_rows, second_mix)], axis=0)]]
    for level in range(1, levels):
        paths.append(
            [dot_rows(p, first_mix) for p in paths[-1]] + [dot_rows(p, second_mix) for p in paths[-1]]
        )
    paths = [[stacked(p, (0, 0, 1)).T.astype(jnp.bfloat16) for p in level] for level in paths]
    fold = fold_rows.T

    received(SIDE, zrecv)
    sides = (own_sides + zrecv[0]) + zrecv[1]
    lane = lax.broadcasted_iota(jnp.int32, sides.shape, 1)
    doubled = jnp.where(lane < RANK, sides, pltpu.roll(sides, RANK, 1))
    product = dot_mid(sides.T, doubled) / jnp.sqrt(f32(SEQ))
    product = jnp.where(z < count_ref[0], product, jnp.zeros_like(product))
    full[...] = product[RANK:]
    even = full[pl.ds(0, RANK // 2, stride=2), :]
    odd = full[pl.ds(1, RANK // 2, stride=2), :]
    lane = lax.broadcasted_iota(jnp.int32, even.shape, 1)
    mine = jnp.where(lane < RANK, even, odd)
    for row in range(n_tp * n_dp):
        grads_rows[row] = mine[row : row + 1]
    for index in range(n_tp):
        slices_send[index] = mine[index * n_dp : (index + 1) * n_dp]
    grads[z] = slices_send[z]
    slot = me * n_tp + z
    grads_all[slot] = grads_rows[z * n_dp + me]
    pl.semaphore_wait(ready_sem, n_dp - 1)
    exchange("tensor", SLICE, lambda t: slices_send.at[t], grads.at[z])
    exchange_all(ROW, lambda d, t: grads_rows.at[t * n_dp + d], grads_all.at[slot])

    flags = [
        [order_ref[0, j * 2 ** (level + 1) + 2**level - 1] == 1 for j in range(n_dp >> (level + 1))]
        for level in range(levels)
    ]

    def pick(flip, lower, upper):
        first = [jnp.where(flip, b, a) for a, b in zip(lower, upper)]
        return first, [jnp.where(flip, a, b) for a, b in zip(lower, upper)]

    def total(value):
        return jnp.sum(jnp.sum(value, axis=0, keepdims=True), axis=1, keepdims=True)

    received(NODE, node_recv.at[: half - 1])
    mixtures = [[[node_recv[j]] for j in range(half)]]
    for level in range(1, levels):
        below = mixtures[-1]
        sides_of = [pick(flags[level][j], below[2 * j], below[2 * j + 1]) for j in range(len(below) // 2)]
        count = len(below[0])
        left = dot_halves(first_halves, halves(jnp.concatenate([v for f, _ in sides_of for v in f], axis=1)))
        right = dot_halves(second_halves, halves(jnp.concatenate([v for _, g in sides_of for v in g], axis=1)))
        mixtures.append(
            [
                [
                    side[:, (j * count + i) * LANES : (j * count + i + 1) * LANES]
                    for side in (left, right)
                    for i in range(count)
                ]
                for j in range(len(sides_of))
            ]
        )

    for index, part in enumerate(mixtures[-1][0]):
        mix_send[index] = part
    push(MIX, mix_send, mix_recv, dp=partner)

    received(SLICE, grads.at[: n_tp - 1])
    leaf_square = jnp.zeros((rows, LANES), f32)
    for tile in range(n_dp):
        leaf = prior[:, tile * LANES : (tile + 1) * LANES]
        for e in range(n_tp):
            step = grads[e, tile : tile + 1, :]
            grads_out[e : e + 1, tile * LANES : (tile + 1) * LANES] = step
            leaf = leaf + fold[:, e : e + 1] * step
        leaf_square = leaf_square + leaf * leaf
    own_mass = total(leaf_square)

    received(ROW, grads_all.at[: n_tp * n_dp - 1])
    push(PEER, grads_all, peer_all, dp=partner)

    def steps_from(rows_of):
        steps_of = [
            [jnp.concatenate([rows_of[r * n_tp + e] for e in range(n_tp)], axis=0)] for r in range(n_dp)
        ]
        return steps_of, jnp.concatenate([step[0] for step in steps_of], axis=0)

    def merge_steps(level, steps_of):
        merged_steps = []
        for j in range(len(steps_of) // 2):
            first, second = pick(flags[level][j], steps_of[2 * j], steps_of[2 * j + 1])
            if level == 0:
                merged_steps.append([jnp.concatenate([first[0], second[0]], axis=0)])
            else:
                merged_steps.append(first + second)
        return merged_steps

    def updates_of(level, merged_steps):
        return [
            jnp.dot(
                path,
                jnp.concatenate([stacked(g[i], (0, 1, 0)) for g in merged_steps], axis=1).astype(jnp.bfloat16),
                preferred_element_type=f32,
            )
            for i, path in enumerate(paths[level])
        ]

    steps_of, every = steps_from(grads_all)
    sums, products, nodes = [], [], []
    for level in range(levels):
        level_products, level_nodes = [], []
        merged_steps = merge_steps(level, steps_of)
        updates = updates_of(level, merged_steps)
        for j in range(len(merged_steps)):
            parts = [
                v + update[:, j * LANES : (j + 1) * LANES]
                for v, update in zip(mixtures[level][j], updates)
            ]
            index_of = {}
            for a in range(len(parts)):
                for b in range(a + 1):
                    index_of[a, b] = n_dp + len(sums)
                    sums.append(total(parts[a] * parts[b]))
            level_products.append(index_of)
            level_nodes.append(parts)
        steps_of = merged_steps
        products.append(level_products)
        nodes = level_nodes
    lane = lax.broadcasted_iota(jnp.int32, (1, LANES), 1)
    packed = jnp.where(lane == me, own_mass, jnp.zeros((1, LANES), f32))
    for index, value in enumerate(sums):
        packed = jnp.where(lane == n_dp + index, value, packed)
    sums_all[slot] = packed
    exchange_all(SUM, lambda d, t: sums_all.at[slot], sums_all.at[slot])
    received(PEER, peer_all)
    received(MIX, mix_recv)
    steps_of, peer_every = steps_from(peer_all)
    for level in range(levels):
        steps_of = merge_steps(level, steps_of)
    peer_parts = [mix_recv[i] + update for i, update in enumerate(updates_of(levels - 1, steps_of))]
    every_halves = halves(jnp.concatenate([every, peer_every], axis=1))
    received(SUM, sums_all.at[: n_tp * n_dp - 1])
    parts_of = [sums_all[index] for index in range(n_tp * n_dp)]
    while len(parts_of) > 1:
        parts_of = [a + b for a, b in zip(parts_of[0::2], parts_of[1::2])]
    packed = parts_of[0]

    def summed(index):
        return jnp.sum(jnp.where(lane == index, packed, 0.0), axis=1, keepdims=True)

    masses = [summed(index) for index in range(n_dp)]
    scales = [[jnp.ones((1, 1), f32)] for _ in range(n_dp)]
    for level in range(levels):
        new_masses, new_scales = [], []
        for j, products_of in enumerate(products[level]):
            flip = flags[level][j]
            lower, upper = scales[2 * j], scales[2 * j + 1]
            if level == 0:
                coefs = [jnp.ones((1, 1), f32)]
            else:
                coefs = [jnp.where(flip, b, a) for a, b in zip(lower, upper)]
                coefs += [jnp.where(flip, a, b) for a, b in zip(lower, upper)]
            square = jnp.zeros((1, 1), f32)
            for (a, b), index in products_of.items():
                term = coefs[a] * (coefs[b] * summed(index))
                square = square + (term if a == b else 2.0 * term)
            mass = masses[2 * j] + masses[2 * j + 1]
            scale = jnp.sqrt(mass / (jnp.maximum(square, 0.0) + 1e-06))
            new_masses.append(mass)
            new_scales.append([scale * c for c in coefs])
        masses, scales = new_masses, new_scales
    chunks = []
    for parts in (nodes[0], peer_parts):
        chunk = scales[0][0] * parts[0]
        for c, part in zip(scales[0][1:], parts[1:]):
            chunk = chunk + c * part
        chunks.append(chunk)
    root[:, tile_of(me)] = chunks[0]
    root[:, tile_of(partner)] = chunks[1]

    chunk_halves = halves(jnp.concatenate(chunks, axis=1))
    upper_halves, lower_halves = [[v[s] for v in chunk_halves] for s in (slice(0, LANES), slice(LANES, rows))]
    targets = dot_flip_halves(every_halves, chunk_halves)
    triangle = jnp.concatenate(
        [
            dot_flip_halves(chunk_halves, upper_halves),
            dot_flip_halves(lower_halves, lower_halves),
            targets[:, :LANES],
            targets[:, LANES:],
        ],
        axis=0,
    )
    for r in range(n_dp):
        gram_part[r] = triangle[r * part_rows : (r + 1) * part_rows]
    gram_rs[chip] = gram_part[me]
    for other in (chip_d, chip_x, chip_y):
        push(SCATTER, gram_part.at[2 * other + core], gram_rs.at[chip], dp=2 * other + core)
    dev_x, dev_y, dev_d = (2 * other + core for other in (chip_x, chip_y, chip_d))
    upper, lower = pl.ds(0, rows // 2), pl.ds(rows // 2, rows // 2)

    def relay(index, owner, device, span=slice(None)):
        block_of = root.at[span, tile_of(owner)]
        pltpu.make_async_remote_copy(
            src_ref=block_of,
            dst_ref=block_of,
            send_sem=root_sems.at[5],
            recv_sem=root_sems.at[index],
            device_id={"dp": device},
            device_id_type=MESH,
        ).start()

    def relayed(index, count):
        drain(root.at[:, : count * LANES] if count else root.at[upper, :LANES], root_sems.at[index])

    relay(0, me, dev_x)
    relay(1, me, dev_y)
    received(SCATTER, gram_rs.at[: half - 1])
    part = gram_rs[0]
    for index in range(1, half):
        part = part + gram_rs[index]
    gram_z[z] = part
    exchange("tensor", ALONG, lambda t: gram_z.at[z], gram_z.at[z])
    relayed(0, 1)
    relay(2, dev_x, dev_y, upper)
    relay(4, dev_x, partner)
    relayed(1, 1)
    relay(3, dev_y, dev_x, lower)
    relay(4, dev_y, partner)
    received(ALONG, gram_z.at[: n_tp - 1])
    part = gram_z[0]
    for index in range(1, n_tp):
        part = part + gram_z[index]
    gram_all[me] = part
    exchange("dp", GATHER, lambda t: gram_all.at[me], gram_all.at[me])
    relayed(2, 0)
    relayed(3, 0)
    relay(4, dev_d, partner)
    relayed(4, half - 1)
    root_write = pltpu.make_async_copy(root, root_out, out_sem.at[0])
    root_write.start()
    for phase, ref in (
        (PAIR, pair_in),
        (NODE, node_recv.at[: half - 1]),
        (MID, zmid),
        (SIDE, zrecv),
        (SLICE, grads.at[: n_tp - 1]),
        (ROW, grads_all.at[: n_tp * n_dp - 1]),
        (SUM, sums_all.at[: n_tp * n_dp - 1]),
        (PEER, peer_all),
        (MIX, mix_recv),
        (SCATTER, gram_rs.at[: half - 1]),
        (ALONG, gram_z.at[: n_tp - 1]),
    ):
        drain(ref, sems.at[0, phase])
    received(GATHER, gram_all.at[: n_dp - 1])
    triangle = jnp.concatenate([gram_all[r] for r in range(n_dp)], axis=0)
    gram_out[...] = triangle[: rows + LANES]
    targets = triangle[rows + LANES :]
    target = jnp.zeros((n_tp, rows), f32)
    for r in range(n_dp):
        span = slice(r * n_tp, (r + 1) * n_tp)
        both = [targets[: n_dp * n_tp][span], targets[n_dp * n_tp :][span]]
        target = jnp.where(me == r, jnp.concatenate(both, axis=1), target)
    target_out[...] = target
    drain(gram_all.at[: n_dp - 1], sems.at[0, GATHER])
    drain(root.at[:, : (n_dp - 2) * LANES], root_sems.at[5])
    root_write.wait()


def last_kernel(root_ref, gram_ref, target_ref, grads_ref, root_out, pre_out, pre, sem):
    write = pltpu.make_async_copy(root_ref, root_out, sem.at[0])
    write.start()
    rows = root_ref.shape[0]
    corner = gram_ref[LANES:rows]
    gram = jnp.concatenate(
        [
            jnp.concatenate([gram_ref[:LANES], corner.T], axis=1),
            jnp.concatenate([corner, gram_ref[rows:]], axis=1),
        ],
        axis=0,
    )
    solved = solve(gram, target_ref[...])
    pre[...] = grads_ref[...] - dot_mid(solved, root_ref[...])
    pre_write = pltpu.make_async_copy(pre, pre_out, sem.at[1])
    pre_write.start()
    write.wait()
    pre_write.wait()


def fused_body(
    activations,
    out_grads,
    input_proj,
    grad_proj,
    example_count,
    child_order,
    prior_sketch,
    fold_map,
    merge_mix,
):
    n_dp, n_tp = lax.axis_size("dp"), lax.axis_size("tensor")
    rows, columns = prior_sketch.shape
    slots = activations.shape[0] // SEQ
    f32, bf16 = jnp.float32, jnp.bfloat16
    width, hidden = activations.shape[1], out_grads.shape[1]
    hbm = pl.BlockSpec(memory_space=pltpu.HBM)
    anywhere = pl.BlockSpec(memory_space=pl.ANY)
    vmem = pl.BlockSpec(memory_space=pltpu.VMEM)
    smem = pl.BlockSpec(memory_space=pltpu.SMEM)
    devices = n_dp * n_tp
    part_rows = (3 * LANES + 2 * n_dp * slots) // n_dp
    pin = functools.partial(pltpu.with_memory_space_constraint, memory_space=pltpu.HBM)
    root, gram, target, grads = pl.pallas_call(
        functools.partial(fused_kernel, n_dp, n_tp),
        out_shape=(
            jax.ShapeDtypeStruct((rows, columns), f32),
            jax.ShapeDtypeStruct((3 * LANES, LANES), f32),
            jax.ShapeDtypeStruct((slots, rows), f32),
            jax.ShapeDtypeStruct((slots, columns), f32),
        ),
        in_specs=[hbm, hbm, hbm, hbm, smem, hbm, hbm, hbm, hbm],
        out_specs=(anywhere, vmem, vmem, vmem),
        scratch_shapes=[
            pltpu.VMEM((slots, SEQ, width + hidden), bf16),
            pltpu.VMEM((RANK, width + hidden), bf16),
            pltpu.SMEM((1, n_dp), jnp.int32),
            pltpu.VMEM((rows, columns), f32),
            pltpu.VMEM((slots, rows), f32),
            pltpu.VMEM((rows, 2 * rows), f32),
            pltpu.VMEM((n_dp // 2, rows, LANES), f32),
            pltpu.VMEM((n_dp // 2, rows, LANES), f32),
            pltpu.VMEM((n_dp // 2, rows, LANES), f32),
            pltpu.VMEM((3, SEQ, LANES), f32),
            pltpu.VMEM((SEQ, LANES), f32),
            pltpu.VMEM((2, SEQ, LANES), f32),
            pltpu.VMEM((RANK, LANES), f32),
            pltpu.VMEM((n_tp, n_dp, LANES), f32),
            pltpu.VMEM((n_tp, n_dp, LANES), f32),
            pltpu.VMEM((devices, 1, LANES), f32),
            pltpu.VMEM((devices, 1, LANES), f32),
            pltpu.VMEM((devices, 1, LANES), f32),
            pltpu.VMEM((n_dp // 2, rows, LANES), f32),
            pltpu.VMEM((n_dp // 2, rows, LANES), f32),
            pltpu.VMEM((devices, 1, LANES), f32),
            pltpu.VMEM((rows, columns), f32),
            pltpu.VMEM((n_dp, part_rows, LANES), f32),
            pltpu.VMEM((n_dp // 2, part_rows, LANES), f32),
            pltpu.VMEM((n_tp, part_rows, LANES), f32),
            pltpu.VMEM((n_dp, part_rows, LANES), f32),
            pltpu.SemaphoreType.DMA((9,)),
            pltpu.SemaphoreType.DMA((2, 12)),
            pltpu.SemaphoreType.DMA((6,)),
            pltpu.SemaphoreType.DMA((1,)),
            pltpu.SemaphoreType.REGULAR,
        ],
        compiler_params=pltpu.CompilerParams(
            collective_id=0, has_side_effects=True, vmem_limit_bytes=32 * 2**20
        ),
    )(
        pin(activations),
        pin(out_grads),
        pin(input_proj.T),
        pin(grad_proj.T),
        example_count,
        pin(child_order.reshape(1, n_dp)),
        pin(prior_sketch),
        pin(fold_map.T),
        pin(merge_mix),
    )
    return pl.pallas_call(
        last_kernel,
        out_shape=(
            jax.ShapeDtypeStruct((rows, columns), f32),
            jax.ShapeDtypeStruct((slots, columns), f32),
        ),
        in_specs=[vmem] * 4,
        out_specs=(anywhere, anywhere),
        scratch_shapes=[pltpu.VMEM((slots, columns), f32), pltpu.SemaphoreType.DMA((2,))],
        compiler_params=pltpu.CompilerParams(vmem_limit_bytes=16 * 2**20),
    )(root, gram, target, grads)


def from_partner(value, axis, stride):
    mask = 2**stride
    pairs = [(source, source ^ mask) for source in range(lax.axis_size(axis))]
    return lax.ppermute(value, axis, pairs)


def body(
    activations,
    out_grads,
    input_proj,
    grad_proj,
    example_count,
    child_order,
    prior_sketch,
    fold_map,
    merge_mix,
):
    tensor_count = lax.axis_size("tensor")
    own_rank = RANK // tensor_count
    example_slots = activations.shape[0] // SEQ
    sketch_rows = prior_sketch.shape[0]
    input_part = jnp.dot(activations, input_proj, preferred_element_type=jnp.float32)
    grad_part = jnp.dot(out_grads, grad_proj, preferred_element_type=jnp.float32)
    input_side, grad_side = lax.psum((input_part, grad_part), "tensor")
    grad_own = lax.dynamic_slice_in_dim(grad_side, lax.axis_index("tensor") * own_rank, own_rank, 1)
    grad_blocks = grad_own.reshape(example_slots, SEQ, own_rank)
    input_blocks = input_side.reshape(example_slots, SEQ, RANK)
    example_grad = jnp.einsum(
        "eta,etb->eab", grad_blocks, input_blocks, precision=lax.Precision.HIGHEST
    )
    example_grad = example_grad.reshape(example_slots, own_rank * RANK) / jnp.sqrt(jnp.float32(SEQ))
    live = jnp.arange(example_slots, dtype=jnp.int32) < example_count[0]
    example_grad = jnp.where(live[:, None], example_grad, jnp.zeros_like(example_grad))
    leaf_node = prior_sketch + jnp.dot(fold_map, example_grad, precision=lax.Precision.HIGHEST)
    leaf_weight = lax.psum(jnp.sum(leaf_node * leaf_node), "tensor")
    mix_first = merge_mix[:, :sketch_rows]
    mix_second = merge_mix[:, sketch_rows:]
    depth_count = lax.axis_size("dp").bit_length() - 1
    rank_index = lax.axis_index("dp")
    sketch_node = leaf_node
    sketch_weight = leaf_weight
    for level_index in range(depth_count):
        sibling_node, sibling_weight = from_partner((sketch_node, sketch_weight), "dp", level_index)
        upper_half = rank_index >> level_index & 1
        block_start = rank_index >> level_index + 1 << level_index + 1
        flip_order = child_order[block_start + (1 << level_index) - 1]
        own_first = upper_half == flip_order
        first = jnp.where(own_first, sketch_node, sibling_node)
        second = jnp.where(own_first, sibling_node, sketch_node)
        first_weight = jnp.where(own_first, sketch_weight, sibling_weight)
        second_weight = jnp.where(own_first, sibling_weight, sketch_weight)
        mixture = jnp.dot(mix_first, first, precision=lax.Precision.HIGHEST) + jnp.dot(
            mix_second, second, precision=lax.Precision.HIGHEST
        )
        mix_total = lax.psum(jnp.sum(mixture * mixture), "tensor")
        sketch_weight = first_weight + second_weight
        sketch_node = mixture * jnp.sqrt(sketch_weight / (mix_total + 1e-06))
    gram_part = jnp.dot(sketch_node, sketch_node.T, precision=lax.Precision.HIGHEST)
    product_part = jnp.dot(sketch_node, example_grad.T, precision=lax.Precision.HIGHEST)
    gram, sketch_grad = lax.psum((gram_part, product_part), "tensor")
    damping = jnp.trace(gram) / sketch_rows
    system = gram + damping * jnp.eye(sketch_rows, dtype=jnp.float32)
    factor = jnp.linalg.cholesky(system)
    solved = jax.scipy.linalg.cho_solve((factor, True), sketch_grad)
    preconditioned = example_grad - jnp.dot(solved.T, sketch_node, precision=lax.Precision.HIGHEST)
    return (sketch_node, preconditioned)


def fits_fused(rows, columns, slots, n_dp, n_tp):
    return (
        columns == n_dp * LANES
        and slots == n_tp
        and 2 * RANK == LANES
        and n_dp == 8
        and n_tp == 4
        and rows == 2 * LANES
        and (3 * LANES + 2 * n_dp * slots) % (8 * n_dp) == 0
    )


def step(*args):
    n_dp, n_tp = lax.axis_size("dp"), lax.axis_size("tensor")
    slots = args[0].shape[0] // SEQ
    rows, columns = args[6].shape
    if fits_fused(rows, columns, slots, n_dp, n_tp):
        return fused_body(*args)
    return body(*args)


def solution(mesh):
    in_specs = (
        P("dp", "tensor"),
        P("dp", "tensor"),
        P("tensor", None),
        P("tensor", None),
        P("dp"),
        P(),
        P("dp", "tensor"),
        P(),
        P(),
    )
    out_specs = (P(None, "tensor"), P("dp", "tensor"))
    return jax.shard_map(step, mesh=mesh, in_specs=in_specs, out_specs=out_specs, check_vma=False)
```

```python
import functools

import jax
import jax.numpy as jnp
from jax import lax
from jax.experimental import pallas as pl
from jax.experimental.pallas import tpu as pltpu
from jax.sharding import PartitionSpec as P

RANK = 64
SEQ = 128
LANES = 128
HIGHEST = lax.Precision.HIGHEST
MESH = pl.DeviceIdType.MESH


def newton_plan(rows):
    low, high = 0.999, (rows + 1) * 1.001
    first = 2.0 / (low + high)
    reach, scales = first * low, []
    while 1.0 - reach > 1e-3:
        grown = reach * (2.0 - reach)
        scale = 2.0 / (1.0 + grown)
        scales.append(scale)
        reach = grown * scale
    return first, scales


def dot_high(left, right):
    return jnp.dot(left, right, precision=HIGHEST, preferred_element_type=jnp.float32)


def dot_flip(left, right):
    return lax.dot_general(left, right, (((1,), (1,)), ((), ())), preferred_element_type=jnp.float32)


def dot_rows(left, right):
    return lax.dot_general(
        left, right, (((1,), (1,)), ((), ())), precision=HIGHEST, preferred_element_type=jnp.float32
    )


def halves(value):
    high = value.astype(jnp.bfloat16)
    return high, (value - high.astype(jnp.float32)).astype(jnp.bfloat16)


def dot_halves(left, right):
    (a, b), (c, d) = left, right
    out = jnp.dot(a, c, preferred_element_type=jnp.float32)
    out = out + jnp.dot(a, d, preferred_element_type=jnp.float32)
    return out + jnp.dot(b, c, preferred_element_type=jnp.float32)


def dot_mid(left, right):
    return dot_halves(halves(left), halves(right))


def dot_flip_halves(left, right):
    (a, b), (c, d) = left, right
    return dot_flip(jnp.concatenate([a, a, b], axis=1), jnp.concatenate([c, d, c], axis=1))


def dot_rows_halved(left, right):
    (a, b), (c, d) = left, right
    left = jnp.concatenate([a, a, b], axis=1)
    right = jnp.concatenate([c, d, c], axis=0)
    half = left.shape[0] // 2
    return jnp.concatenate(
        [
            jnp.dot(left[:half], right, preferred_element_type=jnp.float32),
            jnp.dot(left[half:], right, preferred_element_type=jnp.float32),
        ],
        axis=0,
    )


def thirds(value):
    high, rest = halves(value)
    rest = value - high.astype(jnp.float32)
    return (high, *halves(rest))


def dot_thirds(left, right):
    count = left.shape[0]
    stack = jnp.concatenate(thirds(left), axis=0)
    a, b, c = (jnp.dot(stack, part, preferred_element_type=jnp.float32) for part in thirds(right))
    high = a[count : 2 * count] + b[:count]
    low = (a[2 * count :] + b[count : 2 * count]) + c[:count]
    return a[:count] + (high + low)


def stacked(value, order):
    high = value.astype(jnp.bfloat16).astype(jnp.float32)
    both = (high, value - high)
    return jnp.concatenate([both[i] for i in order], axis=0)


def solve(gram, target, between):
    rows = gram.shape[0]
    eye = lax.broadcasted_iota(jnp.int32, gram.shape, 0) == lax.broadcasted_iota(jnp.int32, gram.shape, 1)
    system = gram + jnp.where(eye, 1.0, 0.0)
    first, scales = newton_plan(rows)
    state, solved, path = first * system, first * target, None
    for index, scale in enumerate(scales):
        factor = jnp.where(eye, 2.0 * scale, 0.0) - scale * state
        factor_halves = halves(factor)
        solved = dot_halves(halves(solved), factor_halves)
        if index < len(scales) - 1:
            state = dot_rows_halved(halves(state), factor_halves)
            if path is None:
                path = factor_halves[0]
            else:
                path = jnp.dot(path, factor_halves[0], preferred_element_type=jnp.float32)
                path = path.astype(jnp.bfloat16)
        between(index)
    rest = (first * (target - dot_thirds(solved, system))).astype(jnp.bfloat16)
    step = jnp.dot(rest, path, preferred_element_type=jnp.float32)
    return solved + dot_halves(halves(step), factor_halves)


def fused_kernel(
    n_dp,
    n_tp,
    act_hbm,
    out_hbm,
    wi_hbm,
    wo_hbm,
    count_ref,
    order_hbm,
    prior_hbm,
    fold_hbm,
    mix_hbm,
    root_out,
    solved_out,
    grads_out,
    tokens,
    weights,
    order_ref,
    prior,
    fold_ref,
    mix_ref,
    pair_in,
    node_send,
    node_recv,
    zsend,
    zmid,
    zrecv,
    full,
    slices_send,
    grads,
    grads_rows,
    grads_all,
    peer_all,
    mix_send,
    mix_recv,
    sums_all,
    root,
    gram_part,
    gram_rs,
    gram_z,
    gram_all,
    load_sem,
    sems,
    root_sems,
    out_sem,
    ready_sem,
):
    f32 = jnp.float32
    me, z = lax.axis_index("dp"), lax.axis_index("tensor")
    rows = prior.shape[0]
    part_rows = gram_z.shape[1]
    levels = n_dp.bit_length() - 1

    def dp_of(k):
        return lax.rem(me + k, n_dp)

    def tp_of(k):
        return lax.rem(z + k, n_tp)

    width = act_hbm.shape[1]
    near = z + 1 - 2 * lax.rem(z, 2)
    far = z + 2 - 4 * (z // 2)
    diagonal = near + 2 - 4 * (near // 2)
    order = (diagonal, far, near, z)
    used = []

    def load(*pairs):
        for source, target in pairs:
            pltpu.make_async_copy(source, target, load_sem.at[len(used)]).start()
        used.append(None)
        return len(used) - 1

    def drain(ref, sem):
        pltpu.make_async_copy(ref, ref, sem).wait()

    def load_chunk(index):
        span = pl.ds(pl.multiple_of(order[index] * SEQ, SEQ), SEQ)
        into = tokens.at[index]
        return load((act_hbm.at[span], into.at[:, :width]), (out_hbm.at[span], into.at[:, width:]))

    order_load = load((order_hbm, order_ref))
    weight_load = load((wi_hbm, weights.at[:, :width]), (wo_hbm, weights.at[:, width:]))
    chunk_loads = [load_chunk(0)]
    prior_load = load((prior_hbm, prior))
    mix_load = load((mix_hbm, mix_ref))
    chunk_loads += [load_chunk(index) for index in range(1, n_tp)]
    fold_load = load((fold_hbm, fold_ref))

    def tile_of(owner):
        return pl.ds(pl.multiple_of(owner * LANES, LANES), LANES)

    barrier = pltpu.get_barrier_semaphore()
    for k in range(1, n_tp):
        pl.semaphore_signal(barrier, inc=1, device_id={"tensor": tp_of(k)}, device_id_type=MESH)
    for k in range(1, n_dp):
        pl.semaphore_signal(barrier, inc=1, device_id={"dp": dp_of(k)}, device_id_type=MESH)
    pl.semaphore_wait(barrier, n_dp + n_tp - 2)
    for k in range(1, n_dp):
        pl.semaphore_signal(ready_sem, inc=1, device_id={"dp": dp_of(k)}, device_id_type=MESH)

    half = n_dp // 2
    core, chip = lax.rem(me, 2), me // 2
    partner = me + 1 - 2 * core
    chip_x = chip + 1 - 2 * lax.rem(chip, 2)
    chip_y = chip + 2 - 4 * (chip // 2)
    chip_d = half - 1 - chip

    PAIR, NODE, MID, LAST, SIDE, SLICE, ROW, PEER, SUM, SCATTER, ALONG, GATHER, MIX = range(13)

    def push(phase, source, target, **device):
        pltpu.make_async_remote_copy(
            src_ref=source,
            dst_ref=target,
            send_sem=sems.at[0, phase],
            recv_sem=sems.at[1, phase],
            device_id=device,
            device_id_type=MESH,
        ).start()

    def received(phase, ref):
        drain(ref, sems.at[1, phase])

    for q in range(half):
        push(PAIR, prior_hbm.at[:, tile_of(2 * q + 1 - core)], pair_in.at[q], dp=partner)

    def exchange(axis, phase, source, target):
        size, other = (n_tp, tp_of) if axis == "tensor" else (n_dp, dp_of)
        for k in range(1, size):
            push(phase, source(other(k)), target, **{axis: other(k)})

    def exchange_all(phase, source, target):
        for j in sorted(range(n_tp), key=lambda j: -min(j, n_tp - j)):
            for k in range(n_dp):
                if (j, k) != (0, 0):
                    push(phase, source(dp_of(k), tp_of(j)), target, dp=dp_of(k), tensor=tp_of(j))

    def sides_of_chunk(index):
        drain(tokens.at[index], load_sem.at[chunk_loads[index]])
        mid = SEQ // 2
        spans = [slice(h * mid, (h + 1) * mid) for h in range(2)]
        right = [dot_flip(tokens[index, span, width:], weights[:, width:]) for span in spans]
        left = [dot_flip(tokens[index, span, :width], weights[:, :width]) for span in spans]
        return jnp.concatenate([jnp.concatenate(pair, axis=1) for pair in zip(left, right)], axis=0)

    drain(weights, load_sem.at[weight_load])
    zsend[0] = sides_of_chunk(0)
    token_halves = (slice(0, SEQ // 2), slice(SEQ // 2, SEQ))
    for phase, span in zip((MID, LAST), token_halves):
        push(phase, zsend.at[0, span], zmid.at[span], tensor=near)
    far_sides = sides_of_chunk(1)

    drain(order_ref, load_sem.at[order_load])
    drain(prior, load_sem.at[prior_load])
    drain(mix_ref, load_sem.at[mix_load])
    received(PAIR, pair_in)
    first_mix, second_mix = mix_ref[:, :rows], mix_ref[:, rows:]
    own_first = order_ref[0, 2 * chip] == core
    own_half = [prior[:, tile_of(2 * q + core)] for q in range(half)]
    firsts = [jnp.where(own_first, own_half[q], pair_in[q]) for q in range(half)]
    seconds = [jnp.where(own_first, pair_in[q], own_half[q]) for q in range(half)]
    first_halves, second_halves = halves(first_mix), halves(second_mix)
    mixed = dot_halves(first_halves, halves(jnp.concatenate(firsts, axis=1)))
    mixed = mixed + dot_halves(second_halves, halves(jnp.concatenate(seconds, axis=1)))
    for q in range(half):
        node_send[q] = mixed[:, q * LANES : (q + 1) * LANES]
    for other in (chip_x, chip_y, chip_d):
        push(NODE, node_send.at[other], node_recv.at[chip], dp=2 * other + core)
    node_recv[chip] = node_send[chip]
    for phase, span in zip((MID, LAST), token_halves):
        received(phase, zmid.at[span])
        zsend[1, span] = far_sides[span] + zmid[span]
        push(SIDE, zsend.at[1, span], zrecv.at[1, span], tensor=far)
    zsend[2] = sides_of_chunk(2)
    push(SIDE, zsend.at[2], zrecv.at[0], tensor=near)
    own_sides = sides_of_chunk(3)

    drain(fold_ref, load_sem.at[fold_load])
    fold_rows = fold_ref[...]
    paths = [[jnp.concatenate([dot_rows(fold_rows, first_mix), dot_rows(fold_rows, second_mix)], axis=0)]]
    for level in range(1, levels):
        paths.append(
            [dot_rows(p, first_mix) for p in paths[-1]] + [dot_rows(p, second_mix) for p in paths[-1]]
        )
    paths = [[stacked(p, (0, 0, 1)).T.astype(jnp.bfloat16) for p in level] for level in paths]
    fold = fold_rows.T

    received(SIDE, zrecv)
    sides = (own_sides + zrecv[0]) + zrecv[1]
    lane = lax.broadcasted_iota(jnp.int32, sides.shape, 1)
    doubled = jnp.where(lane < RANK, sides, pltpu.roll(sides, RANK, 1))
    product = dot_mid(sides.T, doubled) / jnp.sqrt(f32(SEQ))
    product = jnp.where(z < count_ref[0], product, jnp.zeros_like(product))
    full[...] = product[RANK:]
    even = full[pl.ds(0, RANK // 2, stride=2), :]
    odd = full[pl.ds(1, RANK // 2, stride=2), :]
    lane = lax.broadcasted_iota(jnp.int32, even.shape, 1)
    mine = jnp.where(lane < RANK, even, odd)
    for row in range(n_tp * n_dp):
        grads_rows[row] = mine[row : row + 1]
    for index in range(n_tp):
        slices_send[index] = mine[index * n_dp : (index + 1) * n_dp]
    grads[z] = slices_send[z]
    slot = me * n_tp + z
    grads_all[slot] = grads_rows[z * n_dp + me]
    pl.semaphore_wait(ready_sem, n_dp - 1)
    exchange_all(ROW, lambda d, t: grads_rows.at[t * n_dp + d], grads_all.at[slot])
    exchange("tensor", SLICE, lambda t: slices_send.at[t], grads.at[z])

    flags = [
        [order_ref[0, j * 2 ** (level + 1) + 2**level - 1] == 1 for j in range(n_dp >> (level + 1))]
        for level in range(levels)
    ]

    def pick(flip, lower, upper):
        first = [jnp.where(flip, b, a) for a, b in zip(lower, upper)]
        return first, [jnp.where(flip, a, b) for a, b in zip(lower, upper)]

    def total(value):
        return jnp.sum(jnp.sum(value, axis=0, keepdims=True), axis=1, keepdims=True)

    received(NODE, node_recv.at[: half - 1])
    mixtures = [[[node_recv[j]] for j in range(half)]]
    for level in range(1, levels):
        below = mixtures[-1]
        sides_of = [pick(flags[level][j], below[2 * j], below[2 * j + 1]) for j in range(len(below) // 2)]
        count = len(below[0])
        left = dot_halves(first_halves, halves(jnp.concatenate([v for f, _ in sides_of for v in f], axis=1)))
        right = dot_halves(second_halves, halves(jnp.concatenate([v for _, g in sides_of for v in g], axis=1)))
        mixtures.append(
            [
                [
                    side[:, (j * count + i) * LANES : (j * count + i + 1) * LANES]
                    for side in (left, right)
                    for i in range(count)
                ]
                for j in range(len(sides_of))
            ]
        )

    for index, part in enumerate(mixtures[-1][0]):
        mix_send[index] = part
    push(MIX, mix_send, mix_recv, dp=partner)

    received(SLICE, grads.at[: n_tp - 1])
    leaf_square = jnp.zeros((rows, LANES), f32)
    for tile in range(n_dp):
        leaf = prior[:, tile * LANES : (tile + 1) * LANES]
        for e in range(n_tp):
            step = grads[e, tile : tile + 1, :]
            grads_out[e : e + 1, tile * LANES : (tile + 1) * LANES] = step
            leaf = leaf + fold[:, e : e + 1] * step
        leaf_square = leaf_square + leaf * leaf
    own_mass = total(leaf_square)

    received(ROW, grads_all.at[: n_tp * n_dp - 1])
    push(PEER, grads_all, peer_all, dp=partner)

    def steps_from(rows_of):
        steps_of = [
            [jnp.concatenate([rows_of[r * n_tp + e] for e in range(n_tp)], axis=0)] for r in range(n_dp)
        ]
        return steps_of, jnp.concatenate([step[0] for step in steps_of], axis=0)

    def merge_steps(level, steps_of):
        merged_steps = []
        for j in range(len(steps_of) // 2):
            first, second = pick(flags[level][j], steps_of[2 * j], steps_of[2 * j + 1])
            if level == 0:
                merged_steps.append([jnp.concatenate([first[0], second[0]], axis=0)])
            else:
                merged_steps.append(first + second)
        return merged_steps

    def updates_of(level, merged_steps):
        return [
            jnp.dot(
                path,
                jnp.concatenate([stacked(g[i], (0, 1, 0)) for g in merged_steps], axis=1).astype(jnp.bfloat16),
                preferred_element_type=f32,
            )
            for i, path in enumerate(paths[level])
        ]

    steps_of, every = steps_from(grads_all)
    sums, products, nodes = [], [], []
    for level in range(levels):
        level_products, level_nodes = [], []
        merged_steps = merge_steps(level, steps_of)
        updates = updates_of(level, merged_steps)
        for j in range(len(merged_steps)):
            parts = [
                v + update[:, j * LANES : (j + 1) * LANES]
                for v, update in zip(mixtures[level][j], updates)
            ]
            index_of = {}
            for a in range(len(parts)):
                for b in range(a + 1):
                    index_of[a, b] = n_dp + len(sums)
                    sums.append(total(parts[a] * parts[b]))
            level_products.append(index_of)
            level_nodes.append(parts)
        steps_of = merged_steps
        products.append(level_products)
        nodes = level_nodes
    lane = lax.broadcasted_iota(jnp.int32, (1, LANES), 1)
    packed = jnp.where(lane == me, own_mass, jnp.zeros((1, LANES), f32))
    for index, value in enumerate(sums):
        packed = jnp.where(lane == n_dp + index, value, packed)
    sums_all[slot] = packed
    exchange_all(SUM, lambda d, t: sums_all.at[slot], sums_all.at[slot])
    received(PEER, peer_all)
    received(MIX, mix_recv)
    steps_of, peer_every = steps_from(peer_all)
    for level in range(levels):
        steps_of = merge_steps(level, steps_of)
    peer_parts = [mix_recv[i] + update for i, update in enumerate(updates_of(levels - 1, steps_of))]
    every_halves = halves(jnp.concatenate([every, peer_every], axis=1))
    received(SUM, sums_all.at[: n_tp * n_dp - 1])
    parts_of = [sums_all[index] for index in range(n_tp * n_dp)]
    while len(parts_of) > 1:
        parts_of = [a + b for a, b in zip(parts_of[0::2], parts_of[1::2])]
    packed = parts_of[0]

    def summed(index):
        return jnp.sum(jnp.where(lane == index, packed, 0.0), axis=1, keepdims=True)

    masses = [summed(index) for index in range(n_dp)]
    scales = [[jnp.ones((1, 1), f32)] for _ in range(n_dp)]
    for level in range(levels):
        new_masses, new_scales = [], []
        for j, products_of in enumerate(products[level]):
            flip = flags[level][j]
            lower, upper = scales[2 * j], scales[2 * j + 1]
            if level == 0:
                coefs = [jnp.ones((1, 1), f32)]
            else:
                coefs = [jnp.where(flip, b, a) for a, b in zip(lower, upper)]
                coefs += [jnp.where(flip, a, b) for a, b in zip(lower, upper)]
            square = jnp.zeros((1, 1), f32)
            for (a, b), index in products_of.items():
                term = coefs[a] * (coefs[b] * summed(index))
                square = square + (term if a == b else 2.0 * term)
            mass = masses[2 * j] + masses[2 * j + 1]
            scale = jnp.sqrt(mass / (jnp.maximum(square, 0.0) + 1e-06))
            trace = scale * scale * square
            new_masses.append(mass)
            new_scales.append([scale * c for c in coefs])
        masses, scales = new_masses, new_scales
    chunks = []
    for parts in (nodes[0], peer_parts):
        chunk = scales[0][0] * parts[0]
        for c, part in zip(scales[0][1:], parts[1:]):
            chunk = chunk + c * part
        chunks.append(chunk)
    root[:, tile_of(me)] = chunks[0]
    root[:, tile_of(partner)] = chunks[1]

    chunk_halves = halves(jnp.concatenate(chunks, axis=1))
    upper_halves, lower_halves = [[v[s] for v in chunk_halves] for s in (slice(0, LANES), slice(LANES, rows))]
    targets = dot_flip_halves(every_halves, chunk_halves)
    unit = rows / trace
    triangle = jnp.concatenate(
        [
            dot_flip_halves(chunk_halves, upper_halves),
            dot_flip_halves(lower_halves, lower_halves),
            targets[:, :LANES],
            targets[:, LANES:],
        ],
        axis=0,
    )
    for r in range(n_dp):
        gram_part[r] = unit * triangle[r * part_rows : (r + 1) * part_rows]
    gram_rs[chip] = gram_part[me]
    for other in (chip_d, chip_x, chip_y):
        push(SCATTER, gram_part.at[2 * other + core], gram_rs.at[chip], dp=2 * other + core)
    dev_x, dev_y, dev_d = (2 * other + core for other in (chip_x, chip_y, chip_d))
    upper, lower = pl.ds(0, rows // 2), pl.ds(rows // 2, rows // 2)

    def relay(index, owner, device, span=slice(None)):
        block_of = root.at[span, tile_of(owner)]
        pltpu.make_async_remote_copy(
            src_ref=block_of,
            dst_ref=block_of,
            send_sem=root_sems.at[5],
            recv_sem=root_sems.at[index],
            device_id={"dp": device},
            device_id_type=MESH,
        ).start()

    def relayed(index, count):
        drain(root.at[:, : count * LANES] if count else root.at[upper, :LANES], root_sems.at[index])

    relay(0, me, dev_x)
    relay(1, me, dev_y)
    received(SCATTER, gram_rs.at[: half - 1])
    part = gram_rs[0]
    for index in range(1, half):
        part = part + gram_rs[index]
    gram_z[z] = part
    exchange("tensor", ALONG, lambda t: gram_z.at[z], gram_z.at[z])
    received(ALONG, gram_z.at[: n_tp - 1])
    part = gram_z[0]
    for index in range(1, n_tp):
        part = part + gram_z[index]
    gram_all[me] = part
    exchange("dp", GATHER, lambda t: gram_all.at[me], gram_all.at[me])
    relayed(0, 1)
    relay(2, dev_x, dev_y, upper)
    relay(4, dev_x, partner)
    relayed(1, 1)
    relay(3, dev_y, dev_x, lower)
    relay(4, dev_y, partner)
    for phase, ref in (
        (PAIR, pair_in),
        (NODE, node_recv.at[: half - 1]),
        (MID, zmid.at[: SEQ // 2]),
        (LAST, zmid.at[SEQ // 2 :]),
        (SIDE, zrecv),
        (SLICE, grads.at[: n_tp - 1]),
        (ROW, grads_all.at[: n_tp * n_dp - 1]),
        (SUM, sums_all.at[: n_tp * n_dp - 1]),
        (PEER, peer_all),
        (MIX, mix_recv),
        (SCATTER, gram_rs.at[: half - 1]),
        (ALONG, gram_z.at[: n_tp - 1]),
    ):
        drain(ref, sems.at[0, phase])
    received(GATHER, gram_all.at[: n_dp - 1])
    triangle = jnp.concatenate([gram_all[r] for r in range(n_dp)], axis=0)
    corner = triangle[LANES:rows]
    gram = jnp.concatenate(
        [
            jnp.concatenate([triangle[:LANES], corner.T], axis=1),
            jnp.concatenate([corner, triangle[rows : rows + LANES]], axis=1),
        ],
        axis=0,
    )
    targets = triangle[rows + LANES :]
    target = jnp.zeros((n_tp, rows), f32)
    for r in range(n_dp):
        span = slice(r * n_tp, (r + 1) * n_tp)
        both = [targets[: n_dp * n_tp][span], targets[n_dp * n_tp :][span]]
        target = jnp.where(me == r, jnp.concatenate(both, axis=1), target)

    def between(index):
        if index == 2:
            relayed(2, 0)
            relayed(3, 0)
            relay(4, dev_d, partner)

    solved_out[...] = solve(gram, target, between)
    drain(gram_all.at[: n_dp - 1], sems.at[0, GATHER])
    relayed(4, half - 1)
    root_write = pltpu.make_async_copy(root, root_out, out_sem.at[0])
    root_write.start()
    drain(root.at[:, : (n_dp - 2) * LANES], root_sems.at[5])
    root_write.wait()


def last_kernel(root_ref, solved_ref, grads_ref, root_out, pre_out, pre, sem):
    write = pltpu.make_async_copy(root_ref, root_out, sem.at[0])
    write.start()
    pre[...] = grads_ref[...] - dot_mid(solved_ref[...], root_ref[...])
    pre_write = pltpu.make_async_copy(pre, pre_out, sem.at[1])
    pre_write.start()
    write.wait()
    pre_write.wait()


def fused_body(
    activations,
    out_grads,
    input_proj,
    grad_proj,
    example_count,
    child_order,
    prior_sketch,
    fold_map,
    merge_mix,
):
    n_dp, n_tp = lax.axis_size("dp"), lax.axis_size("tensor")
    rows, columns = prior_sketch.shape
    slots = activations.shape[0] // SEQ
    f32, bf16 = jnp.float32, jnp.bfloat16
    width, hidden = activations.shape[1], out_grads.shape[1]
    hbm = pl.BlockSpec(memory_space=pltpu.HBM)
    anywhere = pl.BlockSpec(memory_space=pl.ANY)
    vmem = pl.BlockSpec(memory_space=pltpu.VMEM)
    smem = pl.BlockSpec(memory_space=pltpu.SMEM)
    devices = n_dp * n_tp
    part_rows = (3 * LANES + 2 * n_dp * slots) // n_dp
    pin = functools.partial(pltpu.with_memory_space_constraint, memory_space=pltpu.HBM)
    root, solved, grads = pl.pallas_call(
        functools.partial(fused_kernel, n_dp, n_tp),
        out_shape=(
            jax.ShapeDtypeStruct((rows, columns), f32),
            jax.ShapeDtypeStruct((slots, rows), f32),
            jax.ShapeDtypeStruct((slots, columns), f32),
        ),
        in_specs=[hbm, hbm, hbm, hbm, smem, hbm, hbm, hbm, hbm],
        out_specs=(anywhere, vmem, vmem),
        scratch_shapes=[
            pltpu.VMEM((slots, SEQ, width + hidden), bf16),
            pltpu.VMEM((RANK, width + hidden), bf16),
            pltpu.SMEM((1, n_dp), jnp.int32),
            pltpu.VMEM((rows, columns), f32),
            pltpu.VMEM((slots, rows), f32),
            pltpu.VMEM((rows, 2 * rows), f32),
            pltpu.VMEM((n_dp // 2, rows, LANES), f32),
            pltpu.VMEM((n_dp // 2, rows, LANES), f32),
            pltpu.VMEM((n_dp // 2, rows, LANES), f32),
            pltpu.VMEM((3, SEQ, LANES), f32),
            pltpu.VMEM((SEQ, LANES), f32),
            pltpu.VMEM((2, SEQ, LANES), f32),
            pltpu.VMEM((RANK, LANES), f32),
            pltpu.VMEM((n_tp, n_dp, LANES), f32),
            pltpu.VMEM((n_tp, n_dp, LANES), f32),
            pltpu.VMEM((devices, 1, LANES), f32),
            pltpu.VMEM((devices, 1, LANES), f32),
            pltpu.VMEM((devices, 1, LANES), f32),
            pltpu.VMEM((n_dp // 2, rows, LANES), f32),
            pltpu.VMEM((n_dp // 2, rows, LANES), f32),
            pltpu.VMEM((devices, 1, LANES), f32),
            pltpu.VMEM((rows, columns), f32),
            pltpu.VMEM((n_dp, part_rows, LANES), f32),
            pltpu.VMEM((n_dp // 2, part_rows, LANES), f32),
            pltpu.VMEM((n_tp, part_rows, LANES), f32),
            pltpu.VMEM((n_dp, part_rows, LANES), f32),
            pltpu.SemaphoreType.DMA((9,)),
            pltpu.SemaphoreType.DMA((2, 13)),
            pltpu.SemaphoreType.DMA((6,)),
            pltpu.SemaphoreType.DMA((1,)),
            pltpu.SemaphoreType.REGULAR,
        ],
        compiler_params=pltpu.CompilerParams(
            collective_id=0, has_side_effects=True, vmem_limit_bytes=32 * 2**20
        ),
    )(
        pin(activations),
        pin(out_grads),
        pin(input_proj.T),
        pin(grad_proj.T),
        example_count,
        pin(child_order.reshape(1, n_dp)),
        pin(prior_sketch),
        pin(fold_map.T),
        pin(merge_mix),
    )
    return pl.pallas_call(
        last_kernel,
        out_shape=(
            jax.ShapeDtypeStruct((rows, columns), f32),
            jax.ShapeDtypeStruct((slots, columns), f32),
        ),
        in_specs=[vmem] * 3,
        out_specs=(anywhere, anywhere),
        scratch_shapes=[pltpu.VMEM((slots, columns), f32), pltpu.SemaphoreType.DMA((2,))],
        compiler_params=pltpu.CompilerParams(vmem_limit_bytes=16 * 2**20),
    )(root, solved, grads)


def from_partner(value, axis, stride):
    mask = 2**stride
    pairs = [(source, source ^ mask) for source in range(lax.axis_size(axis))]
    return lax.ppermute(value, axis, pairs)


def body(
    activations,
    out_grads,
    input_proj,
    grad_proj,
    example_count,
    child_order,
    prior_sketch,
    fold_map,
    merge_mix,
):
    tensor_count = lax.axis_size("tensor")
    own_rank = RANK // tensor_count
    example_slots = activations.shape[0] // SEQ
    sketch_rows = prior_sketch.shape[0]
    input_part = jnp.dot(activations, input_proj, preferred_element_type=jnp.float32)
    grad_part = jnp.dot(out_grads, grad_proj, preferred_element_type=jnp.float32)
    input_side, grad_side = lax.psum((input_part, grad_part), "tensor")
    grad_own = lax.dynamic_slice_in_dim(grad_side, lax.axis_index("tensor") * own_rank, own_rank, 1)
    grad_blocks = grad_own.reshape(example_slots, SEQ, own_rank)
    input_blocks = input_side.reshape(example_slots, SEQ, RANK)
    example_grad = jnp.einsum(
        "eta,etb->eab", grad_blocks, input_blocks, precision=lax.Precision.HIGHEST
    )
    example_grad = example_grad.reshape(example_slots, own_rank * RANK) / jnp.sqrt(jnp.float32(SEQ))
    live = jnp.arange(example_slots, dtype=jnp.int32) < example_count[0]
    example_grad = jnp.where(live[:, None], example_grad, jnp.zeros_like(example_grad))
    leaf_node = prior_sketch + jnp.dot(fold_map, example_grad, precision=lax.Precision.HIGHEST)
    leaf_weight = lax.psum(jnp.sum(leaf_node * leaf_node), "tensor")
    mix_first = merge_mix[:, :sketch_rows]
    mix_second = merge_mix[:, sketch_rows:]
    depth_count = lax.axis_size("dp").bit_length() - 1
    rank_index = lax.axis_index("dp")
    sketch_node = leaf_node
    sketch_weight = leaf_weight
    for level_index in range(depth_count):
        sibling_node, sibling_weight = from_partner((sketch_node, sketch_weight), "dp", level_index)
        upper_half = rank_index >> level_index & 1
        block_start = rank_index >> level_index + 1 << level_index + 1
        flip_order = child_order[block_start + (1 << level_index) - 1]
        own_first = upper_half == flip_order
        first = jnp.where(own_first, sketch_node, sibling_node)
        second = jnp.where(own_first, sibling_node, sketch_node)
        first_weight = jnp.where(own_first, sketch_weight, sibling_weight)
        second_weight = jnp.where(own_first, sibling_weight, sketch_weight)
        mixture = jnp.dot(mix_first, first, precision=lax.Precision.HIGHEST) + jnp.dot(
            mix_second, second, precision=lax.Precision.HIGHEST
        )
        mix_total = lax.psum(jnp.sum(mixture * mixture), "tensor")
        sketch_weight = first_weight + second_weight
        sketch_node = mixture * jnp.sqrt(sketch_weight / (mix_total + 1e-06))
    gram_part = jnp.dot(sketch_node, sketch_node.T, precision=lax.Precision.HIGHEST)
    product_part = jnp.dot(sketch_node, example_grad.T, precision=lax.Precision.HIGHEST)
    gram, sketch_grad = lax.psum((gram_part, product_part), "tensor")
    damping = jnp.trace(gram) / sketch_rows
    system = gram + damping * jnp.eye(sketch_rows, dtype=jnp.float32)
    factor = jnp.linalg.cholesky(system)
    solved = jax.scipy.linalg.cho_solve((factor, True), sketch_grad)
    preconditioned = example_grad - jnp.dot(solved.T, sketch_node, precision=lax.Precision.HIGHEST)
    return (sketch_node, preconditioned)


def fits_fused(rows, columns, slots, n_dp, n_tp):
    return (
        columns == n_dp * LANES
        and slots == n_tp
        and 2 * RANK == LANES
        and n_dp == 8
        and n_tp == 4
        and rows == 2 * LANES
        and (3 * LANES + 2 * n_dp * slots) % (8 * n_dp) == 0
    )


def step(*args):
    n_dp, n_tp = lax.axis_size("dp"), lax.axis_size("tensor")
    slots = args[0].shape[0] // SEQ
    rows, columns = args[6].shape
    if fits_fused(rows, columns, slots, n_dp, n_tp):
        return fused_body(*args)
    return body(*args)


def solution(mesh):
    in_specs = (
        P("dp", "tensor"),
        P("dp", "tensor"),
        P("tensor", None),
        P("tensor", None),
        P("dp"),
        P(),
        P("dp", "tensor"),
        P(),
        P(),
    )
    out_specs = (P(None, "tensor"), P("dp", "tensor"))
    return jax.shard_map(step, mesh=mesh, in_specs=in_specs, out_specs=out_specs, check_vma=False)
```

```python
import functools

import jax
import jax.numpy as jnp
from jax import lax
from jax.experimental import pallas as pl
from jax.experimental.pallas import tpu as pltpu
from jax.sharding import PartitionSpec as P

RANK = 64
SEQ = 128
LANES = 128
HIGHEST = lax.Precision.HIGHEST
MESH = pl.DeviceIdType.MESH


def newton_plan(rows):
    low, high = 0.999, (rows + 1) * 1.001
    first = 2.0 / (low + high)
    reach, scales = first * low, []
    while 1.0 - reach > 1e-3:
        grown = reach * (2.0 - reach)
        scale = 2.0 / (1.0 + grown)
        scales.append(scale)
        reach = grown * scale
    return first, scales


def dot_high(left, right):
    return jnp.dot(left, right, precision=HIGHEST, preferred_element_type=jnp.float32)


def dot_flip(left, right):
    return lax.dot_general(left, right, (((1,), (1,)), ((), ())), preferred_element_type=jnp.float32)


def dot_rows(left, right):
    return lax.dot_general(
        left, right, (((1,), (1,)), ((), ())), precision=HIGHEST, preferred_element_type=jnp.float32
    )


def halves(value):
    high = value.astype(jnp.bfloat16)
    return high, (value - high.astype(jnp.float32)).astype(jnp.bfloat16)


def dot_halves(left, right):
    (a, b), (c, d) = left, right
    out = jnp.dot(a, c, preferred_element_type=jnp.float32)
    out = out + jnp.dot(a, d, preferred_element_type=jnp.float32)
    return out + jnp.dot(b, c, preferred_element_type=jnp.float32)


def dot_mid(left, right):
    return dot_halves(halves(left), halves(right))


def dot_flip_halves(left, right):
    (a, b), (c, d) = left, right
    return dot_flip(jnp.concatenate([a, a, b], axis=1), jnp.concatenate([c, d, c], axis=1))


def dot_rows_halved(left, right):
    (a, b), (c, d) = left, right
    left = jnp.concatenate([a, a, b], axis=1)
    right = jnp.concatenate([c, d, c], axis=0)
    half = left.shape[0] // 2
    return jnp.concatenate(
        [
            jnp.dot(left[:half], right, preferred_element_type=jnp.float32),
            jnp.dot(left[half:], right, preferred_element_type=jnp.float32),
        ],
        axis=0,
    )


def thirds(value):
    high = value.astype(jnp.bfloat16)
    return (high, *halves(value - high.astype(jnp.float32)))


def dot_thirds(left, right):
    count = left.shape[0]
    stack = jnp.concatenate(thirds(left), axis=0)
    a, b, c = (jnp.dot(stack, part, preferred_element_type=jnp.float32) for part in thirds(right))
    high = a[count : 2 * count] + b[:count]
    low = (a[2 * count :] + b[count : 2 * count]) + c[:count]
    return a[:count] + (high + low)


def stacked(value, order):
    high = value.astype(jnp.bfloat16).astype(jnp.float32)
    both = (high, value - high)
    return jnp.concatenate([both[i] for i in order], axis=0)


def solve(gram, target):
    rows = gram.shape[0]
    eye = lax.broadcasted_iota(jnp.int32, gram.shape, 0) == lax.broadcasted_iota(jnp.int32, gram.shape, 1)
    system = gram + jnp.where(eye, 1.0, 0.0)
    first, scales = newton_plan(rows)
    state, solved, path = first * system, first * target, None
    for index, scale in enumerate(scales):
        factor = jnp.where(eye, 2.0 * scale, 0.0) - scale * state
        factor_halves = halves(factor)
        solved = dot_halves(halves(solved), factor_halves)
        if index < len(scales) - 1:
            state = dot_rows_halved(halves(state), factor_halves)
            if path is None:
                path = factor_halves[0]
            else:
                path = jnp.dot(path, factor_halves[0], preferred_element_type=jnp.float32)
                path = path.astype(jnp.bfloat16)
    rest = (first * (target - dot_thirds(solved, system))).astype(jnp.bfloat16)
    step = jnp.dot(rest, path, preferred_element_type=jnp.float32)
    return solved + dot_halves(halves(step), factor_halves)


def fused_kernel(
    n_dp,
    n_tp,
    act_hbm,
    out_hbm,
    wi_hbm,
    wo_hbm,
    count_ref,
    order_hbm,
    prior_hbm,
    fold_hbm,
    mix_hbm,
    root_out,
    solved_out,
    grads_out,
    tokens,
    weights,
    order_ref,
    prior,
    fold_ref,
    mix_ref,
    pair_in,
    node_send,
    node_recv,
    zsend,
    zmid,
    zrecv,
    full,
    slices_send,
    grads,
    grads_rows,
    grads_all,
    peer_all,
    mix_send,
    mix_recv,
    sums_all,
    root,
    gram_part,
    gram_rs,
    gram_z,
    gram_all,
    load_sem,
    sems,
    root_sems,
    out_sem,
    ready_sem,
):
    f32 = jnp.float32
    me, z = lax.axis_index("dp"), lax.axis_index("tensor")
    rows = prior.shape[0]
    part_rows = gram_z.shape[1]
    levels = n_dp.bit_length() - 1

    def dp_of(k):
        return lax.rem(me + k, n_dp)

    def tp_of(k):
        return lax.rem(z + k, n_tp)

    width = act_hbm.shape[1]
    near = z + 1 - 2 * lax.rem(z, 2)
    far = z + 2 - 4 * (z // 2)
    diagonal = near + 2 - 4 * (near // 2)
    order = (diagonal, far, near, z)
    used = []

    def load(*pairs):
        for source, target in pairs:
            pltpu.make_async_copy(source, target, load_sem.at[len(used)]).start()
        used.append(None)
        return len(used) - 1

    def drain(ref, sem):
        pltpu.make_async_copy(ref, ref, sem).wait()

    def load_chunk(index):
        span = pl.ds(pl.multiple_of(order[index] * SEQ, SEQ), SEQ)
        into = tokens.at[index]
        return load((act_hbm.at[span], into.at[:, :width]), (out_hbm.at[span], into.at[:, width:]))

    order_load = load((order_hbm, order_ref))
    weight_load = load((wi_hbm, weights.at[:, :width]), (wo_hbm, weights.at[:, width:]))
    chunk_loads = [load_chunk(0)]
    prior_load = load((prior_hbm, prior))
    mix_load = load((mix_hbm, mix_ref))
    chunk_loads += [load_chunk(index) for index in range(1, n_tp)]
    fold_load = load((fold_hbm, fold_ref))

    def tile_of(owner):
        return pl.ds(pl.multiple_of(owner * LANES, LANES), LANES)

    barrier = pltpu.get_barrier_semaphore()
    for k in range(1, n_tp):
        pl.semaphore_signal(barrier, inc=1, device_id={"tensor": tp_of(k)}, device_id_type=MESH)
    for k in range(1, n_dp):
        pl.semaphore_signal(barrier, inc=1, device_id={"dp": dp_of(k)}, device_id_type=MESH)
    pl.semaphore_wait(barrier, n_dp + n_tp - 2)
    for k in range(1, n_dp):
        pl.semaphore_signal(ready_sem, inc=1, device_id={"dp": dp_of(k)}, device_id_type=MESH)

    half = n_dp // 2
    core, chip = lax.rem(me, 2), me // 2
    partner = me + 1 - 2 * core
    chip_x = chip + 1 - 2 * lax.rem(chip, 2)
    chip_y = chip + 2 - 4 * (chip // 2)
    chip_d = half - 1 - chip

    PAIR, NODE, MID, LAST, SIDE, SLICE, ROW, PEER, SUM, SCATTER, ALONG, GATHER, MIX = range(13)

    def push(phase, source, target, **device):
        pltpu.make_async_remote_copy(
            src_ref=source,
            dst_ref=target,
            send_sem=sems.at[0, phase],
            recv_sem=sems.at[1, phase],
            device_id=device,
            device_id_type=MESH,
        ).start()

    def received(phase, ref):
        drain(ref, sems.at[1, phase])

    for q in range(half):
        push(PAIR, prior_hbm.at[:, tile_of(2 * q + 1 - core)], pair_in.at[q], dp=partner)

    def exchange(axis, phase, source, target):
        size, other = (n_tp, tp_of) if axis == "tensor" else (n_dp, dp_of)
        for k in range(1, size):
            push(phase, source(other(k)), target, **{axis: other(k)})

    def exchange_all(phase, source, target):
        for j in sorted(range(n_tp), key=lambda j: -min(j, n_tp - j)):
            for k in range(n_dp):
                if (j, k) != (0, 0):
                    push(phase, source(dp_of(k), tp_of(j)), target, dp=dp_of(k), tensor=tp_of(j))

    def sides_of_chunk(index):
        drain(tokens.at[index], load_sem.at[chunk_loads[index]])
        mid = SEQ // 2
        spans = [slice(h * mid, (h + 1) * mid) for h in range(2)]
        right = [dot_flip(tokens[index, span, width:], weights[:, width:]) for span in spans]
        left = [dot_flip(tokens[index, span, :width], weights[:, :width]) for span in spans]
        return jnp.concatenate([jnp.concatenate(pair, axis=1) for pair in zip(left, right)], axis=0)

    drain(weights, load_sem.at[weight_load])
    zsend[0] = sides_of_chunk(0)
    token_halves = (slice(0, SEQ // 2), slice(SEQ // 2, SEQ))
    for phase, span in zip((MID, LAST), token_halves):
        push(phase, zsend.at[0, span], zmid.at[span], tensor=near)

    drain(order_ref, load_sem.at[order_load])
    drain(prior, load_sem.at[prior_load])
    drain(mix_ref, load_sem.at[mix_load])
    received(PAIR, pair_in)
    first_mix, second_mix = mix_ref[:, :rows], mix_ref[:, rows:]
    own_first = order_ref[0, 2 * chip] == core
    own_half = [prior[:, tile_of(2 * q + core)] for q in range(half)]
    firsts = [jnp.where(own_first, own_half[q], pair_in[q]) for q in range(half)]
    seconds = [jnp.where(own_first, pair_in[q], own_half[q]) for q in range(half)]
    first_halves, second_halves = halves(first_mix), halves(second_mix)
    mixed = dot_halves(first_halves, halves(jnp.concatenate(firsts, axis=1)))
    mixed = mixed + dot_halves(second_halves, halves(jnp.concatenate(seconds, axis=1)))
    for q in range(half):
        node_send[q] = mixed[:, q * LANES : (q + 1) * LANES]
    for other in (chip_x, chip_y, chip_d):
        push(NODE, node_send.at[other], node_recv.at[chip], dp=2 * other + core)
    node_recv[chip] = node_send[chip]
    far_sides = sides_of_chunk(1)
    for phase, span in zip((MID, LAST), token_halves):
        received(phase, zmid.at[span])
        zsend[1, span] = far_sides[span] + zmid[span]
        push(SIDE, zsend.at[1, span], zrecv.at[1, span], tensor=far)
    zsend[2] = sides_of_chunk(2)
    push(SIDE, zsend.at[2], zrecv.at[0], tensor=near)
    own_sides = sides_of_chunk(3)

    drain(fold_ref, load_sem.at[fold_load])
    fold_rows = fold_ref[...]
    paths = [[jnp.concatenate([dot_rows(fold_rows, first_mix), dot_rows(fold_rows, second_mix)], axis=0)]]
    for level in range(1, levels):
        paths.append(
            [dot_rows(p, first_mix) for p in paths[-1]] + [dot_rows(p, second_mix) for p in paths[-1]]
        )
    paths = [[stacked(p, (0, 0, 1)).T.astype(jnp.bfloat16) for p in level] for level in paths]
    fold = fold_rows.T

    received(SIDE, zrecv)
    sides = (own_sides + zrecv[0]) + zrecv[1]
    lane = lax.broadcasted_iota(jnp.int32, sides.shape, 1)
    doubled = jnp.where(lane < RANK, sides, pltpu.roll(sides, RANK, 1))
    product = dot_mid(sides.T, doubled) / jnp.sqrt(f32(SEQ))
    product = jnp.where(z < count_ref[0], product, jnp.zeros_like(product))
    full[...] = product[RANK:]
    even = full[pl.ds(0, RANK // 2, stride=2), :]
    odd = full[pl.ds(1, RANK // 2, stride=2), :]
    lane = lax.broadcasted_iota(jnp.int32, even.shape, 1)
    mine = jnp.where(lane < RANK, even, odd)
    for row in range(n_tp * n_dp):
        grads_rows[row] = mine[row : row + 1]
    for index in range(n_tp):
        slices_send[index] = mine[index * n_dp : (index + 1) * n_dp]
    grads[z] = slices_send[z]
    slot = me * n_tp + z
    grads_all[slot] = grads_rows[z * n_dp + me]
    pl.semaphore_wait(ready_sem, n_dp - 1)
    exchange("tensor", SLICE, lambda t: slices_send.at[t], grads.at[z])
    exchange_all(ROW, lambda d, t: grads_rows.at[t * n_dp + d], grads_all.at[slot])

    flags = [
        [order_ref[0, j * 2 ** (level + 1) + 2**level - 1] == 1 for j in range(n_dp >> (level + 1))]
        for level in range(levels)
    ]

    def pick(flip, lower, upper):
        first = [jnp.where(flip, b, a) for a, b in zip(lower, upper)]
        return first, [jnp.where(flip, a, b) for a, b in zip(lower, upper)]

    def total(value):
        return jnp.sum(jnp.sum(value, axis=0, keepdims=True), axis=1, keepdims=True)

    received(NODE, node_recv.at[: half - 1])
    mixtures = [[[node_recv[j]] for j in range(half)]]
    for level in range(1, levels):
        below = mixtures[-1]
        sides_of = [pick(flags[level][j], below[2 * j], below[2 * j + 1]) for j in range(len(below) // 2)]
        count = len(below[0])
        left = dot_halves(first_halves, halves(jnp.concatenate([v for f, _ in sides_of for v in f], axis=1)))
        right = dot_halves(second_halves, halves(jnp.concatenate([v for _, g in sides_of for v in g], axis=1)))
        mixtures.append(
            [
                [
                    side[:, (j * count + i) * LANES : (j * count + i + 1) * LANES]
                    for side in (left, right)
                    for i in range(count)
                ]
                for j in range(len(sides_of))
            ]
        )

    for index, part in enumerate(mixtures[-1][0]):
        mix_send[index] = part
    push(MIX, mix_send, mix_recv, dp=partner)

    received(SLICE, grads.at[: n_tp - 1])
    leaf_square = jnp.zeros((rows, LANES), f32)
    for tile in range(n_dp):
        leaf = prior[:, tile * LANES : (tile + 1) * LANES]
        for e in range(n_tp):
            step = grads[e, tile : tile + 1, :]
            grads_out[e : e + 1, tile * LANES : (tile + 1) * LANES] = step
            leaf = leaf + fold[:, e : e + 1] * step
        leaf_square = leaf_square + leaf * leaf
    own_mass = total(leaf_square)

    received(ROW, grads_all.at[: n_tp * n_dp - 1])
    push(PEER, grads_all, peer_all, dp=partner)

    def steps_from(rows_of):
        steps_of = [
            [jnp.concatenate([rows_of[r * n_tp + e] for e in range(n_tp)], axis=0)] for r in range(n_dp)
        ]
        return steps_of, jnp.concatenate([step[0] for step in steps_of], axis=0)

    def merge_steps(level, steps_of):
        merged_steps = []
        for j in range(len(steps_of) // 2):
            first, second = pick(flags[level][j], steps_of[2 * j], steps_of[2 * j + 1])
            if level == 0:
                merged_steps.append([jnp.concatenate([first[0], second[0]], axis=0)])
            else:
                merged_steps.append(first + second)
        return merged_steps

    def updates_of(level, merged_steps):
        return [
            jnp.dot(
                path,
                jnp.concatenate([stacked(g[i], (0, 1, 0)) for g in merged_steps], axis=1).astype(jnp.bfloat16),
                preferred_element_type=f32,
            )
            for i, path in enumerate(paths[level])
        ]

    steps_of, every = steps_from(grads_all)
    sums, products, nodes = [], [], []
    for level in range(levels):
        level_products, level_nodes = [], []
        merged_steps = merge_steps(level, steps_of)
        updates = updates_of(level, merged_steps)
        for j in range(len(merged_steps)):
            parts = [
                v + update[:, j * LANES : (j + 1) * LANES]
                for v, update in zip(mixtures[level][j], updates)
            ]
            index_of = {}
            for a in range(len(parts)):
                for b in range(a + 1):
                    index_of[a, b] = n_dp + len(sums)
                    sums.append(total(parts[a] * parts[b]))
            level_products.append(index_of)
            level_nodes.append(parts)
        steps_of = merged_steps
        products.append(level_products)
        nodes = level_nodes
    lane = lax.broadcasted_iota(jnp.int32, (1, LANES), 1)
    packed = jnp.where(lane == me, own_mass, jnp.zeros((1, LANES), f32))
    for index, value in enumerate(sums):
        packed = jnp.where(lane == n_dp + index, value, packed)
    sums_all[slot] = packed
    exchange_all(SUM, lambda d, t: sums_all.at[slot], sums_all.at[slot])
    received(PEER, peer_all)
    received(MIX, mix_recv)
    steps_of, peer_every = steps_from(peer_all)
    for level in range(levels):
        steps_of = merge_steps(level, steps_of)
    peer_parts = [mix_recv[i] + update for i, update in enumerate(updates_of(levels - 1, steps_of))]
    every_halves = halves(jnp.concatenate([every, peer_every], axis=1))
    received(SUM, sums_all.at[: n_tp * n_dp - 1])
    parts_of = [sums_all[index] for index in range(n_tp * n_dp)]
    while len(parts_of) > 1:
        parts_of = [a + b for a, b in zip(parts_of[0::2], parts_of[1::2])]
    packed = parts_of[0]

    def summed(index):
        return jnp.sum(jnp.where(lane == index, packed, 0.0), axis=1, keepdims=True)

    masses = [summed(index) for index in range(n_dp)]
    scales = [[jnp.ones((1, 1), f32)] for _ in range(n_dp)]
    for level in range(levels):
        new_masses, new_scales = [], []
        for j, products_of in enumerate(products[level]):
            flip = flags[level][j]
            lower, upper = scales[2 * j], scales[2 * j + 1]
            if level == 0:
                coefs = [jnp.ones((1, 1), f32)]
            else:
                coefs = [jnp.where(flip, b, a) for a, b in zip(lower, upper)]
                coefs += [jnp.where(flip, a, b) for a, b in zip(lower, upper)]
            square = jnp.zeros((1, 1), f32)
            for (a, b), index in products_of.items():
                term = coefs[a] * (coefs[b] * summed(index))
                square = square + (term if a == b else 2.0 * term)
            mass = masses[2 * j] + masses[2 * j + 1]
            scale = jnp.sqrt(mass / (jnp.maximum(square, 0.0) + 1e-06))
            trace = scale * scale * square
            new_masses.append(mass)
            new_scales.append([scale * c for c in coefs])
        masses, scales = new_masses, new_scales
    chunks = []
    for parts in (nodes[0], peer_parts):
        chunk = scales[0][0] * parts[0]
        for c, part in zip(scales[0][1:], parts[1:]):
            chunk = chunk + c * part
        chunks.append(chunk)
    root[:, tile_of(me)] = chunks[0]
    root[:, tile_of(partner)] = chunks[1]

    chunk_halves = halves(jnp.concatenate(chunks, axis=1))
    upper_halves, lower_halves = [[v[s] for v in chunk_halves] for s in (slice(0, LANES), slice(LANES, rows))]
    targets = dot_flip_halves(every_halves, chunk_halves)
    unit = rows / trace
    triangle = jnp.concatenate(
        [
            dot_flip_halves(upper_halves, upper_halves),
            dot_flip_halves(lower_halves, upper_halves),
            dot_flip_halves(lower_halves, lower_halves),
            targets[:, :LANES],
            targets[:, LANES:],
        ],
        axis=0,
    )
    for r in range(n_dp):
        gram_part[r] = unit * triangle[r * part_rows : (r + 1) * part_rows]
    gram_rs[chip] = gram_part[me]
    for other in (chip_d, chip_x, chip_y):
        push(SCATTER, gram_part.at[2 * other + core], gram_rs.at[chip], dp=2 * other + core)
    dev_x, dev_y, dev_d = (2 * other + core for other in (chip_x, chip_y, chip_d))
    upper, lower = pl.ds(0, rows // 2), pl.ds(rows // 2, rows // 2)

    def relay(index, owner, device, span=slice(None)):
        block_of = root.at[span, tile_of(owner)]
        pltpu.make_async_remote_copy(
            src_ref=block_of,
            dst_ref=block_of,
            send_sem=root_sems.at[5],
            recv_sem=root_sems.at[index],
            device_id={"dp": device},
            device_id_type=MESH,
        ).start()

    def relayed(index, count):
        drain(root.at[:, : count * LANES] if count else root.at[upper, :LANES], root_sems.at[index])

    relay(0, me, dev_x)
    relay(1, me, dev_y)
    received(SCATTER, gram_rs.at[: half - 1])
    part = gram_rs[0]
    for index in range(1, half):
        part = part + gram_rs[index]
    gram_z[z] = part
    exchange("tensor", ALONG, lambda t: gram_z.at[z], gram_z.at[z])
    relayed(0, 1)
    relay(2, dev_x, dev_y, upper)
    relay(4, dev_x, partner)
    relayed(1, 1)
    relay(3, dev_y, dev_x, lower)
    relay(4, dev_y, partner)
    received(ALONG, gram_z.at[: n_tp - 1])
    part = gram_z[0]
    for index in range(1, n_tp):
        part = part + gram_z[index]
    gram_all[me] = part
    exchange("dp", GATHER, lambda t: gram_all.at[me], gram_all.at[me])
    relayed(2, 0)
    relayed(3, 0)
    relay(4, dev_d, partner)
    for phase, ref in (
        (PAIR, pair_in),
        (NODE, node_recv.at[: half - 1]),
        (MID, zmid.at[: SEQ // 2]),
        (LAST, zmid.at[SEQ // 2 :]),
        (SIDE, zrecv),
        (SLICE, grads.at[: n_tp - 1]),
        (ROW, grads_all.at[: n_tp * n_dp - 1]),
        (SUM, sums_all.at[: n_tp * n_dp - 1]),
        (PEER, peer_all),
        (MIX, mix_recv),
        (SCATTER, gram_rs.at[: half - 1]),
        (ALONG, gram_z.at[: n_tp - 1]),
    ):
        drain(ref, sems.at[0, phase])
    received(GATHER, gram_all.at[: n_dp - 1])
    triangle = jnp.concatenate([gram_all[r] for r in range(n_dp)], axis=0)
    corner = triangle[LANES:rows]
    gram = jnp.concatenate(
        [
            jnp.concatenate([triangle[:LANES], corner.T], axis=1),
            jnp.concatenate([corner, triangle[rows : rows + LANES]], axis=1),
        ],
        axis=0,
    )
    targets = triangle[rows + LANES :]
    target = jnp.zeros((n_tp, rows), f32)
    for r in range(n_dp):
        span = slice(r * n_tp, (r + 1) * n_tp)
        both = [targets[: n_dp * n_tp][span], targets[n_dp * n_tp :][span]]
        target = jnp.where(me == r, jnp.concatenate(both, axis=1), target)
    solved_out[...] = solve(gram, target)
    drain(gram_all.at[: n_dp - 1], sems.at[0, GATHER])
    relayed(4, half - 1)
    root_write = pltpu.make_async_copy(root, root_out, out_sem.at[0])
    root_write.start()
    drain(root.at[:, : (n_dp - 2) * LANES], root_sems.at[5])
    root_write.wait()


def last_kernel(root_ref, solved_ref, grads_ref, root_out, pre_out, pre, sem):
    write = pltpu.make_async_copy(root_ref, root_out, sem.at[0])
    write.start()
    pre[...] = grads_ref[...] - dot_mid(solved_ref[...], root_ref[...])
    pre_write = pltpu.make_async_copy(pre, pre_out, sem.at[1])
    pre_write.start()
    write.wait()
    pre_write.wait()


def fused_body(
    activations,
    out_grads,
    input_proj,
    grad_proj,
    example_count,
    child_order,
    prior_sketch,
    fold_map,
    merge_mix,
):
    n_dp, n_tp = lax.axis_size("dp"), lax.axis_size("tensor")
    rows, columns = prior_sketch.shape
    slots = activations.shape[0] // SEQ
    f32, bf16 = jnp.float32, jnp.bfloat16
    width, hidden = activations.shape[1], out_grads.shape[1]
    hbm = pl.BlockSpec(memory_space=pltpu.HBM)
    anywhere = pl.BlockSpec(memory_space=pl.ANY)
    vmem = pl.BlockSpec(memory_space=pltpu.VMEM)
    smem = pl.BlockSpec(memory_space=pltpu.SMEM)
    devices = n_dp * n_tp
    part_rows = (3 * LANES + 2 * n_dp * slots) // n_dp
    pin = functools.partial(pltpu.with_memory_space_constraint, memory_space=pltpu.HBM)
    root, solved, grads = pl.pallas_call(
        functools.partial(fused_kernel, n_dp, n_tp),
        out_shape=(
            jax.ShapeDtypeStruct((rows, columns), f32),
            jax.ShapeDtypeStruct((slots, rows), f32),
            jax.ShapeDtypeStruct((slots, columns), f32),
        ),
        in_specs=[hbm, hbm, hbm, hbm, smem, hbm, hbm, hbm, hbm],
        out_specs=(anywhere, vmem, vmem),
        scratch_shapes=[
            pltpu.VMEM((slots, SEQ, width + hidden), bf16),
            pltpu.VMEM((RANK, width + hidden), bf16),
            pltpu.SMEM((1, n_dp), jnp.int32),
            pltpu.VMEM((rows, columns), f32),
            pltpu.VMEM((slots, rows), f32),
            pltpu.VMEM((rows, 2 * rows), f32),
            pltpu.VMEM((n_dp // 2, rows, LANES), f32),
            pltpu.VMEM((n_dp // 2, rows, LANES), f32),
            pltpu.VMEM((n_dp // 2, rows, LANES), f32),
            pltpu.VMEM((3, SEQ, LANES), f32),
            pltpu.VMEM((SEQ, LANES), f32),
            pltpu.VMEM((2, SEQ, LANES), f32),
            pltpu.VMEM((RANK, LANES), f32),
            pltpu.VMEM((n_tp, n_dp, LANES), f32),
            pltpu.VMEM((n_tp, n_dp, LANES), f32),
            pltpu.VMEM((devices, 1, LANES), f32),
            pltpu.VMEM((devices, 1, LANES), f32),
            pltpu.VMEM((devices, 1, LANES), f32),
            pltpu.VMEM((n_dp // 2, rows, LANES), f32),
            pltpu.VMEM((n_dp // 2, rows, LANES), f32),
            pltpu.VMEM((devices, 1, LANES), f32),
            pltpu.VMEM((rows, columns), f32),
            pltpu.VMEM((n_dp, part_rows, LANES), f32),
            pltpu.VMEM((n_dp // 2, part_rows, LANES), f32),
            pltpu.VMEM((n_tp, part_rows, LANES), f32),
            pltpu.VMEM((n_dp, part_rows, LANES), f32),
            pltpu.SemaphoreType.DMA((9,)),
            pltpu.SemaphoreType.DMA((2, 13)),
            pltpu.SemaphoreType.DMA((6,)),
            pltpu.SemaphoreType.DMA((1,)),
            pltpu.SemaphoreType.REGULAR,
        ],
        compiler_params=pltpu.CompilerParams(
            collective_id=0, has_side_effects=True, vmem_limit_bytes=32 * 2**20
        ),
    )(
        pin(activations),
        pin(out_grads),
        pin(input_proj.T),
        pin(grad_proj.T),
        example_count,
        pin(child_order.reshape(1, n_dp)),
        pin(prior_sketch),
        pin(fold_map.T),
        pin(merge_mix),
    )
    return pl.pallas_call(
        last_kernel,
        out_shape=(
            jax.ShapeDtypeStruct((rows, columns), f32),
            jax.ShapeDtypeStruct((slots, columns), f32),
        ),
        in_specs=[vmem] * 3,
        out_specs=(anywhere, anywhere),
        scratch_shapes=[pltpu.VMEM((slots, columns), f32), pltpu.SemaphoreType.DMA((2,))],
        compiler_params=pltpu.CompilerParams(vmem_limit_bytes=16 * 2**20),
    )(root, solved, grads)


def from_partner(value, axis, stride):
    mask = 2**stride
    pairs = [(source, source ^ mask) for source in range(lax.axis_size(axis))]
    return lax.ppermute(value, axis, pairs)


def body(
    activations,
    out_grads,
    input_proj,
    grad_proj,
    example_count,
    child_order,
    prior_sketch,
    fold_map,
    merge_mix,
):
    tensor_count = lax.axis_size("tensor")
    own_rank = RANK // tensor_count
    example_slots = activations.shape[0] // SEQ
    sketch_rows = prior_sketch.shape[0]
    input_part = jnp.dot(activations, input_proj, preferred_element_type=jnp.float32)
    grad_part = jnp.dot(out_grads, grad_proj, preferred_element_type=jnp.float32)
    input_side, grad_side = lax.psum((input_part, grad_part), "tensor")
    grad_own = lax.dynamic_slice_in_dim(grad_side, lax.axis_index("tensor") * own_rank, own_rank, 1)
    grad_blocks = grad_own.reshape(example_slots, SEQ, own_rank)
    input_blocks = input_side.reshape(example_slots, SEQ, RANK)
    example_grad = jnp.einsum(
        "eta,etb->eab", grad_blocks, input_blocks, precision=lax.Precision.HIGHEST
    )
    example_grad = example_grad.reshape(example_slots, own_rank * RANK) / jnp.sqrt(jnp.float32(SEQ))
    live = jnp.arange(example_slots, dtype=jnp.int32) < example_count[0]
    example_grad = jnp.where(live[:, None], example_grad, jnp.zeros_like(example_grad))
    leaf_node = prior_sketch + jnp.dot(fold_map, example_grad, precision=lax.Precision.HIGHEST)
    leaf_weight = lax.psum(jnp.sum(leaf_node * leaf_node), "tensor")
    mix_first = merge_mix[:, :sketch_rows]
    mix_second = merge_mix[:, sketch_rows:]
    depth_count = lax.axis_size("dp").bit_length() - 1
    rank_index = lax.axis_index("dp")
    sketch_node = leaf_node
    sketch_weight = leaf_weight
    for level_index in range(depth_count):
        sibling_node, sibling_weight = from_partner((sketch_node, sketch_weight), "dp", level_index)
        upper_half = rank_index >> level_index & 1
        block_start = rank_index >> level_index + 1 << level_index + 1
        flip_order = child_order[block_start + (1 << level_index) - 1]
        own_first = upper_half == flip_order
        first = jnp.where(own_first, sketch_node, sibling_node)
        second = jnp.where(own_first, sibling_node, sketch_node)
        first_weight = jnp.where(own_first, sketch_weight, sibling_weight)
        second_weight = jnp.where(own_first, sibling_weight, sketch_weight)
        mixture = jnp.dot(mix_first, first, precision=lax.Precision.HIGHEST) + jnp.dot(
            mix_second, second, precision=lax.Precision.HIGHEST
        )
        mix_total = lax.psum(jnp.sum(mixture * mixture), "tensor")
        sketch_weight = first_weight + second_weight
        sketch_node = mixture * jnp.sqrt(sketch_weight / (mix_total + 1e-06))
    gram_part = jnp.dot(sketch_node, sketch_node.T, precision=lax.Precision.HIGHEST)
    product_part = jnp.dot(sketch_node, example_grad.T, precision=lax.Precision.HIGHEST)
    gram, sketch_grad = lax.psum((gram_part, product_part), "tensor")
    damping = jnp.trace(gram) / sketch_rows
    system = gram + damping * jnp.eye(sketch_rows, dtype=jnp.float32)
    factor = jnp.linalg.cholesky(system)
    solved = jax.scipy.linalg.cho_solve((factor, True), sketch_grad)
    preconditioned = example_grad - jnp.dot(solved.T, sketch_node, precision=lax.Precision.HIGHEST)
    return (sketch_node, preconditioned)


def fits_fused(rows, columns, slots, n_dp, n_tp):
    return (
        columns == n_dp * LANES
        and slots == n_tp
        and 2 * RANK == LANES
        and n_dp == 8
        and n_tp == 4
        and rows == 2 * LANES
        and (3 * LANES + 2 * n_dp * slots) % (8 * n_dp) == 0
    )


def step(*args):
    n_dp, n_tp = lax.axis_size("dp"), lax.axis_size("tensor")
    slots = args[0].shape[0] // SEQ
    rows, columns = args[6].shape
    if fits_fused(rows, columns, slots, n_dp, n_tp):
        return fused_body(*args)
    return body(*args)


def solution(mesh):
    in_specs = (
        P("dp", "tensor"),
        P("dp", "tensor"),
        P("tensor", None),
        P("tensor", None),
        P("dp"),
        P(),
        P("dp", "tensor"),
        P(),
        P(),
    )
    out_specs = (P(None, "tensor"), P("dp", "tensor"))
    return jax.shard_map(step, mesh=mesh, in_specs=in_specs, out_specs=out_specs, check_vma=False)
```

```python
import functools

import jax
import jax.numpy as jnp
from jax import lax
from jax.experimental import pallas as pl
from jax.experimental.pallas import tpu as pltpu
from jax.sharding import PartitionSpec as P

RANK = 64
SEQ = 128
LANES = 128
HIGHEST = lax.Precision.HIGHEST
MESH = pl.DeviceIdType.MESH


def newton_plan(rows):
    low, high = 0.999, (rows + 1) * 1.001
    first = 2.0 / (low + high)
    reach, scales = first * low, []
    while 1.0 - reach > 1e-3:
        grown = reach * (2.0 - reach)
        scale = 2.0 / (1.0 + grown)
        scales.append(scale)
        reach = grown * scale
    return first, scales


def dot_high(left, right):
    return jnp.dot(left, right, precision=HIGHEST, preferred_element_type=jnp.float32)


def dot_flip(left, right):
    return lax.dot_general(left, right, (((1,), (1,)), ((), ())), preferred_element_type=jnp.float32)


def halves(value):
    high = value.astype(jnp.bfloat16)
    return high, (value - high.astype(jnp.float32)).astype(jnp.bfloat16)


def dot_halves(left, right):
    (a, b), (c, d) = left, right
    out = jnp.dot(a, c, preferred_element_type=jnp.float32)
    out = out + jnp.dot(a, d, preferred_element_type=jnp.float32)
    return out + jnp.dot(b, c, preferred_element_type=jnp.float32)


def dot_mid(left, right):
    return dot_halves(halves(left), halves(right))


def dot_flip_halves(left, right):
    (a, b), (c, d) = left, right
    return dot_flip(jnp.concatenate([a, a, b], axis=1), jnp.concatenate([c, d, c], axis=1))


def dot_rows_halved(left, right):
    (a, b), (c, d) = left, right
    left = jnp.concatenate([a, a, b], axis=1)
    right = jnp.concatenate([c, d, c], axis=0)
    half = left.shape[0] // 2
    return jnp.concatenate(
        [
            jnp.dot(left[:half], right, preferred_element_type=jnp.float32),
            jnp.dot(left[half:], right, preferred_element_type=jnp.float32),
        ],
        axis=0,
    )


def thirds(value):
    high = value.astype(jnp.bfloat16)
    return (high, *halves(value - high.astype(jnp.float32)))


def dot_thirds(left, right):
    count = left.shape[0]
    stack = jnp.concatenate(thirds(left), axis=0)
    a, b, c = (jnp.dot(stack, part, preferred_element_type=jnp.float32) for part in thirds(right))
    high = a[count : 2 * count] + b[:count]
    low = (a[2 * count :] + b[count : 2 * count]) + c[:count]
    return a[:count] + (high + low)


def stacked(value, order):
    high = value.astype(jnp.bfloat16).astype(jnp.float32)
    both = (high, value - high)
    return jnp.concatenate([both[i] for i in order], axis=0)


def solve(gram, target):
    rows = gram.shape[0]
    eye = lax.broadcasted_iota(jnp.int32, gram.shape, 0) == lax.broadcasted_iota(jnp.int32, gram.shape, 1)
    system = gram + jnp.where(eye, 1.0, 0.0)
    first, scales = newton_plan(rows)
    state, solved, path = first * system, first * target, None
    for index, scale in enumerate(scales):
        factor = jnp.where(eye, 2.0 * scale, 0.0) - scale * state
        factor_halves = halves(factor)
        solved = dot_halves(halves(solved), factor_halves)
        if index < len(scales) - 1:
            state = dot_rows_halved(halves(state), factor_halves)
            if path is None:
                path = factor_halves[0]
            else:
                path = jnp.dot(path, factor_halves[0], preferred_element_type=jnp.float32)
                path = path.astype(jnp.bfloat16)
    rest = (first * (target - dot_thirds(solved, system))).astype(jnp.bfloat16)
    step = jnp.dot(rest, path, preferred_element_type=jnp.float32)
    return solved + dot_halves(halves(step), factor_halves)


def fused_kernel(
    n_dp,
    n_tp,
    act_hbm,
    out_hbm,
    wi_hbm,
    wo_hbm,
    count_ref,
    order_hbm,
    prior_hbm,
    fold_hbm,
    mix_hbm,
    root_out,
    solved_out,
    grads_out,
    tokens,
    weights,
    order_ref,
    prior,
    fold_ref,
    mix_ref,
    pair_in,
    node_send,
    node_recv,
    zsend,
    zmid,
    zrecv,
    full,
    slices_send,
    grads,
    grads_rows,
    grads_all,
    peer_all,
    mix_send,
    mix_recv,
    sums_all,
    root,
    gram_part,
    gram_rs,
    gram_z,
    gram_all,
    load_sem,
    sems,
    root_sems,
    out_sem,
    ready_sem,
):
    f32 = jnp.float32
    me, z = lax.axis_index("dp"), lax.axis_index("tensor")
    rows = prior.shape[0]
    part_rows = gram_z.shape[1]
    levels = n_dp.bit_length() - 1

    def dp_of(k):
        return lax.rem(me + k, n_dp)

    def tp_of(k):
        return lax.rem(z + k, n_tp)

    width = act_hbm.shape[1]
    near = z + 1 - 2 * lax.rem(z, 2)
    far = z + 2 - 4 * (z // 2)
    diagonal = near + 2 - 4 * (near // 2)
    order = (diagonal, far, near, z)
    used = []

    def load(*pairs):
        for source, target in pairs:
            pltpu.make_async_copy(source, target, load_sem.at[len(used)]).start()
        used.append(None)
        return len(used) - 1

    def drain(ref, sem):
        pltpu.make_async_copy(ref, ref, sem).wait()

    def load_chunk(index):
        span = pl.ds(pl.multiple_of(order[index] * SEQ, SEQ), SEQ)
        into = tokens.at[index]
        return load((act_hbm.at[span], into.at[:, :width]), (out_hbm.at[span], into.at[:, width:]))

    order_load = load((order_hbm, order_ref))
    weight_load = load((wi_hbm, weights.at[:, :width]), (wo_hbm, weights.at[:, width:]))
    chunk_loads = [load_chunk(0)]
    prior_load = load((prior_hbm, prior))
    mix_load = load((mix_hbm, mix_ref))
    chunk_loads += [load_chunk(index) for index in range(1, n_tp)]
    fold_load = load((fold_hbm, fold_ref))

    def tile_of(owner):
        return pl.ds(pl.multiple_of(owner * LANES, LANES), LANES)

    barrier = pltpu.get_barrier_semaphore()
    for k in range(1, n_tp):
        pl.semaphore_signal(barrier, inc=1, device_id={"tensor": tp_of(k)}, device_id_type=MESH)
    for k in range(1, n_dp):
        pl.semaphore_signal(barrier, inc=1, device_id={"dp": dp_of(k)}, device_id_type=MESH)
    pl.semaphore_wait(barrier, n_dp + n_tp - 2)
    for k in range(1, n_dp):
        pl.semaphore_signal(ready_sem, inc=1, device_id={"dp": dp_of(k)}, device_id_type=MESH)

    half = n_dp // 2
    core, chip = lax.rem(me, 2), me // 2
    partner = me + 1 - 2 * core
    chip_x = chip + 1 - 2 * lax.rem(chip, 2)
    chip_y = chip + 2 - 4 * (chip // 2)
    chip_d = half - 1 - chip

    PAIR, NODE, MID, SIDE, SLICE, ROW, PEER, SUM, SCATTER, ALONG, GATHER, MIX = range(12)

    def push(phase, source, target, **device):
        pltpu.make_async_remote_copy(
            src_ref=source,
            dst_ref=target,
            send_sem=sems.at[0, phase],
            recv_sem=sems.at[1, phase],
            device_id=device,
            device_id_type=MESH,
        ).start()

    def received(phase, ref):
        drain(ref, sems.at[1, phase])

    for q in range(half):
        push(PAIR, prior_hbm.at[:, tile_of(2 * q + 1 - core)], pair_in.at[q], dp=partner)

    def exchange(axis, phase, source, target):
        size, other = (n_tp, tp_of) if axis == "tensor" else (n_dp, dp_of)
        for k in range(1, size):
            push(phase, source(other(k)), target, **{axis: other(k)})

    def exchange_all(phase, source, target):
        for j in sorted(range(n_tp), key=lambda j: -min(j, n_tp - j)):
            for k in range(n_dp):
                if (j, k) != (0, 0):
                    push(phase, source(dp_of(k), tp_of(j)), target, dp=dp_of(k), tensor=tp_of(j))

    def sides_of_chunk(index):
        drain(tokens.at[index], load_sem.at[chunk_loads[index]])
        mid = SEQ // 2
        spans = [slice(h * mid, (h + 1) * mid) for h in range(2)]
        right = [dot_flip(tokens[index, span, width:], weights[:, width:]) for span in spans]
        left = [dot_flip(tokens[index, span, :width], weights[:, :width]) for span in spans]
        return [jnp.concatenate(pair, axis=1) for pair in zip(left, right)]

    drain(weights, load_sem.at[weight_load])
    zsend[0], zsend[1] = sides_of_chunk(0)
    push(MID, zsend.at[0], zmid, tensor=near)
    push(SIDE, zsend.at[1], zrecv.at[4], tensor=diagonal)
    far_sides = sides_of_chunk(1)
    zsend[3] = far_sides[1]
    push(SIDE, zsend.at[3], zrecv.at[3], tensor=far)

    drain(order_ref, load_sem.at[order_load])
    drain(prior, load_sem.at[prior_load])
    drain(mix_ref, load_sem.at[mix_load])
    received(PAIR, pair_in)
    first_mix, second_mix = mix_ref[:, :rows], mix_ref[:, rows:]
    own_first = order_ref[0, 2 * chip] == core
    own_half = [prior[:, tile_of(2 * q + core)] for q in range(half)]
    firsts = [jnp.where(own_first, own_half[q], pair_in[q]) for q in range(half)]
    seconds = [jnp.where(own_first, pair_in[q], own_half[q]) for q in range(half)]
    first_halves, second_halves = halves(first_mix), halves(second_mix)
    mixed = dot_halves(first_halves, halves(jnp.concatenate(firsts, axis=1)))
    mixed = mixed + dot_halves(second_halves, halves(jnp.concatenate(seconds, axis=1)))
    for q in range(half):
        node_send[q] = mixed[:, q * LANES : (q + 1) * LANES]
    for other in (chip_x, chip_y, chip_d):
        push(NODE, node_send.at[other], node_recv.at[chip], dp=2 * other + core)
    node_recv[chip] = node_send[chip]
    received(MID, zmid)
    zsend[2] = far_sides[0] + zmid[...]
    push(SIDE, zsend.at[2], zrecv.at[2], tensor=far)
    zsend[4], zsend[5] = sides_of_chunk(2)
    push(SIDE, zsend.at[4:6], zrecv.at[0:2], tensor=near)
    own_sides = sides_of_chunk(3)

    drain(fold_ref, load_sem.at[fold_load])
    fold_rows = fold_ref[...]

    def through(value):
        count = value.shape[0]
        both = stacked(value, (0, 1)).astype(jnp.bfloat16)
        high = value.astype(jnp.bfloat16)
        results = []
        for top, bottom in (first_halves, second_halves):
            most = dot_flip(both, top)
            results.append(most[:count] + (most[count:] + dot_flip(high, bottom)))
        return results

    paths = [[jnp.concatenate(through(fold_rows), axis=0)]]
    for level in range(1, levels):
        count = paths[-1][0].shape[0]
        mapped = through(jnp.concatenate(paths[-1], axis=0))
        paths.append([v[i : i + count] for v in mapped for i in range(0, v.shape[0], count)])
    paths = [[stacked(p, (0, 0, 1)).T.astype(jnp.bfloat16) for p in level] for level in paths]
    fold = fold_rows.T

    received(SIDE, zrecv)
    sides = jnp.concatenate(
        [
            (own_sides[0] + zrecv[0]) + zrecv[2],
            (own_sides[1] + zrecv[1]) + (zrecv[3] + zrecv[4]),
        ],
        axis=0,
    )
    lane = lax.broadcasted_iota(jnp.int32, sides.shape, 1)
    doubled = jnp.where(lane < RANK, sides, pltpu.roll(sides, RANK, 1))
    product = dot_mid(sides.T, doubled) / jnp.sqrt(f32(SEQ))
    product = jnp.where(z < count_ref[0], product, jnp.zeros_like(product))
    full[...] = product[RANK:]
    even = full[pl.ds(0, RANK // 2, stride=2), :]
    odd = full[pl.ds(1, RANK // 2, stride=2), :]
    lane = lax.broadcasted_iota(jnp.int32, even.shape, 1)
    mine = jnp.where(lane < RANK, even, odd)
    for row in range(n_tp * n_dp):
        grads_rows[row] = mine[row : row + 1]
    for index in range(n_tp):
        slices_send[index] = mine[index * n_dp : (index + 1) * n_dp]
    grads[z] = slices_send[z]
    slot = me * n_tp + z
    grads_all[slot] = grads_rows[z * n_dp + me]
    pl.semaphore_wait(ready_sem, n_dp - 1)
    exchange("tensor", SLICE, lambda t: slices_send.at[t], grads.at[z])
    exchange_all(ROW, lambda d, t: grads_rows.at[t * n_dp + d], grads_all.at[slot])

    flags = [
        [order_ref[0, j * 2 ** (level + 1) + 2**level - 1] == 1 for j in range(n_dp >> (level + 1))]
        for level in range(levels)
    ]

    def pick(flip, lower, upper):
        first = [jnp.where(flip, b, a) for a, b in zip(lower, upper)]
        return first, [jnp.where(flip, a, b) for a, b in zip(lower, upper)]

    def total(value):
        return jnp.sum(jnp.sum(value, axis=0, keepdims=True), axis=1, keepdims=True)

    received(NODE, node_recv.at[: half - 1])
    mixtures = [[[node_recv[j]] for j in range(half)]]
    for level in range(1, levels):
        below = mixtures[-1]
        sides_of = [pick(flags[level][j], below[2 * j], below[2 * j + 1]) for j in range(len(below) // 2)]
        count = len(below[0])
        left = dot_halves(first_halves, halves(jnp.concatenate([v for f, _ in sides_of for v in f], axis=1)))
        right = dot_halves(second_halves, halves(jnp.concatenate([v for _, g in sides_of for v in g], axis=1)))
        mixtures.append(
            [
                [
                    side[:, (j * count + i) * LANES : (j * count + i + 1) * LANES]
                    for side in (left, right)
                    for i in range(count)
                ]
                for j in range(len(sides_of))
            ]
        )

    for index, part in enumerate(mixtures[-1][0]):
        mix_send[index] = part
    push(MIX, mix_send, mix_recv, dp=partner)

    received(SLICE, grads.at[: n_tp - 1])
    leaf_square = jnp.zeros((rows, LANES), f32)
    for tile in range(n_dp):
        leaf = prior[:, tile * LANES : (tile + 1) * LANES]
        for e in range(n_tp):
            step = grads[e, tile : tile + 1, :]
            grads_out[e : e + 1, tile * LANES : (tile + 1) * LANES] = step
            leaf = leaf + fold[:, e : e + 1] * step
        leaf_square = leaf_square + leaf * leaf
    own_mass = total(leaf_square)

    received(ROW, grads_all.at[: n_tp * n_dp - 1])
    push(PEER, grads_all, peer_all, dp=partner)

    def steps_from(rows_of):
        steps_of = [
            [jnp.concatenate([rows_of[r * n_tp + e] for e in range(n_tp)], axis=0)] for r in range(n_dp)
        ]
        return steps_of, jnp.concatenate([step[0] for step in steps_of], axis=0)

    def merge_steps(level, steps_of):
        merged_steps = []
        for j in range(len(steps_of) // 2):
            first, second = pick(flags[level][j], steps_of[2 * j], steps_of[2 * j + 1])
            if level == 0:
                merged_steps.append([jnp.concatenate([first[0], second[0]], axis=0)])
            else:
                merged_steps.append(first + second)
        return merged_steps

    def updates_of(level, merged_steps):
        return [
            jnp.dot(
                path,
                jnp.concatenate([stacked(g[i], (0, 1, 0)) for g in merged_steps], axis=1).astype(jnp.bfloat16),
                preferred_element_type=f32,
            )
            for i, path in enumerate(paths[level])
        ]

    steps_of, every = steps_from(grads_all)
    sums, products, nodes = [], [], []
    for level in range(levels):
        level_products, level_nodes = [], []
        merged_steps = merge_steps(level, steps_of)
        updates = updates_of(level, merged_steps)
        for j in range(len(merged_steps)):
            parts = [
                v + update[:, j * LANES : (j + 1) * LANES]
                for v, update in zip(mixtures[level][j], updates)
            ]
            index_of = {}
            for a in range(len(parts)):
                for b in range(a + 1):
                    index_of[a, b] = n_dp + len(sums)
                    sums.append(total(parts[a] * parts[b]))
            level_products.append(index_of)
            level_nodes.append(parts)
        steps_of = merged_steps
        products.append(level_products)
        nodes = level_nodes
    lane = lax.broadcasted_iota(jnp.int32, (1, LANES), 1)
    packed = jnp.where(lane == me, own_mass, jnp.zeros((1, LANES), f32))
    for index, value in enumerate(sums):
        packed = jnp.where(lane == n_dp + index, value, packed)
    sums_all[slot] = packed
    exchange_all(SUM, lambda d, t: sums_all.at[slot], sums_all.at[slot])
    received(PEER, peer_all)
    received(MIX, mix_recv)
    steps_of, peer_every = steps_from(peer_all)
    for level in range(levels):
        steps_of = merge_steps(level, steps_of)
    peer_parts = [mix_recv[i] + update for i, update in enumerate(updates_of(levels - 1, steps_of))]
    every_halves = halves(jnp.concatenate([every, peer_every], axis=1))
    received(SUM, sums_all.at[: n_tp * n_dp - 1])
    parts_of = [sums_all[index] for index in range(n_tp * n_dp)]
    while len(parts_of) > 1:
        parts_of = [a + b for a, b in zip(parts_of[0::2], parts_of[1::2])]
    packed = parts_of[0]

    def summed(index):
        return jnp.sum(jnp.where(lane == index, packed, 0.0), axis=1, keepdims=True)

    masses = [summed(index) for index in range(n_dp)]
    scales = [[jnp.ones((1, 1), f32)] for _ in range(n_dp)]
    for level in range(levels):
        new_masses, new_scales = [], []
        for j, products_of in enumerate(products[level]):
            flip = flags[level][j]
            lower, upper = scales[2 * j], scales[2 * j + 1]
            if level == 0:
                coefs = [jnp.ones((1, 1), f32)]
            else:
                coefs = [jnp.where(flip, b, a) for a, b in zip(lower, upper)]
                coefs += [jnp.where(flip, a, b) for a, b in zip(lower, upper)]
            square = jnp.zeros((1, 1), f32)
            for (a, b), index in products_of.items():
                term = coefs[a] * (coefs[b] * summed(index))
                square = square + (term if a == b else 2.0 * term)
            mass = masses[2 * j] + masses[2 * j + 1]
            scale = jnp.sqrt(mass / (jnp.maximum(square, 0.0) + 1e-06))
            trace = scale * scale * square
            new_masses.append(mass)
            new_scales.append([scale * c for c in coefs])
        masses, scales = new_masses, new_scales
    chunks = []
    for parts in (nodes[0], peer_parts):
        chunk = scales[0][0] * parts[0]
        for c, part in zip(scales[0][1:], parts[1:]):
            chunk = chunk + c * part
        chunks.append(chunk)
    root[:, tile_of(me)] = chunks[0]
    root[:, tile_of(partner)] = chunks[1]

    chunk_halves = halves(jnp.concatenate(chunks, axis=1))
    upper_halves, lower_halves = [[v[s] for v in chunk_halves] for s in (slice(0, LANES), slice(LANES, rows))]
    targets = dot_flip_halves(every_halves, chunk_halves)
    unit = rows / trace
    triangle = jnp.concatenate(
        [
            dot_flip_halves(upper_halves, upper_halves),
            dot_flip_halves(lower_halves, upper_halves),
            dot_flip_halves(lower_halves, lower_halves),
            targets[:, :LANES],
            targets[:, LANES:],
        ],
        axis=0,
    )
    for r in range(n_dp):
        gram_part[r] = unit * triangle[r * part_rows : (r + 1) * part_rows]
    gram_rs[chip] = gram_part[me]
    for other in (chip_d, chip_x, chip_y):
        push(SCATTER, gram_part.at[2 * other + core], gram_rs.at[chip], dp=2 * other + core)
    dev_x, dev_y, dev_d = (2 * other + core for other in (chip_x, chip_y, chip_d))
    upper, lower = pl.ds(0, rows // 2), pl.ds(rows // 2, rows // 2)

    def relay(index, owner, device, span=slice(None)):
        block_of = root.at[span, tile_of(owner)]
        pltpu.make_async_remote_copy(
            src_ref=block_of,
            dst_ref=block_of,
            send_sem=root_sems.at[5],
            recv_sem=root_sems.at[index],
            device_id={"dp": device},
            device_id_type=MESH,
        ).start()

    def relayed(index, count):
        drain(root.at[:, : count * LANES] if count else root.at[upper, :LANES], root_sems.at[index])

    relay(0, me, dev_x)
    relay(1, me, dev_y)
    received(SCATTER, gram_rs.at[: half - 1])
    part = gram_rs[0]
    for index in range(1, half):
        part = part + gram_rs[index]
    gram_z[z] = part
    exchange("tensor", ALONG, lambda t: gram_z.at[z], gram_z.at[z])
    relayed(0, 1)
    relay(2, dev_x, dev_y, upper)
    relay(4, dev_x, partner)
    relayed(1, 1)
    relay(3, dev_y, dev_x, lower)
    relay(4, dev_y, partner)
    received(ALONG, gram_z.at[: n_tp - 1])
    part = gram_z[0]
    for index in range(1, n_tp):
        part = part + gram_z[index]
    gram_all[me] = part
    exchange("dp", GATHER, lambda t: gram_all.at[me], gram_all.at[me])
    relayed(2, 0)
    relayed(3, 0)
    relay(4, dev_d, partner)
    for phase, ref in (
        (PAIR, pair_in),
        (NODE, node_recv.at[: half - 1]),
        (MID, zmid),
        (SIDE, zrecv),
        (SLICE, grads.at[: n_tp - 1]),
        (ROW, grads_all.at[: n_tp * n_dp - 1]),
        (SUM, sums_all.at[: n_tp * n_dp - 1]),
        (PEER, peer_all),
        (MIX, mix_recv),
        (SCATTER, gram_rs.at[: half - 1]),
        (ALONG, gram_z.at[: n_tp - 1]),
    ):
        drain(ref, sems.at[0, phase])
    received(GATHER, gram_all.at[: n_dp - 1])
    triangle = jnp.concatenate([gram_all[r] for r in range(n_dp)], axis=0)
    corner = triangle[LANES:rows]
    gram = jnp.concatenate(
        [
            jnp.concatenate([triangle[:LANES], corner.T], axis=1),
            jnp.concatenate([corner, triangle[rows : rows + LANES]], axis=1),
        ],
        axis=0,
    )
    targets = triangle[rows + LANES :]
    target = jnp.zeros((n_tp, rows), f32)
    for r in range(n_dp):
        span = slice(r * n_tp, (r + 1) * n_tp)
        both = [targets[: n_dp * n_tp][span], targets[n_dp * n_tp :][span]]
        target = jnp.where(me == r, jnp.concatenate(both, axis=1), target)
    solved_out[...] = solve(gram, target)
    drain(gram_all.at[: n_dp - 1], sems.at[0, GATHER])
    relayed(4, half - 1)
    root_write = pltpu.make_async_copy(root, root_out, out_sem.at[0])
    root_write.start()
    drain(root.at[:, : (n_dp - 2) * LANES], root_sems.at[5])
    root_write.wait()


def last_kernel(root_ref, solved_ref, grads_ref, root_out, pre_out, pre, sem):
    write = pltpu.make_async_copy(root_ref, root_out, sem.at[0])
    write.start()
    pre[...] = grads_ref[...] - dot_mid(solved_ref[...], root_ref[...])
    pre_write = pltpu.make_async_copy(pre, pre_out, sem.at[1])
    pre_write.start()
    write.wait()
    pre_write.wait()


def fused_body(
    activations,
    out_grads,
    input_proj,
    grad_proj,
    example_count,
    child_order,
    prior_sketch,
    fold_map,
    merge_mix,
):
    n_dp, n_tp = lax.axis_size("dp"), lax.axis_size("tensor")
    rows, columns = prior_sketch.shape
    slots = activations.shape[0] // SEQ
    f32, bf16 = jnp.float32, jnp.bfloat16
    width, hidden = activations.shape[1], out_grads.shape[1]
    hbm = pl.BlockSpec(memory_space=pltpu.HBM)
    anywhere = pl.BlockSpec(memory_space=pl.ANY)
    vmem = pl.BlockSpec(memory_space=pltpu.VMEM)
    smem = pl.BlockSpec(memory_space=pltpu.SMEM)
    devices = n_dp * n_tp
    part_rows = (3 * LANES + 2 * n_dp * slots) // n_dp
    pin = functools.partial(pltpu.with_memory_space_constraint, memory_space=pltpu.HBM)
    root, solved, grads = pl.pallas_call(
        functools.partial(fused_kernel, n_dp, n_tp),
        out_shape=(
            jax.ShapeDtypeStruct((rows, columns), f32),
            jax.ShapeDtypeStruct((slots, rows), f32),
            jax.ShapeDtypeStruct((slots, columns), f32),
        ),
        in_specs=[hbm, hbm, hbm, hbm, smem, hbm, hbm, hbm, hbm],
        out_specs=(anywhere, vmem, vmem),
        scratch_shapes=[
            pltpu.VMEM((slots, SEQ, width + hidden), bf16),
            pltpu.VMEM((RANK, width + hidden), bf16),
            pltpu.SMEM((1, n_dp), jnp.int32),
            pltpu.VMEM((rows, columns), f32),
            pltpu.VMEM((slots, rows), f32),
            pltpu.VMEM((rows, 2 * rows), f32),
            pltpu.VMEM((n_dp // 2, rows, LANES), f32),
            pltpu.VMEM((n_dp // 2, rows, LANES), f32),
            pltpu.VMEM((n_dp // 2, rows, LANES), f32),
            pltpu.VMEM((6, SEQ // 2, LANES), f32),
            pltpu.VMEM((SEQ // 2, LANES), f32),
            pltpu.VMEM((5, SEQ // 2, LANES), f32),
            pltpu.VMEM((RANK, LANES), f32),
            pltpu.VMEM((n_tp, n_dp, LANES), f32),
            pltpu.VMEM((n_tp, n_dp, LANES), f32),
            pltpu.VMEM((devices, 1, LANES), f32),
            pltpu.VMEM((devices, 1, LANES), f32),
            pltpu.VMEM((devices, 1, LANES), f32),
            pltpu.VMEM((n_dp // 2, rows, LANES), f32),
            pltpu.VMEM((n_dp // 2, rows, LANES), f32),
            pltpu.VMEM((devices, 1, LANES), f32),
            pltpu.VMEM((rows, columns), f32),
            pltpu.VMEM((n_dp, part_rows, LANES), f32),
            pltpu.VMEM((n_dp // 2, part_rows, LANES), f32),
            pltpu.VMEM((n_tp, part_rows, LANES), f32),
            pltpu.VMEM((n_dp, part_rows, LANES), f32),
            pltpu.SemaphoreType.DMA((9,)),
            pltpu.SemaphoreType.DMA((2, 12)),
            pltpu.SemaphoreType.DMA((6,)),
            pltpu.SemaphoreType.DMA((1,)),
            pltpu.SemaphoreType.REGULAR,
        ],
        compiler_params=pltpu.CompilerParams(
            collective_id=0, has_side_effects=True, vmem_limit_bytes=32 * 2**20
        ),
    )(
        pin(activations),
        pin(out_grads),
        pin(input_proj.T),
        pin(grad_proj.T),
        example_count,
        pin(child_order.reshape(1, n_dp)),
        pin(prior_sketch),
        pin(fold_map.T),
        pin(merge_mix),
    )
    return pl.pallas_call(
        last_kernel,
        out_shape=(
            jax.ShapeDtypeStruct((rows, columns), f32),
            jax.ShapeDtypeStruct((slots, columns), f32),
        ),
        in_specs=[vmem] * 3,
        out_specs=(anywhere, anywhere),
        scratch_shapes=[pltpu.VMEM((slots, columns), f32), pltpu.SemaphoreType.DMA((2,))],
        compiler_params=pltpu.CompilerParams(vmem_limit_bytes=16 * 2**20),
    )(root, solved, grads)


def from_partner(value, axis, stride):
    mask = 2**stride
    pairs = [(source, source ^ mask) for source in range(lax.axis_size(axis))]
    return lax.ppermute(value, axis, pairs)


def body(
    activations,
    out_grads,
    input_proj,
    grad_proj,
    example_count,
    child_order,
    prior_sketch,
    fold_map,
    merge_mix,
):
    tensor_count = lax.axis_size("tensor")
    own_rank = RANK // tensor_count
    example_slots = activations.shape[0] // SEQ
    sketch_rows = prior_sketch.shape[0]
    input_part = jnp.dot(activations, input_proj, preferred_element_type=jnp.float32)
    grad_part = jnp.dot(out_grads, grad_proj, preferred_element_type=jnp.float32)
    input_side, grad_side = lax.psum((input_part, grad_part), "tensor")
    grad_own = lax.dynamic_slice_in_dim(grad_side, lax.axis_index("tensor") * own_rank, own_rank, 1)
    grad_blocks = grad_own.reshape(example_slots, SEQ, own_rank)
    input_blocks = input_side.reshape(example_slots, SEQ, RANK)
    example_grad = jnp.einsum(
        "eta,etb->eab", grad_blocks, input_blocks, precision=lax.Precision.HIGHEST
    )
    example_grad = example_grad.reshape(example_slots, own_rank * RANK) / jnp.sqrt(jnp.float32(SEQ))
    live = jnp.arange(example_slots, dtype=jnp.int32) < example_count[0]
    example_grad = jnp.where(live[:, None], example_grad, jnp.zeros_like(example_grad))
    leaf_node = prior_sketch + jnp.dot(fold_map, example_grad, precision=lax.Precision.HIGHEST)
    leaf_weight = lax.psum(jnp.sum(leaf_node * leaf_node), "tensor")
    mix_first = merge_mix[:, :sketch_rows]
    mix_second = merge_mix[:, sketch_rows:]
    depth_count = lax.axis_size("dp").bit_length() - 1
    rank_index = lax.axis_index("dp")
    sketch_node = leaf_node
    sketch_weight = leaf_weight
    for level_index in range(depth_count):
        sibling_node, sibling_weight = from_partner((sketch_node, sketch_weight), "dp", level_index)
        upper_half = rank_index >> level_index & 1
        block_start = rank_index >> level_index + 1 << level_index + 1
        flip_order = child_order[block_start + (1 << level_index) - 1]
        own_first = upper_half == flip_order
        first = jnp.where(own_first, sketch_node, sibling_node)
        second = jnp.where(own_first, sibling_node, sketch_node)
        first_weight = jnp.where(own_first, sketch_weight, sibling_weight)
        second_weight = jnp.where(own_first, sibling_weight, sketch_weight)
        mixture = jnp.dot(mix_first, first, precision=lax.Precision.HIGHEST) + jnp.dot(
            mix_second, second, precision=lax.Precision.HIGHEST
        )
        mix_total = lax.psum(jnp.sum(mixture * mixture), "tensor")
        sketch_weight = first_weight + second_weight
        sketch_node = mixture * jnp.sqrt(sketch_weight / (mix_total + 1e-06))
    gram_part = jnp.dot(sketch_node, sketch_node.T, precision=lax.Precision.HIGHEST)
    product_part = jnp.dot(sketch_node, example_grad.T, precision=lax.Precision.HIGHEST)
    gram, sketch_grad = lax.psum((gram_part, product_part), "tensor")
    damping = jnp.trace(gram) / sketch_rows
    system = gram + damping * jnp.eye(sketch_rows, dtype=jnp.float32)
    factor = jnp.linalg.cholesky(system)
    solved = jax.scipy.linalg.cho_solve((factor, True), sketch_grad)
    preconditioned = example_grad - jnp.dot(solved.T, sketch_node, precision=lax.Precision.HIGHEST)
    return (sketch_node, preconditioned)


def fits_fused(rows, columns, slots, n_dp, n_tp):
    return (
        columns == n_dp * LANES
        and slots == n_tp
        and 2 * RANK == LANES
        and n_dp == 8
        and n_tp == 4
        and rows == 2 * LANES
        and (3 * LANES + 2 * n_dp * slots) % (8 * n_dp) == 0
    )


def step(*args):
    n_dp, n_tp = lax.axis_size("dp"), lax.axis_size("tensor")
    slots = args[0].shape[0] // SEQ
    rows, columns = args[6].shape
    if fits_fused(rows, columns, slots, n_dp, n_tp):
        return fused_body(*args)
    return body(*args)


def solution(mesh):
    in_specs = (
        P("dp", "tensor"),
        P("dp", "tensor"),
        P("tensor", None),
        P("tensor", None),
        P("dp"),
        P(),
        P("dp", "tensor"),
        P(),
        P(),
    )
    out_specs = (P(None, "tensor"), P("dp", "tensor"))
    return jax.shard_map(step, mesh=mesh, in_specs=in_specs, out_specs=out_specs, check_vma=False)
```

```python
import functools

import jax
import jax.numpy as jnp
from jax import lax
from jax.experimental import pallas as pl
from jax.experimental.pallas import tpu as pltpu
from jax.sharding import PartitionSpec as P

RANK = 64
SEQ = 128
LANES = 128
HIGHEST = lax.Precision.HIGHEST
MESH = pl.DeviceIdType.MESH


def newton_plan(rows):
    low, high = 0.999, (rows + 1) * 1.001
    first = 2.0 / (low + high)
    reach, scales = first * low, []
    while 1.0 - reach > 1e-3:
        grown = reach * (2.0 - reach)
        scale = 2.0 / (1.0 + grown)
        scales.append(scale)
        reach = grown * scale
    return first, scales


def dot_high(left, right):
    return jnp.dot(left, right, precision=HIGHEST, preferred_element_type=jnp.float32)


def dot_flip(left, right):
    return lax.dot_general(left, right, (((1,), (1,)), ((), ())), preferred_element_type=jnp.float32)


def halves(value):
    high = value.astype(jnp.bfloat16)
    return high, (value - high.astype(jnp.float32)).astype(jnp.bfloat16)


def dot_halves(left, right):
    (a, b), (c, d) = left, right
    out = jnp.dot(a, c, preferred_element_type=jnp.float32)
    out = out + jnp.dot(a, d, preferred_element_type=jnp.float32)
    return out + jnp.dot(b, c, preferred_element_type=jnp.float32)


def dot_mid(left, right):
    return dot_halves(halves(left), halves(right))


def dot_flip_halves(left, right):
    (a, b), (c, d) = left, right
    return dot_flip(jnp.concatenate([a, a, b], axis=1), jnp.concatenate([c, d, c], axis=1))


def dot_rows_halved(left, right):
    (a, b), (c, d) = left, right
    left = jnp.concatenate([a, a, b], axis=1)
    right = jnp.concatenate([c, d, c], axis=0)
    half = left.shape[0] // 2
    return jnp.concatenate(
        [
            jnp.dot(left[:half], right, preferred_element_type=jnp.float32),
            jnp.dot(left[half:], right, preferred_element_type=jnp.float32),
        ],
        axis=0,
    )


def thirds(value):
    high = value.astype(jnp.bfloat16)
    return (high, *halves(value - high.astype(jnp.float32)))


def dot_thirds(left, right):
    count = left.shape[0]
    stack = jnp.concatenate(thirds(left), axis=0)
    a, b, c = (jnp.dot(stack, part, preferred_element_type=jnp.float32) for part in thirds(right))
    high = a[count : 2 * count] + b[:count]
    low = (a[2 * count :] + b[count : 2 * count]) + c[:count]
    return a[:count] + (high + low)


def stacked(value, order):
    high = value.astype(jnp.bfloat16).astype(jnp.float32)
    both = (high, value - high)
    return jnp.concatenate([both[i] for i in order], axis=0)


def solve(gram, target):
    rows = gram.shape[0]
    eye = lax.broadcasted_iota(jnp.int32, gram.shape, 0) == lax.broadcasted_iota(jnp.int32, gram.shape, 1)
    system = gram + jnp.where(eye, 1.0, 0.0)
    first, scales = newton_plan(rows)
    state, solved, path = first * system, first * target, None
    for index, scale in enumerate(scales):
        factor = jnp.where(eye, 2.0 * scale, 0.0) - scale * state
        factor_halves = halves(factor)
        solved = dot_halves(halves(solved), factor_halves)
        if index < len(scales) - 1:
            state = dot_rows_halved(halves(state), factor_halves)
            if path is None:
                path = factor_halves[0]
            else:
                path = jnp.dot(path, factor_halves[0], preferred_element_type=jnp.float32)
                path = path.astype(jnp.bfloat16)
    rest = (first * (target - dot_thirds(solved, system))).astype(jnp.bfloat16)
    step = jnp.dot(rest, path, preferred_element_type=jnp.float32)
    return solved + dot_halves(halves(step), factor_halves)


def fused_kernel(
    n_dp,
    n_tp,
    act_hbm,
    out_hbm,
    wi_hbm,
    wo_hbm,
    count_ref,
    order_hbm,
    prior_hbm,
    fold_hbm,
    mix_hbm,
    root_out,
    solved_out,
    grads_out,
    tokens,
    weights,
    order_ref,
    prior,
    fold_ref,
    mix_ref,
    pair_in,
    node_send,
    node_recv,
    zsend,
    zmid,
    zrecv,
    full,
    slices_send,
    grads,
    grads_rows,
    grads_all,
    peer_all,
    mix_send,
    mix_recv,
    sums_all,
    root,
    gram_part,
    gram_rs,
    gram_z,
    gram_all,
    load_sem,
    sems,
    root_sems,
    out_sem,
    ready_sem,
):
    f32 = jnp.float32
    me, z = lax.axis_index("dp"), lax.axis_index("tensor")
    rows = prior.shape[0]
    levels = n_dp.bit_length() - 1

    def dp_of(k):
        return lax.rem(me + k, n_dp)

    def tp_of(k):
        return lax.rem(z + k, n_tp)

    width = act_hbm.shape[1]
    near = z + 1 - 2 * lax.rem(z, 2)
    far = z + 2 - 4 * (z // 2)
    diagonal = near + 2 - 4 * (near // 2)
    order = (diagonal, far, near, z)
    used = []

    def load(*pairs):
        for source, target in pairs:
            pltpu.make_async_copy(source, target, load_sem.at[len(used)]).start()
        used.append(None)
        return len(used) - 1

    def drain(ref, sem):
        pltpu.make_async_copy(ref, ref, sem).wait()

    def load_chunk(index):
        span = pl.ds(pl.multiple_of(order[index] * SEQ, SEQ), SEQ)
        into = tokens.at[index]
        return load((act_hbm.at[span], into.at[:, :width]), (out_hbm.at[span], into.at[:, width:]))

    order_load = load((order_hbm, order_ref))
    weight_load = load((wi_hbm, weights.at[:, :width]), (wo_hbm, weights.at[:, width:]))
    chunk_loads = [load_chunk(0)]
    prior_load = load((prior_hbm, prior))
    mix_load = load((mix_hbm, mix_ref))
    chunk_loads += [load_chunk(index) for index in range(1, n_tp)]
    fold_load = load((fold_hbm, fold_ref))

    def tile_of(owner):
        return pl.ds(pl.multiple_of(owner * LANES, LANES), LANES)

    barrier = pltpu.get_barrier_semaphore()
    for k in range(1, n_tp):
        pl.semaphore_signal(barrier, inc=1, device_id={"tensor": tp_of(k)}, device_id_type=MESH)
    for k in range(1, n_dp):
        pl.semaphore_signal(barrier, inc=1, device_id={"dp": dp_of(k)}, device_id_type=MESH)

    half = n_dp // 2
    core, chip = lax.rem(me, 2), me // 2
    partner = me + 1 - 2 * core
    chip_x = chip + 1 - 2 * lax.rem(chip, 2)
    chip_y = chip + 2 - 4 * (chip // 2)
    chip_d = half - 1 - chip

    PAIR, NODE, MID, SIDE, SLICE, ROW, PEER, SUM, SCATTER, ALONG, GATHER, MIX = range(12)

    def push(phase, source, target, **device):
        pltpu.make_async_remote_copy(
            src_ref=source,
            dst_ref=target,
            send_sem=sems.at[0, phase],
            recv_sem=sems.at[1, phase],
            device_id=device,
            device_id_type=MESH,
        ).start()

    def received(phase, ref):
        drain(ref, sems.at[1, phase])

    def exchange(axis, phase, source, target):
        size, other = (n_tp, tp_of) if axis == "tensor" else (n_dp, dp_of)
        for k in range(1, size):
            push(phase, source(other(k)), target, **{axis: other(k)})

    def exchange_all(phase, source, target):
        for j in sorted(range(n_tp), key=lambda j: -min(j, n_tp - j)):
            for k in range(n_dp):
                if (j, k) != (0, 0):
                    push(phase, source(dp_of(k), tp_of(j)), target, dp=dp_of(k), tensor=tp_of(j))

    def sides_of_chunk(index):
        drain(tokens.at[index], load_sem.at[chunk_loads[index]])
        mid = SEQ // 2
        spans = [slice(h * mid, (h + 1) * mid) for h in range(2)]
        right = [dot_flip(tokens[index, span, width:], weights[:, width:]) for span in spans]
        left = [dot_flip(tokens[index, span, :width], weights[:, :width]) for span in spans]
        return [jnp.concatenate(pair, axis=1) for pair in zip(left, right)]

    drain(weights, load_sem.at[weight_load])
    zsend[0], zsend[1] = sides_of_chunk(0)
    pl.semaphore_wait(barrier, n_dp + n_tp - 2)
    push(MID, zsend.at[0], zmid, tensor=near)
    push(SIDE, zsend.at[1], zrecv.at[4], tensor=diagonal)
    for q in range(half):
        push(PAIR, prior_hbm.at[:, tile_of(2 * q + 1 - core)], pair_in.at[q], dp=partner)
    for k in range(1, n_dp):
        pl.semaphore_signal(ready_sem, inc=1, device_id={"dp": dp_of(k)}, device_id_type=MESH)
    far_sides = sides_of_chunk(1)
    zsend[3] = far_sides[1]
    push(SIDE, zsend.at[3], zrecv.at[3], tensor=far)
    zsend[4], zsend[5] = sides_of_chunk(2)
    push(SIDE, zsend.at[4:6], zrecv.at[0:2], tensor=near)

    drain(order_ref, load_sem.at[order_load])
    drain(prior, load_sem.at[prior_load])
    drain(mix_ref, load_sem.at[mix_load])
    received(PAIR, pair_in)
    first_mix, second_mix = mix_ref[:, :rows], mix_ref[:, rows:]
    own_first = order_ref[0, 2 * chip] == core
    own_half = [prior[:, tile_of(2 * q + core)] for q in range(half)]
    firsts = [jnp.where(own_first, own_half[q], pair_in[q]) for q in range(half)]
    seconds = [jnp.where(own_first, pair_in[q], own_half[q]) for q in range(half)]
    first_halves, second_halves = halves(first_mix), halves(second_mix)
    mixed = dot_halves(first_halves, halves(jnp.concatenate(firsts, axis=1)))
    mixed = mixed + dot_halves(second_halves, halves(jnp.concatenate(seconds, axis=1)))
    for q in range(half):
        node_send[q] = mixed[:, q * LANES : (q + 1) * LANES]
    for other in (chip_x, chip_y, chip_d):
        push(NODE, node_send.at[other], node_recv.at[chip], dp=2 * other + core)
    node_recv[chip] = node_send[chip]
    received(MID, zmid)
    zsend[2] = far_sides[0] + zmid[...]
    push(SIDE, zsend.at[2], zrecv.at[2], tensor=far)
    own_sides = sides_of_chunk(3)

    drain(fold_ref, load_sem.at[fold_load])
    fold_rows = fold_ref[...]

    def through(value):
        count = value.shape[0]
        both = stacked(value, (0, 1)).astype(jnp.bfloat16)
        high = value.astype(jnp.bfloat16)
        results = []
        for top, bottom in (first_halves, second_halves):
            most = dot_flip(both, top)
            results.append(most[:count] + (most[count:] + dot_flip(high, bottom)))
        return results

    paths = [[jnp.concatenate(through(fold_rows), axis=0)]]
    for level in range(1, levels):
        count = paths[-1][0].shape[0]
        mapped = through(jnp.concatenate(paths[-1], axis=0))
        paths.append([v[i : i + count] for v in mapped for i in range(0, v.shape[0], count)])
    paths = [[stacked(p, (0, 0, 1)).T.astype(jnp.bfloat16) for p in level] for level in paths]
    fold = fold_rows.T

    received(SIDE, zrecv)
    sides = jnp.concatenate(
        [
            (own_sides[0] + zrecv[0]) + zrecv[2],
            (own_sides[1] + zrecv[1]) + (zrecv[3] + zrecv[4]),
        ],
        axis=0,
    )
    lane = lax.broadcasted_iota(jnp.int32, sides.shape, 1)
    doubled = jnp.where(lane < RANK, sides, pltpu.roll(sides, RANK, 1))
    product = dot_mid(sides.T, doubled) / jnp.sqrt(f32(SEQ))
    product = jnp.where(z < count_ref[0], product, jnp.zeros_like(product))
    full[...] = product[RANK:]
    even = full[pl.ds(0, RANK // 2, stride=2), :]
    odd = full[pl.ds(1, RANK // 2, stride=2), :]
    lane = lax.broadcasted_iota(jnp.int32, even.shape, 1)
    mine = jnp.where(lane < RANK, even, odd)
    for row in range(n_tp * n_dp):
        grads_rows[row] = mine[row : row + 1]
    for index in range(n_tp):
        slices_send[index] = mine[index * n_dp : (index + 1) * n_dp]
    grads[z] = slices_send[z]
    slot = me * n_tp + z
    grads_all[slot] = grads_rows[z * n_dp + me]
    pl.semaphore_wait(ready_sem, n_dp - 1)
    exchange("tensor", SLICE, lambda t: slices_send.at[t], grads.at[z])
    exchange_all(ROW, lambda d, t: grads_rows.at[t * n_dp + d], grads_all.at[slot])

    flags = [
        [order_ref[0, j * 2 ** (level + 1) + 2**level - 1] == 1 for j in range(n_dp >> (level + 1))]
        for level in range(levels)
    ]

    def pick(flip, lower, upper):
        first = [jnp.where(flip, b, a) for a, b in zip(lower, upper)]
        return first, [jnp.where(flip, a, b) for a, b in zip(lower, upper)]

    def total(value):
        return jnp.sum(jnp.sum(value, axis=0, keepdims=True), axis=1, keepdims=True)

    received(SLICE, grads.at[: n_tp - 1])
    leaf_square = jnp.zeros((rows, LANES), f32)
    for tile in range(n_dp):
        leaf = prior[:, tile * LANES : (tile + 1) * LANES]
        for e in range(n_tp):
            step = grads[e, tile : tile + 1, :]
            grads_out[e : e + 1, tile * LANES : (tile + 1) * LANES] = step
            leaf = leaf + fold[:, e : e + 1] * step
        leaf_square = leaf_square + leaf * leaf
    own_mass = total(leaf_square)

    received(NODE, node_recv.at[: half - 1])
    mixtures = [[[node_recv[j]] for j in range(half)]]
    for level in range(1, levels):
        below = mixtures[-1]
        sides_of = [pick(flags[level][j], below[2 * j], below[2 * j + 1]) for j in range(len(below) // 2)]
        count = len(below[0])
        left = dot_halves(first_halves, halves(jnp.concatenate([v for f, _ in sides_of for v in f], axis=1)))
        right = dot_halves(second_halves, halves(jnp.concatenate([v for _, g in sides_of for v in g], axis=1)))
        mixtures.append(
            [
                [
                    side[:, (j * count + i) * LANES : (j * count + i + 1) * LANES]
                    for side in (left, right)
                    for i in range(count)
                ]
                for j in range(len(sides_of))
            ]
        )

    for index, part in enumerate(mixtures[-1][0]):
        mix_send[index] = part
    push(MIX, mix_send, mix_recv, dp=partner)

    received(ROW, grads_all.at[: n_tp * n_dp - 1])
    push(PEER, grads_all, peer_all, dp=partner)

    def steps_from(rows_of):
        steps_of = [
            [jnp.concatenate([rows_of[r * n_tp + e] for e in range(n_tp)], axis=0)] for r in range(n_dp)
        ]
        return steps_of, jnp.concatenate([step[0] for step in steps_of], axis=0)

    def merge_steps(level, steps_of):
        merged_steps = []
        for j in range(len(steps_of) // 2):
            first, second = pick(flags[level][j], steps_of[2 * j], steps_of[2 * j + 1])
            if level == 0:
                merged_steps.append([jnp.concatenate([first[0], second[0]], axis=0)])
            else:
                merged_steps.append(first + second)
        return merged_steps

    def updates_of(level, merged_steps):
        return [
            jnp.dot(
                path,
                jnp.concatenate([stacked(g[i], (0, 1, 0)) for g in merged_steps], axis=1).astype(jnp.bfloat16),
                preferred_element_type=f32,
            )
            for i, path in enumerate(paths[level])
        ]

    steps_of, every = steps_from(grads_all)
    sums, products, nodes = [], [], []
    for level in range(levels):
        level_products, level_nodes = [], []
        merged_steps = merge_steps(level, steps_of)
        updates = updates_of(level, merged_steps)
        for j in range(len(merged_steps)):
            parts = [
                v + update[:, j * LANES : (j + 1) * LANES]
                for v, update in zip(mixtures[level][j], updates)
            ]
            index_of = {}
            for a in range(len(parts)):
                for b in range(a + 1):
                    index_of[a, b] = n_dp + len(sums)
                    sums.append(total(parts[a] * parts[b]))
            level_products.append(index_of)
            level_nodes.append(parts)
        steps_of = merged_steps
        products.append(level_products)
        nodes = level_nodes
    lane = lax.broadcasted_iota(jnp.int32, (1, LANES), 1)
    packed = jnp.where(lane == me, own_mass, jnp.zeros((1, LANES), f32))
    for index, value in enumerate(sums):
        packed = jnp.where(lane == n_dp + index, value, packed)
    sums_all[slot] = packed
    exchange_all(SUM, lambda d, t: sums_all.at[slot], sums_all.at[slot])
    received(PEER, peer_all)
    received(MIX, mix_recv)
    steps_of, peer_every = steps_from(peer_all)
    for level in range(levels):
        steps_of = merge_steps(level, steps_of)
    peer_parts = [mix_recv[i] + update for i, update in enumerate(updates_of(levels - 1, steps_of))]
    every_halves = halves(jnp.concatenate([every, peer_every], axis=1))
    received(SUM, sums_all.at[: n_tp * n_dp - 1])
    parts_of = [sums_all[index] for index in range(n_tp * n_dp)]
    while len(parts_of) > 1:
        parts_of = [a + b for a, b in zip(parts_of[0::2], parts_of[1::2])]
    packed = parts_of[0]

    def summed(index):
        return jnp.sum(jnp.where(lane == index, packed, 0.0), axis=1, keepdims=True)

    masses = [summed(index) for index in range(n_dp)]
    scales = [[jnp.ones((1, 1), f32)] for _ in range(n_dp)]
    for level in range(levels):
        new_masses, new_scales = [], []
        for j, products_of in enumerate(products[level]):
            flip = flags[level][j]
            lower, upper = scales[2 * j], scales[2 * j + 1]
            if level == 0:
                coefs = [jnp.ones((1, 1), f32)]
            else:
                coefs = [jnp.where(flip, b, a) for a, b in zip(lower, upper)]
                coefs += [jnp.where(flip, a, b) for a, b in zip(lower, upper)]
            square = jnp.zeros((1, 1), f32)
            for (a, b), index in products_of.items():
                term = coefs[a] * (coefs[b] * summed(index))
                square = square + (term if a == b else 2.0 * term)
            mass = masses[2 * j] + masses[2 * j + 1]
            scale = jnp.sqrt(mass / (jnp.maximum(square, 0.0) + 1e-06))
            trace = scale * scale * square
            new_masses.append(mass)
            new_scales.append([scale * c for c in coefs])
        masses, scales = new_masses, new_scales
    chunks = []
    for parts in (nodes[0], peer_parts):
        chunk = scales[0][0] * parts[0]
        for c, part in zip(scales[0][1:], parts[1:]):
            chunk = chunk + c * part
        chunks.append(chunk)
    root[:, tile_of(me)] = chunks[0]
    root[:, tile_of(partner)] = chunks[1]

    chunk_halves = halves(jnp.concatenate(chunks, axis=1))
    upper_halves, lower_halves = [[v[s] for v in chunk_halves] for s in (slice(0, LANES), slice(LANES, rows))]
    targets = dot_flip_halves(every_halves, chunk_halves)
    unit = rows / trace
    triangle = jnp.concatenate(
        [
            dot_flip_halves(upper_halves, upper_halves),
            dot_flip_halves(lower_halves, upper_halves),
            dot_flip_halves(lower_halves, lower_halves),
        ],
        axis=0,
    )
    own_rows = gram_all.shape[1]
    for r in range(n_dp):
        gram_part[r, :own_rows] = unit * triangle[r * own_rows : (r + 1) * own_rows]
        own = targets[r * n_tp : (r + 1) * n_tp]
        gram_part[r, own_rows:] = unit * jnp.concatenate([own[:, :LANES], own[:, LANES:]], axis=0)
    gram_rs[chip] = gram_part[me]
    for other in (chip_d, chip_x, chip_y):
        push(SCATTER, gram_part.at[2 * other + core], gram_rs.at[chip], dp=2 * other + core)
    dev_x, dev_y, dev_d = (2 * other + core for other in (chip_x, chip_y, chip_d))
    upper, lower = pl.ds(0, rows // 2), pl.ds(rows // 2, rows // 2)

    def relay(index, owner, device, span=slice(None)):
        block_of = root.at[span, tile_of(owner)]
        pltpu.make_async_remote_copy(
            src_ref=block_of,
            dst_ref=block_of,
            send_sem=root_sems.at[5],
            recv_sem=root_sems.at[index],
            device_id={"dp": device},
            device_id_type=MESH,
        ).start()

    def relayed(index, count):
        drain(root.at[:, : count * LANES] if count else root.at[upper, :LANES], root_sems.at[index])

    drain(gram_rs.at[: half - 1], sems.at[0, SCATTER])
    relay(0, me, dev_x)
    relay(1, me, dev_y)
    received(SCATTER, gram_rs.at[: half - 1])
    part = gram_rs[0]
    for index in range(1, half):
        part = part + gram_rs[index]
    gram_z[z] = part
    exchange("tensor", ALONG, lambda t: gram_z.at[z], gram_z.at[z])
    relayed(0, 1)
    relay(2, dev_x, dev_y, upper)
    relay(4, dev_x, partner)
    relayed(1, 1)
    relay(3, dev_y, dev_x, lower)
    relay(4, dev_y, partner)
    received(ALONG, gram_z.at[: n_tp - 1])
    part = gram_z[0]
    for index in range(1, n_tp):
        part = part + gram_z[index]
    gram_all[me] = part[:own_rows]
    target = jnp.concatenate([part[own_rows : own_rows + n_tp], part[own_rows + n_tp :]], axis=1)
    exchange("dp", GATHER, lambda t: gram_all.at[me], gram_all.at[me])
    relayed(2, 0)
    relayed(3, 0)
    relay(4, dev_d, partner)
    for phase, ref in (
        (PAIR, pair_in),
        (NODE, node_recv.at[: half - 1]),
        (MID, zmid),
        (SIDE, zrecv),
        (SLICE, grads.at[: n_tp - 1]),
        (ROW, grads_all.at[: n_tp * n_dp - 1]),
        (SUM, sums_all.at[: n_tp * n_dp - 1]),
        (PEER, peer_all),
        (MIX, mix_recv),
        (ALONG, gram_z.at[: n_tp - 1]),
    ):
        drain(ref, sems.at[0, phase])
    received(GATHER, gram_all.at[: n_dp - 1])
    triangle = jnp.concatenate([gram_all[r] for r in range(n_dp)], axis=0)
    corner = triangle[LANES:rows]
    gram = jnp.concatenate(
        [
            jnp.concatenate([triangle[:LANES], corner.T], axis=1),
            jnp.concatenate([corner, triangle[rows : rows + LANES]], axis=1),
        ],
        axis=0,
    )
    solved_out[...] = solve(gram, target)
    drain(gram_all.at[: n_dp - 1], sems.at[0, GATHER])
    relayed(4, half - 1)
    root_write = pltpu.make_async_copy(root, root_out, out_sem.at[0])
    root_write.start()
    drain(root.at[:, : (n_dp - 2) * LANES], root_sems.at[5])
    root_write.wait()


def last_kernel(root_ref, solved_ref, grads_ref, root_out, pre_out, pre, sem):
    write = pltpu.make_async_copy(root_ref, root_out, sem.at[0])
    write.start()
    pre[...] = grads_ref[...] - dot_mid(solved_ref[...], root_ref[...])
    pre_write = pltpu.make_async_copy(pre, pre_out, sem.at[1])
    pre_write.start()
    write.wait()
    pre_write.wait()


def fused_body(
    activations,
    out_grads,
    input_proj,
    grad_proj,
    example_count,
    child_order,
    prior_sketch,
    fold_map,
    merge_mix,
):
    n_dp, n_tp = lax.axis_size("dp"), lax.axis_size("tensor")
    rows, columns = prior_sketch.shape
    slots = activations.shape[0] // SEQ
    f32, bf16 = jnp.float32, jnp.bfloat16
    width, hidden = activations.shape[1], out_grads.shape[1]
    hbm = pl.BlockSpec(memory_space=pltpu.HBM)
    anywhere = pl.BlockSpec(memory_space=pl.ANY)
    vmem = pl.BlockSpec(memory_space=pltpu.VMEM)
    smem = pl.BlockSpec(memory_space=pltpu.SMEM)
    devices = n_dp * n_tp
    own_rows = 3 * LANES // n_dp
    part_rows = own_rows + 2 * slots
    pin = functools.partial(pltpu.with_memory_space_constraint, memory_space=pltpu.HBM)
    root, solved, grads = pl.pallas_call(
        functools.partial(fused_kernel, n_dp, n_tp),
        out_shape=(
            jax.ShapeDtypeStruct((rows, columns), f32),
            jax.ShapeDtypeStruct((slots, rows), f32),
            jax.ShapeDtypeStruct((slots, columns), f32),
        ),
        in_specs=[hbm, hbm, hbm, hbm, smem, hbm, hbm, hbm, hbm],
        out_specs=(anywhere, vmem, vmem),
        scratch_shapes=[
            pltpu.VMEM((slots, SEQ, width + hidden), bf16),
            pltpu.VMEM((RANK, width + hidden), bf16),
            pltpu.SMEM((1, n_dp), jnp.int32),
            pltpu.VMEM((rows, columns), f32),
            pltpu.VMEM((slots, rows), f32),
            pltpu.VMEM((rows, 2 * rows), f32),
            pltpu.VMEM((n_dp // 2, rows, LANES), f32),
            pltpu.VMEM((n_dp // 2, rows, LANES), f32),
            pltpu.VMEM((n_dp // 2, rows, LANES), f32),
            pltpu.VMEM((6, SEQ // 2, LANES), f32),
            pltpu.VMEM((SEQ // 2, LANES), f32),
            pltpu.VMEM((5, SEQ // 2, LANES), f32),
            pltpu.VMEM((RANK, LANES), f32),
            pltpu.VMEM((n_tp, n_dp, LANES), f32),
            pltpu.VMEM((n_tp, n_dp, LANES), f32),
            pltpu.VMEM((devices, 1, LANES), f32),
            pltpu.VMEM((devices, 1, LANES), f32),
            pltpu.VMEM((devices, 1, LANES), f32),
            pltpu.VMEM((n_dp // 2, rows, LANES), f32),
            pltpu.VMEM((n_dp // 2, rows, LANES), f32),
            pltpu.VMEM((devices, 1, LANES), f32),
            pltpu.VMEM((rows, columns), f32),
            pltpu.VMEM((n_dp, part_rows, LANES), f32),
            pltpu.VMEM((n_dp // 2, part_rows, LANES), f32),
            pltpu.VMEM((n_tp, part_rows, LANES), f32),
            pltpu.VMEM((n_dp, own_rows, LANES), f32),
            pltpu.SemaphoreType.DMA((9,)),
            pltpu.SemaphoreType.DMA((2, 12)),
            pltpu.SemaphoreType.DMA((6,)),
            pltpu.SemaphoreType.DMA((1,)),
            pltpu.SemaphoreType.REGULAR,
        ],
        compiler_params=pltpu.CompilerParams(
            collective_id=0, has_side_effects=True, vmem_limit_bytes=32 * 2**20
        ),
    )(
        pin(activations),
        pin(out_grads),
        pin(input_proj.T),
        pin(grad_proj.T),
        example_count,
        pin(child_order.reshape(1, n_dp)),
        pin(prior_sketch),
        pin(fold_map.T),
        pin(merge_mix),
    )
    return pl.pallas_call(
        last_kernel,
        out_shape=(
            jax.ShapeDtypeStruct((rows, columns), f32),
            jax.ShapeDtypeStruct((slots, columns), f32),
        ),
        in_specs=[vmem] * 3,
        out_specs=(anywhere, anywhere),
        scratch_shapes=[pltpu.VMEM((slots, columns), f32), pltpu.SemaphoreType.DMA((2,))],
        compiler_params=pltpu.CompilerParams(vmem_limit_bytes=16 * 2**20),
    )(root, solved, grads)


def from_partner(value, axis, stride):
    mask = 2**stride
    pairs = [(source, source ^ mask) for source in range(lax.axis_size(axis))]
    return lax.ppermute(value, axis, pairs)


def body(
    activations,
    out_grads,
    input_proj,
    grad_proj,
    example_count,
    child_order,
    prior_sketch,
    fold_map,
    merge_mix,
):
    tensor_count = lax.axis_size("tensor")
    own_rank = RANK // tensor_count
    example_slots = activations.shape[0] // SEQ
    sketch_rows = prior_sketch.shape[0]
    input_part = jnp.dot(activations, input_proj, preferred_element_type=jnp.float32)
    grad_part = jnp.dot(out_grads, grad_proj, preferred_element_type=jnp.float32)
    input_side, grad_side = lax.psum((input_part, grad_part), "tensor")
    grad_own = lax.dynamic_slice_in_dim(grad_side, lax.axis_index("tensor") * own_rank, own_rank, 1)
    grad_blocks = grad_own.reshape(example_slots, SEQ, own_rank)
    input_blocks = input_side.reshape(example_slots, SEQ, RANK)
    example_grad = jnp.einsum(
        "eta,etb->eab", grad_blocks, input_blocks, precision=lax.Precision.HIGHEST
    )
    example_grad = example_grad.reshape(example_slots, own_rank * RANK) / jnp.sqrt(jnp.float32(SEQ))
    live = jnp.arange(example_slots, dtype=jnp.int32) < example_count[0]
    example_grad = jnp.where(live[:, None], example_grad, jnp.zeros_like(example_grad))
    leaf_node = prior_sketch + jnp.dot(fold_map, example_grad, precision=lax.Precision.HIGHEST)
    leaf_weight = lax.psum(jnp.sum(leaf_node * leaf_node), "tensor")
    mix_first = merge_mix[:, :sketch_rows]
    mix_second = merge_mix[:, sketch_rows:]
    depth_count = lax.axis_size("dp").bit_length() - 1
    rank_index = lax.axis_index("dp")
    sketch_node = leaf_node
    sketch_weight = leaf_weight
    for level_index in range(depth_count):
        sibling_node, sibling_weight = from_partner((sketch_node, sketch_weight), "dp", level_index)
        upper_half = rank_index >> level_index & 1
        block_start = rank_index >> level_index + 1 << level_index + 1
        flip_order = child_order[block_start + (1 << level_index) - 1]
        own_first = upper_half == flip_order
        first = jnp.where(own_first, sketch_node, sibling_node)
        second = jnp.where(own_first, sibling_node, sketch_node)
        first_weight = jnp.where(own_first, sketch_weight, sibling_weight)
        second_weight = jnp.where(own_first, sibling_weight, sketch_weight)
        mixture = jnp.dot(mix_first, first, precision=lax.Precision.HIGHEST) + jnp.dot(
            mix_second, second, precision=lax.Precision.HIGHEST
        )
        mix_total = lax.psum(jnp.sum(mixture * mixture), "tensor")
        sketch_weight = first_weight + second_weight
        sketch_node = mixture * jnp.sqrt(sketch_weight / (mix_total + 1e-06))
    gram_part = jnp.dot(sketch_node, sketch_node.T, precision=lax.Precision.HIGHEST)
    product_part = jnp.dot(sketch_node, example_grad.T, precision=lax.Precision.HIGHEST)
    gram, sketch_grad = lax.psum((gram_part, product_part), "tensor")
    damping = jnp.trace(gram) / sketch_rows
    system = gram + damping * jnp.eye(sketch_rows, dtype=jnp.float32)
    factor = jnp.linalg.cholesky(system)
    solved = jax.scipy.linalg.cho_solve((factor, True), sketch_grad)
    preconditioned = example_grad - jnp.dot(solved.T, sketch_node, precision=lax.Precision.HIGHEST)
    return (sketch_node, preconditioned)


def fits_fused(rows, columns, slots, n_dp, n_tp):
    return (
        columns == n_dp * LANES
        and slots == n_tp
        and 2 * RANK == LANES
        and n_dp == 8
        and n_tp == 4
        and rows == 2 * LANES
    )


def step(*args):
    n_dp, n_tp = lax.axis_size("dp"), lax.axis_size("tensor")
    slots = args[0].shape[0] // SEQ
    rows, columns = args[6].shape
    if fits_fused(rows, columns, slots, n_dp, n_tp):
        return fused_body(*args)
    return body(*args)


def solution(mesh):
    in_specs = (
        P("dp", "tensor"),
        P("dp", "tensor"),
        P("tensor", None),
        P("tensor", None),
        P("dp"),
        P(),
        P("dp", "tensor"),
        P(),
        P(),
    )
    out_specs = (P(None, "tensor"), P("dp", "tensor"))
    return jax.shard_map(step, mesh=mesh, in_specs=in_specs, out_specs=out_specs, check_vma=False)
```

```python
import functools

import jax
import jax.numpy as jnp
from jax import lax
from jax.experimental import pallas as pl
from jax.experimental.pallas import tpu as pltpu
from jax.sharding import PartitionSpec as P

RANK = 64
SEQ = 128
LANES = 128
HIGHEST = lax.Precision.HIGHEST
MESH = pl.DeviceIdType.MESH


def newton_plan(rows):
    low, high = 0.999, (rows + 1) * 1.001
    first = 2.0 / (low + high)
    reach, scales = first * low, []
    while 1.0 - reach > 1e-3:
        grown = reach * (2.0 - reach)
        scale = 2.0 / (1.0 + grown)
        scales.append(scale)
        reach = grown * scale
    return first, scales


def dot_high(left, right):
    return jnp.dot(left, right, precision=HIGHEST, preferred_element_type=jnp.float32)


def dot_flip(left, right):
    return lax.dot_general(left, right, (((1,), (1,)), ((), ())), preferred_element_type=jnp.float32)


def halves(value):
    high = value.astype(jnp.bfloat16)
    return high, (value - high.astype(jnp.float32)).astype(jnp.bfloat16)


def dot_halves(left, right):
    (a, b), (c, d) = left, right
    out = jnp.dot(a, c, preferred_element_type=jnp.float32)
    out = out + jnp.dot(a, d, preferred_element_type=jnp.float32)
    return out + jnp.dot(b, c, preferred_element_type=jnp.float32)


def dot_mid(left, right):
    return dot_halves(halves(left), halves(right))


def dot_flip_halves(left, right):
    (a, b), (c, d) = left, right
    return dot_flip(jnp.concatenate([a, a, b], axis=1), jnp.concatenate([c, d, c], axis=1))


def dot_rows_halved(left, right):
    (a, b), (c, d) = left, right
    left = jnp.concatenate([a, a, b], axis=1)
    right = jnp.concatenate([c, d, c], axis=0)
    half = left.shape[0] // 2
    return jnp.concatenate(
        [
            jnp.dot(left[:half], right, preferred_element_type=jnp.float32),
            jnp.dot(left[half:], right, preferred_element_type=jnp.float32),
        ],
        axis=0,
    )


def thirds(value):
    high = value.astype(jnp.bfloat16)
    return (high, *halves(value - high.astype(jnp.float32)))


def dot_thirds(left, right):
    count = left.shape[0]
    stack = jnp.concatenate(thirds(left), axis=0)
    a, b, c = (jnp.dot(stack, part, preferred_element_type=jnp.float32) for part in thirds(right))
    high = a[count : 2 * count] + b[:count]
    low = (a[2 * count :] + b[count : 2 * count]) + c[:count]
    return a[:count] + (high + low)


def stacked(value, order):
    high = value.astype(jnp.bfloat16).astype(jnp.float32)
    both = (high, value - high)
    return jnp.concatenate([both[i] for i in order], axis=0)


def solve(gram, target):
    rows = gram.shape[0]
    eye = lax.broadcasted_iota(jnp.int32, gram.shape, 0) == lax.broadcasted_iota(jnp.int32, gram.shape, 1)
    system = gram + jnp.where(eye, 1.0, 0.0)
    first, scales = newton_plan(rows)
    state, solved, path = first * system, first * target, None
    for index, scale in enumerate(scales):
        factor = jnp.where(eye, 2.0 * scale, 0.0) - scale * state
        factor_halves = halves(factor)
        solved = dot_halves(halves(solved), factor_halves)
        if index < len(scales) - 1:
            state = dot_rows_halved(halves(state), factor_halves)
            if path is None:
                path = factor_halves[0]
            else:
                path = jnp.dot(path, factor_halves[0], preferred_element_type=jnp.float32)
                path = path.astype(jnp.bfloat16)
    rest = (first * (target - dot_thirds(solved, system))).astype(jnp.bfloat16)
    step = jnp.dot(rest, path, preferred_element_type=jnp.float32)
    return solved + dot_halves(halves(step), factor_halves)


def fused_kernel(
    n_dp,
    n_tp,
    act_hbm,
    out_hbm,
    wi_hbm,
    wo_hbm,
    count_ref,
    order_hbm,
    prior_hbm,
    fold_hbm,
    mix_hbm,
    root_out,
    solved_out,
    grads_out,
    tokens,
    weights,
    order_ref,
    prior,
    fold_ref,
    mix_ref,
    pair_in,
    node_send,
    node_recv,
    zsend,
    zmid,
    zrecv,
    full,
    slices_send,
    grads,
    grads_rows,
    grads_all,
    peer_all,
    mix_send,
    mix_recv,
    sums_all,
    root,
    gram_part,
    gram_rs,
    gram_z,
    gram_all,
    load_sem,
    sems,
    root_sems,
    out_sem,
    ready_sem,
):
    f32 = jnp.float32
    me, z = lax.axis_index("dp"), lax.axis_index("tensor")
    rows = prior.shape[0]
    levels = n_dp.bit_length() - 1

    def dp_of(k):
        return lax.rem(me + k, n_dp)

    def tp_of(k):
        return lax.rem(z + k, n_tp)

    width = act_hbm.shape[1]
    near = z + 1 - 2 * lax.rem(z, 2)
    far = z + 2 - 4 * (z // 2)
    diagonal = near + 2 - 4 * (near // 2)
    order = (diagonal, far, near, z)
    used = []

    def load(*pairs):
        for source, target in pairs:
            pltpu.make_async_copy(source, target, load_sem.at[len(used)]).start()
        used.append(None)
        return len(used) - 1

    def drain(ref, sem):
        pltpu.make_async_copy(ref, ref, sem).wait()

    def load_chunk(index, start=0, count=SEQ):
        span = pl.ds(pl.multiple_of(order[index] * SEQ + start, count), count)
        into = tokens.at[index, start : start + count]
        return load((act_hbm.at[span], into.at[:, :width]), (out_hbm.at[span], into.at[:, width:]))

    order_load = load((order_hbm, order_ref))
    weight_load = load((wi_hbm, weights.at[:, :width]), (wo_hbm, weights.at[:, width:]))
    mid = SEQ // 2
    half_loads = [load_chunk(0, start, mid) for start in (0, mid)]
    prior_load = load((prior_hbm, prior))
    mix_load = load((mix_hbm, mix_ref))
    chunk_loads = [None] + [load_chunk(index) for index in range(1, n_tp)]
    fold_load = load((fold_hbm, fold_ref))

    def tile_of(owner):
        return pl.ds(pl.multiple_of(owner * LANES, LANES), LANES)

    barrier = pltpu.get_barrier_semaphore()
    for k in range(1, n_tp):
        pl.semaphore_signal(barrier, inc=1, device_id={"tensor": tp_of(k)}, device_id_type=MESH)
    for k in range(1, n_dp):
        pl.semaphore_signal(barrier, inc=1, device_id={"dp": dp_of(k)}, device_id_type=MESH)

    half = n_dp // 2
    core, chip = lax.rem(me, 2), me // 2
    partner = me + 1 - 2 * core
    chip_x = chip + 1 - 2 * lax.rem(chip, 2)
    chip_y = chip + 2 - 4 * (chip // 2)
    chip_d = half - 1 - chip

    PAIR, NODE, MID, SIDE, SLICE, ROW, PEER, SUM, SCATTER, ALONG, GATHER, MIX = range(12)

    def push(phase, source, target, **device):
        pltpu.make_async_remote_copy(
            src_ref=source,
            dst_ref=target,
            send_sem=sems.at[0, phase],
            recv_sem=sems.at[1, phase],
            device_id=device,
            device_id_type=MESH,
        ).start()

    def received(phase, ref):
        drain(ref, sems.at[1, phase])

    def exchange(axis, phase, source, target):
        size, other = (n_tp, tp_of) if axis == "tensor" else (n_dp, dp_of)
        for k in range(1, size):
            push(phase, source(other(k)), target, **{axis: other(k)})

    def exchange_all(phase, source, target):
        for j in sorted(range(n_tp), key=lambda j: -min(j, n_tp - j)):
            for k in range(n_dp):
                if (j, k) != (0, 0):
                    push(phase, source(dp_of(k), tp_of(j)), target, dp=dp_of(k), tensor=tp_of(j))

    def sides_of_rows(index, start, count):
        spans = [slice(start + h * count, start + (h + 1) * count) for h in range(2)]
        right = [dot_flip(tokens[index, span, width:], weights[:, width:]) for span in spans]
        left = [dot_flip(tokens[index, span, :width], weights[:, :width]) for span in spans]
        return [jnp.concatenate(pair, axis=1) for pair in zip(left, right)]

    def sides_of_chunk(index):
        drain(tokens.at[index], load_sem.at[chunk_loads[index]])
        return sides_of_rows(index, 0, mid)

    def sides_of_half(h):
        drain(tokens.at[0, h * mid : (h + 1) * mid], load_sem.at[half_loads[h]])
        zsend[h] = jnp.concatenate(sides_of_rows(0, h * mid, mid // 2), axis=0)

    drain(weights, load_sem.at[weight_load])
    sides_of_half(0)
    pl.semaphore_wait(barrier, n_dp + n_tp - 2)
    push(MID, zsend.at[0], zmid, tensor=near)
    for q in range(half):
        push(PAIR, prior_hbm.at[:, tile_of(2 * q + 1 - core)], pair_in.at[q], dp=partner)
    for k in range(1, n_dp):
        pl.semaphore_signal(ready_sem, inc=1, device_id={"dp": dp_of(k)}, device_id_type=MESH)
    sides_of_half(1)
    push(SIDE, zsend.at[1], zrecv.at[4], tensor=diagonal)
    far_sides = sides_of_chunk(1)
    zsend[3] = far_sides[1]
    push(SIDE, zsend.at[3], zrecv.at[3], tensor=far)
    zsend[4], zsend[5] = sides_of_chunk(2)
    push(SIDE, zsend.at[4:6], zrecv.at[0:2], tensor=near)

    drain(order_ref, load_sem.at[order_load])
    drain(prior, load_sem.at[prior_load])
    drain(mix_ref, load_sem.at[mix_load])
    received(PAIR, pair_in)
    first_mix, second_mix = mix_ref[:, :rows], mix_ref[:, rows:]
    own_first = order_ref[0, 2 * chip] == core
    own_half = [prior[:, tile_of(2 * q + core)] for q in range(half)]
    firsts = [jnp.where(own_first, own_half[q], pair_in[q]) for q in range(half)]
    seconds = [jnp.where(own_first, pair_in[q], own_half[q]) for q in range(half)]
    first_halves, second_halves = halves(first_mix), halves(second_mix)
    mixed = dot_halves(first_halves, halves(jnp.concatenate(firsts, axis=1)))
    mixed = mixed + dot_halves(second_halves, halves(jnp.concatenate(seconds, axis=1)))
    for q in range(half):
        node_send[q] = mixed[:, q * LANES : (q + 1) * LANES]
    for other in (chip_x, chip_y, chip_d):
        push(NODE, node_send.at[other], node_recv.at[chip], dp=2 * other + core)
    node_recv[chip] = node_send[chip]
    received(MID, zmid)
    zsend[2] = far_sides[0] + zmid[...]
    push(SIDE, zsend.at[2], zrecv.at[2], tensor=far)
    own_sides = sides_of_chunk(3)

    drain(fold_ref, load_sem.at[fold_load])
    fold_rows = fold_ref[...]

    def through(value):
        count = value.shape[0]
        both = stacked(value, (0, 1)).astype(jnp.bfloat16)
        high = value.astype(jnp.bfloat16)
        results = []
        for top, bottom in (first_halves, second_halves):
            most = dot_flip(both, top)
            results.append(most[:count] + (most[count:] + dot_flip(high, bottom)))
        return results

    paths = [[jnp.concatenate(through(fold_rows), axis=0)]]
    for level in range(1, levels):
        count = paths[-1][0].shape[0]
        mapped = through(jnp.concatenate(paths[-1], axis=0))
        paths.append([v[i : i + count] for v in mapped for i in range(0, v.shape[0], count)])
    paths = [[stacked(p, (0, 0, 1)).T.astype(jnp.bfloat16) for p in level] for level in paths]
    fold = fold_rows.T

    received(SIDE, zrecv)
    sides = jnp.concatenate(
        [
            (own_sides[0] + zrecv[0]) + zrecv[2],
            (own_sides[1] + zrecv[1]) + (zrecv[3] + zrecv[4]),
        ],
        axis=0,
    )
    lane = lax.broadcasted_iota(jnp.int32, sides.shape, 1)
    doubled = jnp.where(lane < RANK, sides, pltpu.roll(sides, RANK, 1))
    product = dot_mid(sides.T, doubled) / jnp.sqrt(f32(SEQ))
    product = jnp.where(z < count_ref[0], product, jnp.zeros_like(product))
    full[...] = product[RANK:]
    even = full[pl.ds(0, RANK // 2, stride=2), :]
    odd = full[pl.ds(1, RANK // 2, stride=2), :]
    lane = lax.broadcasted_iota(jnp.int32, even.shape, 1)
    mine = jnp.where(lane < RANK, even, odd)
    for row in range(n_tp * n_dp):
        grads_rows[row] = mine[row : row + 1]
    for index in range(n_tp):
        slices_send[index] = mine[index * n_dp : (index + 1) * n_dp]
    grads[z] = slices_send[z]
    slot = me * n_tp + z
    grads_all[slot] = grads_rows[z * n_dp + me]
    pl.semaphore_wait(ready_sem, n_dp - 1)
    exchange("tensor", SLICE, lambda t: slices_send.at[t], grads.at[z])
    exchange_all(ROW, lambda d, t: grads_rows.at[t * n_dp + d], grads_all.at[slot])

    flags = [
        [order_ref[0, j * 2 ** (level + 1) + 2**level - 1] == 1 for j in range(n_dp >> (level + 1))]
        for level in range(levels)
    ]

    def pick(flip, lower, upper):
        first = [jnp.where(flip, b, a) for a, b in zip(lower, upper)]
        return first, [jnp.where(flip, a, b) for a, b in zip(lower, upper)]

    def total(value):
        return jnp.sum(jnp.sum(value, axis=0, keepdims=True), axis=1, keepdims=True)

    received(SLICE, grads.at[: n_tp - 1])
    leaf_square = jnp.zeros((rows, LANES), f32)
    for tile in range(n_dp):
        leaf = prior[:, tile * LANES : (tile + 1) * LANES]
        for e in range(n_tp):
            step = grads[e, tile : tile + 1, :]
            grads_out[e : e + 1, tile * LANES : (tile + 1) * LANES] = step
            leaf = leaf + fold[:, e : e + 1] * step
        leaf_square = leaf_square + leaf * leaf
    own_mass = total(leaf_square)

    received(NODE, node_recv.at[: half - 1])
    mixtures = [[[node_recv[j]] for j in range(half)]]
    for level in range(1, levels):
        below = mixtures[-1]
        sides_of = [pick(flags[level][j], below[2 * j], below[2 * j + 1]) for j in range(len(below) // 2)]
        count = len(below[0])
        left = dot_halves(first_halves, halves(jnp.concatenate([v for f, _ in sides_of for v in f], axis=1)))
        right = dot_halves(second_halves, halves(jnp.concatenate([v for _, g in sides_of for v in g], axis=1)))
        mixtures.append(
            [
                [
                    side[:, (j * count + i) * LANES : (j * count + i + 1) * LANES]
                    for side in (left, right)
                    for i in range(count)
                ]
                for j in range(len(sides_of))
            ]
        )

    for index, part in enumerate(mixtures[-1][0]):
        mix_send[index] = part
    push(MIX, mix_send, mix_recv, dp=partner)

    received(ROW, grads_all.at[: n_tp * n_dp - 1])
    push(PEER, grads_all, peer_all, dp=partner)

    def steps_from(rows_of):
        steps_of = [
            [jnp.concatenate([rows_of[r * n_tp + e] for e in range(n_tp)], axis=0)] for r in range(n_dp)
        ]
        return steps_of, jnp.concatenate([step[0] for step in steps_of], axis=0)

    def merge_steps(level, steps_of):
        merged_steps = []
        for j in range(len(steps_of) // 2):
            first, second = pick(flags[level][j], steps_of[2 * j], steps_of[2 * j + 1])
            if level == 0:
                merged_steps.append([jnp.concatenate([first[0], second[0]], axis=0)])
            else:
                merged_steps.append(first + second)
        return merged_steps

    def updates_of(level, merged_steps):
        return [
            jnp.dot(
                path,
                jnp.concatenate([stacked(g[i], (0, 1, 0)) for g in merged_steps], axis=1).astype(jnp.bfloat16),
                preferred_element_type=f32,
            )
            for i, path in enumerate(paths[level])
        ]

    steps_of, every = steps_from(grads_all)
    sums, products, nodes = [], [], []
    for level in range(levels):
        level_products, level_nodes = [], []
        merged_steps = merge_steps(level, steps_of)
        updates = updates_of(level, merged_steps)
        for j in range(len(merged_steps)):
            parts = [
                v + update[:, j * LANES : (j + 1) * LANES]
                for v, update in zip(mixtures[level][j], updates)
            ]
            index_of = {}
            for a in range(len(parts)):
                for b in range(a + 1):
                    index_of[a, b] = n_dp + len(sums)
                    sums.append(total(parts[a] * parts[b]))
            level_products.append(index_of)
            level_nodes.append(parts)
        steps_of = merged_steps
        products.append(level_products)
        nodes = level_nodes
    lane = lax.broadcasted_iota(jnp.int32, (1, LANES), 1)
    packed = jnp.where(lane == me, own_mass, jnp.zeros((1, LANES), f32))
    for index, value in enumerate(sums):
        packed = jnp.where(lane == n_dp + index, value, packed)
    sums_all[slot] = packed
    exchange_all(SUM, lambda d, t: sums_all.at[slot], sums_all.at[slot])
    received(PEER, peer_all)
    received(MIX, mix_recv)
    steps_of, peer_every = steps_from(peer_all)
    for level in range(levels):
        steps_of = merge_steps(level, steps_of)
    peer_parts = [mix_recv[i] + update for i, update in enumerate(updates_of(levels - 1, steps_of))]
    every_halves = halves(jnp.concatenate([every, peer_every], axis=1))
    received(SUM, sums_all.at[: n_tp * n_dp - 1])
    parts_of = [sums_all[index] for index in range(n_tp * n_dp)]
    while len(parts_of) > 1:
        parts_of = [a + b for a, b in zip(parts_of[0::2], parts_of[1::2])]
    packed = parts_of[0]

    def summed(index):
        return jnp.sum(jnp.where(lane == index, packed, 0.0), axis=1, keepdims=True)

    masses = [summed(index) for index in range(n_dp)]
    scales = [[jnp.ones((1, 1), f32)] for _ in range(n_dp)]
    for level in range(levels):
        new_masses, new_scales = [], []
        for j, products_of in enumerate(products[level]):
            flip = flags[level][j]
            lower, upper = scales[2 * j], scales[2 * j + 1]
            if level == 0:
                coefs = [jnp.ones((1, 1), f32)]
            else:
                coefs = [jnp.where(flip, b, a) for a, b in zip(lower, upper)]
                coefs += [jnp.where(flip, a, b) for a, b in zip(lower, upper)]
            square = jnp.zeros((1, 1), f32)
            for (a, b), index in products_of.items():
                term = coefs[a] * (coefs[b] * summed(index))
                square = square + (term if a == b else 2.0 * term)
            mass = masses[2 * j] + masses[2 * j + 1]
            scale = jnp.sqrt(mass / (jnp.maximum(square, 0.0) + 1e-06))
            trace = scale * scale * square
            new_masses.append(mass)
            new_scales.append([scale * c for c in coefs])
        masses, scales = new_masses, new_scales
    chunks = []
    for parts in (nodes[0], peer_parts):
        chunk = scales[0][0] * parts[0]
        for c, part in zip(scales[0][1:], parts[1:]):
            chunk = chunk + c * part
        chunks.append(chunk)
    root[:, tile_of(me)] = chunks[0]
    root[:, tile_of(partner)] = chunks[1]

    chunk_halves = halves(jnp.concatenate(chunks, axis=1))
    upper_halves, lower_halves = [[v[s] for v in chunk_halves] for s in (slice(0, LANES), slice(LANES, rows))]
    targets = dot_flip_halves(every_halves, chunk_halves)
    unit = rows / trace
    triangle = jnp.concatenate(
        [
            dot_flip_halves(upper_halves, upper_halves),
            dot_flip_halves(lower_halves, upper_halves),
            dot_flip_halves(lower_halves, lower_halves),
        ],
        axis=0,
    )
    own_rows = gram_all.shape[1]
    for r in range(n_dp):
        gram_part[r, :own_rows] = unit * triangle[r * own_rows : (r + 1) * own_rows]
        own = targets[r * n_tp : (r + 1) * n_tp]
        gram_part[r, own_rows:] = unit * jnp.concatenate([own[:, :LANES], own[:, LANES:]], axis=0)
    gram_rs[chip] = gram_part[me]
    for other in (chip_d, chip_x, chip_y):
        push(SCATTER, gram_part.at[2 * other + core], gram_rs.at[chip], dp=2 * other + core)
    dev_x, dev_y, dev_d = (2 * other + core for other in (chip_x, chip_y, chip_d))
    upper, lower = pl.ds(0, rows // 2), pl.ds(rows // 2, rows // 2)

    def relay(index, owner, device, span=slice(None)):
        block_of = root.at[span, tile_of(owner)]
        pltpu.make_async_remote_copy(
            src_ref=block_of,
            dst_ref=block_of,
            send_sem=root_sems.at[5],
            recv_sem=root_sems.at[index],
            device_id={"dp": device},
            device_id_type=MESH,
        ).start()

    def relayed(index, count):
        drain(root.at[:, : count * LANES] if count else root.at[upper, :LANES], root_sems.at[index])

    drain(gram_rs.at[: half - 1], sems.at[0, SCATTER])
    relay(0, me, dev_x)
    relay(1, me, dev_y)
    received(SCATTER, gram_rs.at[: half - 1])
    part = gram_rs[0]
    for index in range(1, half):
        part = part + gram_rs[index]
    gram_z[z] = part
    exchange("tensor", ALONG, lambda t: gram_z.at[z], gram_z.at[z])
    relayed(0, 1)
    relay(2, dev_x, dev_y, upper)
    relay(4, dev_x, partner)
    relayed(1, 1)
    relay(3, dev_y, dev_x, lower)
    relay(4, dev_y, partner)
    received(ALONG, gram_z.at[: n_tp - 1])
    part = gram_z[0]
    for index in range(1, n_tp):
        part = part + gram_z[index]
    gram_all[me] = part[:own_rows]
    target = jnp.concatenate([part[own_rows : own_rows + n_tp], part[own_rows + n_tp :]], axis=1)
    exchange("dp", GATHER, lambda t: gram_all.at[me], gram_all.at[me])
    relayed(2, 0)
    relayed(3, 0)
    relay(4, dev_d, partner)
    for phase, ref in (
        (PAIR, pair_in),
        (NODE, node_recv.at[: half - 1]),
        (MID, zmid),
        (SIDE, zrecv),
        (SLICE, grads.at[: n_tp - 1]),
        (ROW, grads_all.at[: n_tp * n_dp - 1]),
        (SUM, sums_all.at[: n_tp * n_dp - 1]),
        (PEER, peer_all),
        (MIX, mix_recv),
        (ALONG, gram_z.at[: n_tp - 1]),
    ):
        drain(ref, sems.at[0, phase])
    received(GATHER, gram_all.at[: n_dp - 1])
    triangle = jnp.concatenate([gram_all[r] for r in range(n_dp)], axis=0)
    corner = triangle[LANES:rows]
    gram = jnp.concatenate(
        [
            jnp.concatenate([triangle[:LANES], corner.T], axis=1),
            jnp.concatenate([corner, triangle[rows : rows + LANES]], axis=1),
        ],
        axis=0,
    )
    solved_out[...] = solve(gram, target)
    drain(gram_all.at[: n_dp - 1], sems.at[0, GATHER])
    relayed(4, half - 1)
    root_write = pltpu.make_async_copy(root, root_out, out_sem.at[0])
    root_write.start()
    drain(root.at[:, : (n_dp - 2) * LANES], root_sems.at[5])
    root_write.wait()


def last_kernel(root_ref, solved_ref, grads_ref, root_out, pre_out, pre, sem):
    write = pltpu.make_async_copy(root_ref, root_out, sem.at[0])
    write.start()
    pre[...] = grads_ref[...] - dot_mid(solved_ref[...], root_ref[...])
    pre_write = pltpu.make_async_copy(pre, pre_out, sem.at[1])
    pre_write.start()
    write.wait()
    pre_write.wait()


def fused_body(
    activations,
    out_grads,
    input_proj,
    grad_proj,
    example_count,
    child_order,
    prior_sketch,
    fold_map,
    merge_mix,
):
    n_dp, n_tp = lax.axis_size("dp"), lax.axis_size("tensor")
    rows, columns = prior_sketch.shape
    slots = activations.shape[0] // SEQ
    f32, bf16 = jnp.float32, jnp.bfloat16
    width, hidden = activations.shape[1], out_grads.shape[1]
    hbm = pl.BlockSpec(memory_space=pltpu.HBM)
    anywhere = pl.BlockSpec(memory_space=pl.ANY)
    vmem = pl.BlockSpec(memory_space=pltpu.VMEM)
    smem = pl.BlockSpec(memory_space=pltpu.SMEM)
    devices = n_dp * n_tp
    own_rows = 3 * LANES // n_dp
    part_rows = own_rows + 2 * slots
    pin = functools.partial(pltpu.with_memory_space_constraint, memory_space=pltpu.HBM)
    root, solved, grads = pl.pallas_call(
        functools.partial(fused_kernel, n_dp, n_tp),
        out_shape=(
            jax.ShapeDtypeStruct((rows, columns), f32),
            jax.ShapeDtypeStruct((slots, rows), f32),
            jax.ShapeDtypeStruct((slots, columns), f32),
        ),
        in_specs=[hbm, hbm, hbm, hbm, smem, hbm, hbm, hbm, hbm],
        out_specs=(anywhere, vmem, vmem),
        scratch_shapes=[
            pltpu.VMEM((slots, SEQ, width + hidden), bf16),
            pltpu.VMEM((RANK, width + hidden), bf16),
            pltpu.SMEM((1, n_dp), jnp.int32),
            pltpu.VMEM((rows, columns), f32),
            pltpu.VMEM((slots, rows), f32),
            pltpu.VMEM((rows, 2 * rows), f32),
            pltpu.VMEM((n_dp // 2, rows, LANES), f32),
            pltpu.VMEM((n_dp // 2, rows, LANES), f32),
            pltpu.VMEM((n_dp // 2, rows, LANES), f32),
            pltpu.VMEM((6, SEQ // 2, LANES), f32),
            pltpu.VMEM((SEQ // 2, LANES), f32),
            pltpu.VMEM((5, SEQ // 2, LANES), f32),
            pltpu.VMEM((RANK, LANES), f32),
            pltpu.VMEM((n_tp, n_dp, LANES), f32),
            pltpu.VMEM((n_tp, n_dp, LANES), f32),
            pltpu.VMEM((devices, 1, LANES), f32),
            pltpu.VMEM((devices, 1, LANES), f32),
            pltpu.VMEM((devices, 1, LANES), f32),
            pltpu.VMEM((n_dp // 2, rows, LANES), f32),
            pltpu.VMEM((n_dp // 2, rows, LANES), f32),
            pltpu.VMEM((devices, 1, LANES), f32),
            pltpu.VMEM((rows, columns), f32),
            pltpu.VMEM((n_dp, part_rows, LANES), f32),
            pltpu.VMEM((n_dp // 2, part_rows, LANES), f32),
            pltpu.VMEM((n_tp, part_rows, LANES), f32),
            pltpu.VMEM((n_dp, own_rows, LANES), f32),
            pltpu.SemaphoreType.DMA((10,)),
            pltpu.SemaphoreType.DMA((2, 12)),
            pltpu.SemaphoreType.DMA((6,)),
            pltpu.SemaphoreType.DMA((1,)),
            pltpu.SemaphoreType.REGULAR,
        ],
        compiler_params=pltpu.CompilerParams(
            collective_id=0, has_side_effects=True, vmem_limit_bytes=32 * 2**20
        ),
    )(
        pin(activations),
        pin(out_grads),
        pin(input_proj.T),
        pin(grad_proj.T),
        example_count,
        pin(child_order.reshape(1, n_dp)),
        pin(prior_sketch),
        pin(fold_map.T),
        pin(merge_mix),
    )
    return pl.pallas_call(
        last_kernel,
        out_shape=(
            jax.ShapeDtypeStruct((rows, columns), f32),
            jax.ShapeDtypeStruct((slots, columns), f32),
        ),
        in_specs=[vmem] * 3,
        out_specs=(anywhere, anywhere),
        scratch_shapes=[pltpu.VMEM((slots, columns), f32), pltpu.SemaphoreType.DMA((2,))],
        compiler_params=pltpu.CompilerParams(vmem_limit_bytes=16 * 2**20),
    )(root, solved, grads)


def from_partner(value, axis, stride):
    mask = 2**stride
    pairs = [(source, source ^ mask) for source in range(lax.axis_size(axis))]
    return lax.ppermute(value, axis, pairs)


def body(
    activations,
    out_grads,
    input_proj,
    grad_proj,
    example_count,
    child_order,
    prior_sketch,
    fold_map,
    merge_mix,
):
    tensor_count = lax.axis_size("tensor")
    own_rank = RANK // tensor_count
    example_slots = activations.shape[0] // SEQ
    sketch_rows = prior_sketch.shape[0]
    input_part = jnp.dot(activations, input_proj, preferred_element_type=jnp.float32)
    grad_part = jnp.dot(out_grads, grad_proj, preferred_element_type=jnp.float32)
    input_side, grad_side = lax.psum((input_part, grad_part), "tensor")
    grad_own = lax.dynamic_slice_in_dim(grad_side, lax.axis_index("tensor") * own_rank, own_rank, 1)
    grad_blocks = grad_own.reshape(example_slots, SEQ, own_rank)
    input_blocks = input_side.reshape(example_slots, SEQ, RANK)
    example_grad = jnp.einsum(
        "eta,etb->eab", grad_blocks, input_blocks, precision=lax.Precision.HIGHEST
    )
    example_grad = example_grad.reshape(example_slots, own_rank * RANK) / jnp.sqrt(jnp.float32(SEQ))
    live = jnp.arange(example_slots, dtype=jnp.int32) < example_count[0]
    example_grad = jnp.where(live[:, None], example_grad, jnp.zeros_like(example_grad))
    leaf_node = prior_sketch + jnp.dot(fold_map, example_grad, precision=lax.Precision.HIGHEST)
    leaf_weight = lax.psum(jnp.sum(leaf_node * leaf_node), "tensor")
    mix_first = merge_mix[:, :sketch_rows]
    mix_second = merge_mix[:, sketch_rows:]
    depth_count = lax.axis_size("dp").bit_length() - 1
    rank_index = lax.axis_index("dp")
    sketch_node = leaf_node
    sketch_weight = leaf_weight
    for level_index in range(depth_count):
        sibling_node, sibling_weight = from_partner((sketch_node, sketch_weight), "dp", level_index)
        upper_half = rank_index >> level_index & 1
        block_start = rank_index >> level_index + 1 << level_index + 1
        flip_order = child_order[block_start + (1 << level_index) - 1]
        own_first = upper_half == flip_order
        first = jnp.where(own_first, sketch_node, sibling_node)
        second = jnp.where(own_first, sibling_node, sketch_node)
        first_weight = jnp.where(own_first, sketch_weight, sibling_weight)
        second_weight = jnp.where(own_first, sibling_weight, sketch_weight)
        mixture = jnp.dot(mix_first, first, precision=lax.Precision.HIGHEST) + jnp.dot(
            mix_second, second, precision=lax.Precision.HIGHEST
        )
        mix_total = lax.psum(jnp.sum(mixture * mixture), "tensor")
        sketch_weight = first_weight + second_weight
        sketch_node = mixture * jnp.sqrt(sketch_weight / (mix_total + 1e-06))
    gram_part = jnp.dot(sketch_node, sketch_node.T, precision=lax.Precision.HIGHEST)
    product_part = jnp.dot(sketch_node, example_grad.T, precision=lax.Precision.HIGHEST)
    gram, sketch_grad = lax.psum((gram_part, product_part), "tensor")
    damping = jnp.trace(gram) / sketch_rows
    system = gram + damping * jnp.eye(sketch_rows, dtype=jnp.float32)
    factor = jnp.linalg.cholesky(system)
    solved = jax.scipy.linalg.cho_solve((factor, True), sketch_grad)
    preconditioned = example_grad - jnp.dot(solved.T, sketch_node, precision=lax.Precision.HIGHEST)
    return (sketch_node, preconditioned)


def fits_fused(rows, columns, slots, n_dp, n_tp):
    return (
        columns == n_dp * LANES
        and slots == n_tp
        and 2 * RANK == LANES
        and n_dp == 8
        and n_tp == 4
        and rows == 2 * LANES
    )


def step(*args):
    n_dp, n_tp = lax.axis_size("dp"), lax.axis_size("tensor")
    slots = args[0].shape[0] // SEQ
    rows, columns = args[6].shape
    if fits_fused(rows, columns, slots, n_dp, n_tp):
        return fused_body(*args)
    return body(*args)


def solution(mesh):
    in_specs = (
        P("dp", "tensor"),
        P("dp", "tensor"),
        P("tensor", None),
        P("tensor", None),
        P("dp"),
        P(),
        P("dp", "tensor"),
        P(),
        P(),
    )
    out_specs = (P(None, "tensor"), P("dp", "tensor"))
    return jax.shard_map(step, mesh=mesh, in_specs=in_specs, out_specs=out_specs, check_vma=False)
```

```python
import functools

import jax
import jax.numpy as jnp
from jax import lax
from jax.experimental import pallas as pl
from jax.experimental.pallas import tpu as pltpu
from jax.sharding import PartitionSpec as P

RANK = 64
SEQ = 128
LANES = 128
HIGHEST = lax.Precision.HIGHEST
MESH = pl.DeviceIdType.MESH


def newton_plan(rows):
    low, high = 0.999, (rows + 1) * 1.001
    first = 2.0 / (low + high)
    reach, scales = first * low, []
    while 1.0 - reach > 1e-3:
        grown = reach * (2.0 - reach)
        scale = 2.0 / (1.0 + grown)
        scales.append(scale)
        reach = grown * scale
    return first, scales


def dot_high(left, right):
    return jnp.dot(left, right, precision=HIGHEST, preferred_element_type=jnp.float32)


def dot_flip(left, right):
    return lax.dot_general(left, right, (((1,), (1,)), ((), ())), preferred_element_type=jnp.float32)


def halves(value):
    high = value.astype(jnp.bfloat16)
    return high, (value - high.astype(jnp.float32)).astype(jnp.bfloat16)


def dot_halves(left, right):
    (a, b), (c, d) = left, right
    out = jnp.dot(a, c, preferred_element_type=jnp.float32)
    out = out + jnp.dot(a, d, preferred_element_type=jnp.float32)
    return out + jnp.dot(b, c, preferred_element_type=jnp.float32)


def dot_mid(left, right):
    return dot_halves(halves(left), halves(right))


def dot_flip_halves(left, right):
    (a, b), (c, d) = left, right
    return dot_flip(jnp.concatenate([a, a, b], axis=1), jnp.concatenate([c, d, c], axis=1))


def dot_rows_halved(left, right):
    (a, b), (c, d) = left, right
    left = jnp.concatenate([a, a, b], axis=1)
    right = jnp.concatenate([c, d, c], axis=0)
    half = left.shape[0] // 2
    return jnp.concatenate(
        [
            jnp.dot(left[:half], right, preferred_element_type=jnp.float32),
            jnp.dot(left[half:], right, preferred_element_type=jnp.float32),
        ],
        axis=0,
    )


def thirds(value):
    high = value.astype(jnp.bfloat16)
    return (high, *halves(value - high.astype(jnp.float32)))


def dot_thirds(left, right):
    count = left.shape[0]
    stack = jnp.concatenate(thirds(left), axis=0)
    a, b, c = (jnp.dot(stack, part, preferred_element_type=jnp.float32) for part in thirds(right))
    high = a[count : 2 * count] + b[:count]
    low = (a[2 * count :] + b[count : 2 * count]) + c[:count]
    return a[:count] + (high + low)


def stacked(value, order):
    high = value.astype(jnp.bfloat16).astype(jnp.float32)
    both = (high, value - high)
    return jnp.concatenate([both[i] for i in order], axis=0)


def solve(gram, target):
    rows = gram.shape[0]
    eye = lax.broadcasted_iota(jnp.int32, gram.shape, 0) == lax.broadcasted_iota(jnp.int32, gram.shape, 1)
    system = gram + jnp.where(eye, 1.0, 0.0)
    first, scales = newton_plan(rows)
    state, solved, path = first * system, first * target, None
    for index, scale in enumerate(scales):
        factor = jnp.where(eye, 2.0 * scale, 0.0) - scale * state
        factor_halves = halves(factor)
        solved = dot_halves(halves(solved), factor_halves)
        if index < len(scales) - 1:
            state = dot_rows_halved(halves(state), factor_halves)
            if path is None:
                path = factor_halves[0]
            else:
                path = jnp.dot(path, factor_halves[0], preferred_element_type=jnp.float32)
                path = path.astype(jnp.bfloat16)
    rest = (first * (target - dot_thirds(solved, system))).astype(jnp.bfloat16)
    step = jnp.dot(rest, path, preferred_element_type=jnp.float32)
    return solved + dot_halves(halves(step), factor_halves)


def fused_kernel(
    n_dp,
    n_tp,
    act_hbm,
    out_hbm,
    wi_hbm,
    wo_hbm,
    count_ref,
    order_hbm,
    prior_hbm,
    fold_hbm,
    mix_hbm,
    root_out,
    solved_out,
    grads_out,
    tokens,
    weights,
    order_ref,
    prior,
    fold_ref,
    mix_ref,
    pair_in,
    node_send,
    node_recv,
    zsend,
    zmid,
    zrecv,
    full,
    slices_send,
    grads,
    grads_rows,
    grads_all,
    peer_all,
    mix_send,
    mix_recv,
    sums_all,
    root,
    gram_part,
    gram_rs,
    gram_z,
    gram_all,
    load_sem,
    sems,
    root_sems,
    out_sem,
    ready_sem,
):
    f32 = jnp.float32
    me, z = lax.axis_index("dp"), lax.axis_index("tensor")
    rows = prior.shape[0]
    levels = n_dp.bit_length() - 1

    def dp_of(k):
        return lax.rem(me + k, n_dp)

    def tp_of(k):
        return lax.rem(z + k, n_tp)

    width = act_hbm.shape[1]
    near = z + 1 - 2 * lax.rem(z, 2)
    far = z + 2 - 4 * (z // 2)
    diagonal = near + 2 - 4 * (near // 2)
    order = (diagonal, far, near, z)
    used = []

    def load(*pairs):
        for source, target in pairs:
            pltpu.make_async_copy(source, target, load_sem.at[len(used)]).start()
        used.append(None)
        return len(used) - 1

    def drain(ref, sem):
        pltpu.make_async_copy(ref, ref, sem).wait()

    def load_chunk(index, start=0, count=SEQ):
        span = pl.ds(pl.multiple_of(order[index] * SEQ + start, count), count)
        into = tokens.at[index, start : start + count]
        return load((act_hbm.at[span], into.at[:, :width]), (out_hbm.at[span], into.at[:, width:]))

    order_load = load((order_hbm, order_ref))
    weight_load = load((wi_hbm, weights.at[:, :width]), (wo_hbm, weights.at[:, width:]))
    mid = SEQ // 2
    half_loads = [load_chunk(0, start, mid) for start in (0, mid)]
    prior_load = load((prior_hbm, prior))
    mix_load = load((mix_hbm, mix_ref))
    chunk_loads = [None] + [load_chunk(index) for index in range(1, n_tp)]
    fold_load = load((fold_hbm, fold_ref))

    def tile_of(owner):
        return pl.ds(pl.multiple_of(owner * LANES, LANES), LANES)

    barrier = pltpu.get_barrier_semaphore()
    for k in range(1, n_tp):
        pl.semaphore_signal(barrier, inc=1, device_id={"tensor": tp_of(k)}, device_id_type=MESH)
    for k in range(1, n_dp):
        pl.semaphore_signal(barrier, inc=1, device_id={"dp": dp_of(k)}, device_id_type=MESH)

    half = n_dp // 2
    core, chip = lax.rem(me, 2), me // 2
    partner = me + 1 - 2 * core
    chip_x = chip + 1 - 2 * lax.rem(chip, 2)
    chip_y = chip + 2 - 4 * (chip // 2)
    chip_d = half - 1 - chip

    PAIR, NODE, MID, SIDE, SLICE, ROW, PEER, SUM, SCATTER, ALONG, GATHER, MIX = range(12)

    def push(phase, source, target, **device):
        pltpu.make_async_remote_copy(
            src_ref=source,
            dst_ref=target,
            send_sem=sems.at[0, phase],
            recv_sem=sems.at[1, phase],
            device_id=device,
            device_id_type=MESH,
        ).start()

    def received(phase, ref):
        drain(ref, sems.at[1, phase])

    def exchange(axis, phase, source, target):
        size, other = (n_tp, tp_of) if axis == "tensor" else (n_dp, dp_of)
        for k in range(1, size):
            push(phase, source(other(k)), target, **{axis: other(k)})

    def exchange_all(phase, source, target):
        for j in sorted(range(n_tp), key=lambda j: -min(j, n_tp - j)):
            for k in range(n_dp):
                if (j, k) != (0, 0):
                    push(phase, source(dp_of(k), tp_of(j)), target, dp=dp_of(k), tensor=tp_of(j))

    def sides_of_rows(index, start, count):
        spans = [slice(start + h * count, start + (h + 1) * count) for h in range(2)]
        right = [dot_flip(tokens[index, span, width:], weights[:, width:]) for span in spans]
        left = [dot_flip(tokens[index, span, :width], weights[:, :width]) for span in spans]
        return [jnp.concatenate(pair, axis=1) for pair in zip(left, right)]

    def sides_of_chunk(index):
        drain(tokens.at[index], load_sem.at[chunk_loads[index]])
        return sides_of_rows(index, 0, mid)

    def sides_of_half(h):
        drain(tokens.at[0, h * mid : (h + 1) * mid], load_sem.at[half_loads[h]])
        zsend[h] = jnp.concatenate(sides_of_rows(0, h * mid, mid // 2), axis=0)

    drain(weights, load_sem.at[weight_load])
    sides_of_half(0)
    pl.semaphore_wait(barrier, n_dp + n_tp - 2)
    push(MID, zsend.at[0], zmid, tensor=near)
    for q in range(half):
        push(PAIR, prior_hbm.at[:, tile_of(2 * q + 1 - core)], pair_in.at[q], dp=partner)
    for k in range(1, n_dp):
        pl.semaphore_signal(ready_sem, inc=1, device_id={"dp": dp_of(k)}, device_id_type=MESH)
    sides_of_half(1)
    push(SIDE, zsend.at[1], zrecv.at[4], tensor=diagonal)
    far_sides = sides_of_chunk(1)
    zsend[3] = far_sides[1]
    push(SIDE, zsend.at[3], zrecv.at[3], tensor=far)
    zsend[4], zsend[5] = sides_of_chunk(2)
    push(SIDE, zsend.at[4:6], zrecv.at[0:2], tensor=near)

    drain(order_ref, load_sem.at[order_load])
    drain(prior, load_sem.at[prior_load])
    drain(mix_ref, load_sem.at[mix_load])
    received(PAIR, pair_in)
    first_mix, second_mix = mix_ref[:, :rows], mix_ref[:, rows:]
    own_first = order_ref[0, 2 * chip] == core
    own_half = [prior[:, tile_of(2 * q + core)] for q in range(half)]
    firsts = [jnp.where(own_first, own_half[q], pair_in[q]) for q in range(half)]
    seconds = [jnp.where(own_first, pair_in[q], own_half[q]) for q in range(half)]
    first_halves, second_halves = halves(first_mix), halves(second_mix)
    mixed = dot_halves(first_halves, halves(jnp.concatenate(firsts, axis=1)))
    mixed = mixed + dot_halves(second_halves, halves(jnp.concatenate(seconds, axis=1)))
    for q in range(half):
        node_send[q] = mixed[:, q * LANES : (q + 1) * LANES]
    for other in (chip_x, chip_y, chip_d):
        push(NODE, node_send.at[other], node_recv.at[chip], dp=2 * other + core)
    node_recv[chip] = node_send[chip]
    received(MID, zmid)
    zsend[2] = far_sides[0] + zmid[...]
    push(SIDE, zsend.at[2], zrecv.at[2], tensor=far)
    own_sides = sides_of_chunk(3)

    drain(fold_ref, load_sem.at[fold_load])
    fold_rows = fold_ref[...]

    def through(value):
        count = value.shape[0]
        both = stacked(value, (0, 1)).astype(jnp.bfloat16)
        high = value.astype(jnp.bfloat16)
        results = []
        for top, bottom in (first_halves, second_halves):
            most = dot_flip(both, top)
            results.append(most[:count] + (most[count:] + dot_flip(high, bottom)))
        return results

    paths = [[jnp.concatenate(through(fold_rows), axis=0)]]
    for level in range(1, levels):
        count = paths[-1][0].shape[0]
        mapped = through(jnp.concatenate(paths[-1], axis=0))
        paths.append([v[i : i + count] for v in mapped for i in range(0, v.shape[0], count)])
    paths = [[stacked(p, (0, 0, 1)).T.astype(jnp.bfloat16) for p in level] for level in paths]
    def total(value):
        return jnp.sum(jnp.sum(value, axis=0, keepdims=True), axis=1, keepdims=True)

    fold_gram = [
        [jnp.sum(fold_rows[e : e + 1] * fold_rows[k : k + 1], axis=1, keepdims=True) for k in range(n_tp)]
        for e in range(n_tp)
    ]
    crossed = dot_halves(halves(fold_rows), halves(prior[...]))
    crossed = [
        jnp.concatenate(
            [crossed[e : e + 1, tile * LANES : (tile + 1) * LANES] for tile in range(n_dp)], axis=0
        )
        for e in range(n_tp)
    ]
    prior_square = jnp.zeros((rows, LANES), f32)
    for tile in range(n_dp):
        part = prior[:, tile * LANES : (tile + 1) * LANES]
        prior_square = prior_square + part * part
    prior_mass = total(prior_square)

    received(SIDE, zrecv)
    sides = jnp.concatenate(
        [
            (own_sides[0] + zrecv[0]) + zrecv[2],
            (own_sides[1] + zrecv[1]) + (zrecv[3] + zrecv[4]),
        ],
        axis=0,
    )
    lane = lax.broadcasted_iota(jnp.int32, sides.shape, 1)
    doubled = jnp.where(lane < RANK, sides, pltpu.roll(sides, RANK, 1))
    product = dot_mid(sides.T, doubled) / jnp.sqrt(f32(SEQ))
    product = jnp.where(z < count_ref[0], product, jnp.zeros_like(product))
    full[...] = product[RANK:]
    even = full[pl.ds(0, RANK // 2, stride=2), :]
    odd = full[pl.ds(1, RANK // 2, stride=2), :]
    lane = lax.broadcasted_iota(jnp.int32, even.shape, 1)
    mine = jnp.where(lane < RANK, even, odd)
    for row in range(n_tp * n_dp):
        grads_rows[row] = mine[row : row + 1]
    for index in range(n_tp):
        slices_send[index] = mine[index * n_dp : (index + 1) * n_dp]
    grads[z] = slices_send[z]
    slot = me * n_tp + z
    grads_all[slot] = grads_rows[z * n_dp + me]
    pl.semaphore_wait(ready_sem, n_dp - 1)
    exchange("tensor", SLICE, lambda t: slices_send.at[t], grads.at[z])
    exchange_all(ROW, lambda d, t: grads_rows.at[t * n_dp + d], grads_all.at[slot])

    flags = [
        [order_ref[0, j * 2 ** (level + 1) + 2**level - 1] == 1 for j in range(n_dp >> (level + 1))]
        for level in range(levels)
    ]

    def pick(flip, lower, upper):
        first = [jnp.where(flip, b, a) for a, b in zip(lower, upper)]
        return first, [jnp.where(flip, a, b) for a, b in zip(lower, upper)]

    received(SLICE, grads.at[: n_tp - 1])
    steps = [grads[e] for e in range(n_tp)]
    growth = jnp.zeros((n_dp, LANES), f32)
    for e, step in enumerate(steps):
        slope = 2.0 * crossed[e]
        for other, weight in zip(steps, fold_gram[e]):
            slope = slope + weight * other
        growth = growth + step * slope
    own_mass = prior_mass + total(growth)

    received(NODE, node_recv.at[: half - 1])
    mixtures = [[[node_recv[j]] for j in range(half)]]
    for level in range(1, levels):
        below = mixtures[-1]
        sides_of = [pick(flags[level][j], below[2 * j], below[2 * j + 1]) for j in range(len(below) // 2)]
        count = len(below[0])
        left = dot_halves(first_halves, halves(jnp.concatenate([v for f, _ in sides_of for v in f], axis=1)))
        right = dot_halves(second_halves, halves(jnp.concatenate([v for _, g in sides_of for v in g], axis=1)))
        mixtures.append(
            [
                [
                    side[:, (j * count + i) * LANES : (j * count + i + 1) * LANES]
                    for side in (left, right)
                    for i in range(count)
                ]
                for j in range(len(sides_of))
            ]
        )

    for index, part in enumerate(mixtures[-1][0]):
        mix_send[index] = part
    push(MIX, mix_send, mix_recv, dp=partner)

    received(ROW, grads_all.at[: n_tp * n_dp - 1])
    push(PEER, grads_all, peer_all, dp=partner)

    def steps_from(rows_of):
        steps_of = [
            [jnp.concatenate([rows_of[r * n_tp + e] for e in range(n_tp)], axis=0)] for r in range(n_dp)
        ]
        return steps_of, jnp.concatenate([step[0] for step in steps_of], axis=0)

    def merge_steps(level, steps_of):
        merged_steps = []
        for j in range(len(steps_of) // 2):
            first, second = pick(flags[level][j], steps_of[2 * j], steps_of[2 * j + 1])
            if level == 0:
                merged_steps.append([jnp.concatenate([first[0], second[0]], axis=0)])
            else:
                merged_steps.append(first + second)
        return merged_steps

    def updates_of(level, merged_steps):
        return [
            jnp.dot(
                path,
                jnp.concatenate([stacked(g[i], (0, 1, 0)) for g in merged_steps], axis=1).astype(jnp.bfloat16),
                preferred_element_type=f32,
            )
            for i, path in enumerate(paths[level])
        ]

    steps_of, every = steps_from(grads_all)
    sums, products, nodes = [], [], []
    for level in range(levels):
        level_products, level_nodes = [], []
        merged_steps = merge_steps(level, steps_of)
        updates = updates_of(level, merged_steps)
        for j in range(len(merged_steps)):
            parts = [
                v + update[:, j * LANES : (j + 1) * LANES]
                for v, update in zip(mixtures[level][j], updates)
            ]
            index_of = {}
            for a in range(len(parts)):
                for b in range(a + 1):
                    index_of[a, b] = n_dp + len(sums)
                    sums.append(total(parts[a] * parts[b]))
            level_products.append(index_of)
            level_nodes.append(parts)
        steps_of = merged_steps
        products.append(level_products)
        nodes = level_nodes
    lane = lax.broadcasted_iota(jnp.int32, (1, LANES), 1)
    packed = jnp.where(lane == me, own_mass, jnp.zeros((1, LANES), f32))
    for index, value in enumerate(sums):
        packed = jnp.where(lane == n_dp + index, value, packed)
    sums_all[slot] = packed
    exchange_all(SUM, lambda d, t: sums_all.at[slot], sums_all.at[slot])
    for e, step in enumerate(steps):
        for tile in range(n_dp):
            grads_out[e : e + 1, tile * LANES : (tile + 1) * LANES] = step[tile : tile + 1]
    received(PEER, peer_all)
    received(MIX, mix_recv)
    steps_of, peer_every = steps_from(peer_all)
    for level in range(levels):
        steps_of = merge_steps(level, steps_of)
    peer_parts = [mix_recv[i] + update for i, update in enumerate(updates_of(levels - 1, steps_of))]
    every_halves = halves(jnp.concatenate([every, peer_every], axis=1))
    received(SUM, sums_all.at[: n_tp * n_dp - 1])
    parts_of = [sums_all[index] for index in range(n_tp * n_dp)]
    while len(parts_of) > 1:
        parts_of = [a + b for a, b in zip(parts_of[0::2], parts_of[1::2])]
    packed = parts_of[0]

    def summed(index):
        return jnp.sum(jnp.where(lane == index, packed, 0.0), axis=1, keepdims=True)

    masses = [summed(index) for index in range(n_dp)]
    scales = [[jnp.ones((1, 1), f32)] for _ in range(n_dp)]
    for level in range(levels):
        new_masses, new_scales = [], []
        for j, products_of in enumerate(products[level]):
            flip = flags[level][j]
            lower, upper = scales[2 * j], scales[2 * j + 1]
            if level == 0:
                coefs = [jnp.ones((1, 1), f32)]
            else:
                coefs = [jnp.where(flip, b, a) for a, b in zip(lower, upper)]
                coefs += [jnp.where(flip, a, b) for a, b in zip(lower, upper)]
            square = jnp.zeros((1, 1), f32)
            for (a, b), index in products_of.items():
                term = coefs[a] * (coefs[b] * summed(index))
                square = square + (term if a == b else 2.0 * term)
            mass = masses[2 * j] + masses[2 * j + 1]
            scale = jnp.sqrt(mass / (jnp.maximum(square, 0.0) + 1e-06))
            trace = scale * scale * square
            new_masses.append(mass)
            new_scales.append([scale * c for c in coefs])
        masses, scales = new_masses, new_scales
    chunks = []
    for parts in (nodes[0], peer_parts):
        chunk = scales[0][0] * parts[0]
        for c, part in zip(scales[0][1:], parts[1:]):
            chunk = chunk + c * part
        chunks.append(chunk)
    root[:, tile_of(me)] = chunks[0]
    root[:, tile_of(partner)] = chunks[1]

    chunk_halves = halves(jnp.concatenate(chunks, axis=1))
    upper_halves, lower_halves = [[v[s] for v in chunk_halves] for s in (slice(0, LANES), slice(LANES, rows))]
    targets = dot_flip_halves(every_halves, chunk_halves)
    unit = rows / trace
    triangle = jnp.concatenate(
        [
            dot_flip_halves(upper_halves, upper_halves),
            dot_flip_halves(lower_halves, upper_halves),
            dot_flip_halves(lower_halves, lower_halves),
        ],
        axis=0,
    )
    own_rows = gram_all.shape[1]
    for r in range(n_dp):
        gram_part[r, :own_rows] = unit * triangle[r * own_rows : (r + 1) * own_rows]
        own = targets[r * n_tp : (r + 1) * n_tp]
        gram_part[r, own_rows:] = unit * jnp.concatenate([own[:, :LANES], own[:, LANES:]], axis=0)
    gram_rs[chip] = gram_part[me]
    for other in (chip_d, chip_x, chip_y):
        push(SCATTER, gram_part.at[2 * other + core], gram_rs.at[chip], dp=2 * other + core)
    dev_x, dev_y, dev_d = (2 * other + core for other in (chip_x, chip_y, chip_d))
    upper, lower = pl.ds(0, rows // 2), pl.ds(rows // 2, rows // 2)

    def relay(index, owner, device, span=slice(None)):
        block_of = root.at[span, tile_of(owner)]
        pltpu.make_async_remote_copy(
            src_ref=block_of,
            dst_ref=block_of,
            send_sem=root_sems.at[5],
            recv_sem=root_sems.at[index],
            device_id={"dp": device},
            device_id_type=MESH,
        ).start()

    def relayed(index, count):
        drain(root.at[:, : count * LANES] if count else root.at[upper, :LANES], root_sems.at[index])

    drain(gram_rs.at[: half - 1], sems.at[0, SCATTER])
    relay(0, me, dev_x)
    relay(1, me, dev_y)
    received(SCATTER, gram_rs.at[: half - 1])
    part = gram_rs[0]
    for index in range(1, half):
        part = part + gram_rs[index]
    gram_z[z] = part
    exchange("tensor", ALONG, lambda t: gram_z.at[z], gram_z.at[z])
    relayed(0, 1)
    relay(2, dev_x, dev_y, upper)
    relay(4, dev_x, partner)
    relayed(1, 1)
    relay(3, dev_y, dev_x, lower)
    relay(4, dev_y, partner)
    received(ALONG, gram_z.at[: n_tp - 1])
    part = gram_z[0]
    for index in range(1, n_tp):
        part = part + gram_z[index]
    gram_all[me] = part[:own_rows]
    target = jnp.concatenate([part[own_rows : own_rows + n_tp], part[own_rows + n_tp :]], axis=1)
    exchange("dp", GATHER, lambda t: gram_all.at[me], gram_all.at[me])
    relayed(2, 0)
    relayed(3, 0)
    relay(4, dev_d, partner)
    for phase, ref in (
        (PAIR, pair_in),
        (NODE, node_recv.at[: half - 1]),
        (MID, zmid),
        (SIDE, zrecv),
        (SLICE, grads.at[: n_tp - 1]),
        (ROW, grads_all.at[: n_tp * n_dp - 1]),
        (SUM, sums_all.at[: n_tp * n_dp - 1]),
        (PEER, peer_all),
        (MIX, mix_recv),
        (ALONG, gram_z.at[: n_tp - 1]),
    ):
        drain(ref, sems.at[0, phase])
    received(GATHER, gram_all.at[: n_dp - 1])
    triangle = jnp.concatenate([gram_all[r] for r in range(n_dp)], axis=0)
    corner = triangle[LANES:rows]
    gram = jnp.concatenate(
        [
            jnp.concatenate([triangle[:LANES], corner.T], axis=1),
            jnp.concatenate([corner, triangle[rows : rows + LANES]], axis=1),
        ],
        axis=0,
    )
    solved_out[...] = solve(gram, target)
    drain(gram_all.at[: n_dp - 1], sems.at[0, GATHER])
    relayed(4, half - 1)
    root_write = pltpu.make_async_copy(root, root_out, out_sem.at[0])
    root_write.start()
    drain(root.at[:, : (n_dp - 2) * LANES], root_sems.at[5])
    root_write.wait()


def last_kernel(root_ref, solved_ref, grads_ref, root_out, pre_out, pre, sem):
    write = pltpu.make_async_copy(root_ref, root_out, sem.at[0])
    write.start()
    pre[...] = grads_ref[...] - dot_mid(solved_ref[...], root_ref[...])
    pre_write = pltpu.make_async_copy(pre, pre_out, sem.at[1])
    pre_write.start()
    write.wait()
    pre_write.wait()


def fused_body(
    activations,
    out_grads,
    input_proj,
    grad_proj,
    example_count,
    child_order,
    prior_sketch,
    fold_map,
    merge_mix,
):
    n_dp, n_tp = lax.axis_size("dp"), lax.axis_size("tensor")
    rows, columns = prior_sketch.shape
    slots = activations.shape[0] // SEQ
    f32, bf16 = jnp.float32, jnp.bfloat16
    width, hidden = activations.shape[1], out_grads.shape[1]
    hbm = pl.BlockSpec(memory_space=pltpu.HBM)
    anywhere = pl.BlockSpec(memory_space=pl.ANY)
    vmem = pl.BlockSpec(memory_space=pltpu.VMEM)
    smem = pl.BlockSpec(memory_space=pltpu.SMEM)
    devices = n_dp * n_tp
    own_rows = 3 * LANES // n_dp
    part_rows = own_rows + 2 * slots
    pin = functools.partial(pltpu.with_memory_space_constraint, memory_space=pltpu.HBM)
    root, solved, grads = pl.pallas_call(
        functools.partial(fused_kernel, n_dp, n_tp),
        out_shape=(
            jax.ShapeDtypeStruct((rows, columns), f32),
            jax.ShapeDtypeStruct((slots, rows), f32),
            jax.ShapeDtypeStruct((slots, columns), f32),
        ),
        in_specs=[hbm, hbm, hbm, hbm, smem, hbm, hbm, hbm, hbm],
        out_specs=(anywhere, vmem, vmem),
        scratch_shapes=[
            pltpu.VMEM((slots, SEQ, width + hidden), bf16),
            pltpu.VMEM((RANK, width + hidden), bf16),
            pltpu.SMEM((1, n_dp), jnp.int32),
            pltpu.VMEM((rows, columns), f32),
            pltpu.VMEM((slots, rows), f32),
            pltpu.VMEM((rows, 2 * rows), f32),
            pltpu.VMEM((n_dp // 2, rows, LANES), f32),
            pltpu.VMEM((n_dp // 2, rows, LANES), f32),
            pltpu.VMEM((n_dp // 2, rows, LANES), f32),
            pltpu.VMEM((6, SEQ // 2, LANES), f32),
            pltpu.VMEM((SEQ // 2, LANES), f32),
            pltpu.VMEM((5, SEQ // 2, LANES), f32),
            pltpu.VMEM((RANK, LANES), f32),
            pltpu.VMEM((n_tp, n_dp, LANES), f32),
            pltpu.VMEM((n_tp, n_dp, LANES), f32),
            pltpu.VMEM((devices, 1, LANES), f32),
            pltpu.VMEM((devices, 1, LANES), f32),
            pltpu.VMEM((devices, 1, LANES), f32),
            pltpu.VMEM((n_dp // 2, rows, LANES), f32),
            pltpu.VMEM((n_dp // 2, rows, LANES), f32),
            pltpu.VMEM((devices, 1, LANES), f32),
            pltpu.VMEM((rows, columns), f32),
            pltpu.VMEM((n_dp, part_rows, LANES), f32),
            pltpu.VMEM((n_dp // 2, part_rows, LANES), f32),
            pltpu.VMEM((n_tp, part_rows, LANES), f32),
            pltpu.VMEM((n_dp, own_rows, LANES), f32),
            pltpu.SemaphoreType.DMA((10,)),
            pltpu.SemaphoreType.DMA((2, 12)),
            pltpu.SemaphoreType.DMA((6,)),
            pltpu.SemaphoreType.DMA((1,)),
            pltpu.SemaphoreType.REGULAR,
        ],
        compiler_params=pltpu.CompilerParams(
            collective_id=0, has_side_effects=True, vmem_limit_bytes=32 * 2**20
        ),
    )(
        pin(activations),
        pin(out_grads),
        pin(input_proj.T),
        pin(grad_proj.T),
        example_count,
        pin(child_order.reshape(1, n_dp)),
        pin(prior_sketch),
        pin(fold_map.T),
        pin(merge_mix),
    )
    return pl.pallas_call(
        last_kernel,
        out_shape=(
            jax.ShapeDtypeStruct((rows, columns), f32),
            jax.ShapeDtypeStruct((slots, columns), f32),
        ),
        in_specs=[vmem] * 3,
        out_specs=(anywhere, anywhere),
        scratch_shapes=[pltpu.VMEM((slots, columns), f32), pltpu.SemaphoreType.DMA((2,))],
        compiler_params=pltpu.CompilerParams(vmem_limit_bytes=16 * 2**20),
    )(root, solved, grads)


def from_partner(value, axis, stride):
    mask = 2**stride
    pairs = [(source, source ^ mask) for source in range(lax.axis_size(axis))]
    return lax.ppermute(value, axis, pairs)


def body(
    activations,
    out_grads,
    input_proj,
    grad_proj,
    example_count,
    child_order,
    prior_sketch,
    fold_map,
    merge_mix,
):
    tensor_count = lax.axis_size("tensor")
    own_rank = RANK // tensor_count
    example_slots = activations.shape[0] // SEQ
    sketch_rows = prior_sketch.shape[0]
    input_part = jnp.dot(activations, input_proj, preferred_element_type=jnp.float32)
    grad_part = jnp.dot(out_grads, grad_proj, preferred_element_type=jnp.float32)
    input_side, grad_side = lax.psum((input_part, grad_part), "tensor")
    grad_own = lax.dynamic_slice_in_dim(grad_side, lax.axis_index("tensor") * own_rank, own_rank, 1)
    grad_blocks = grad_own.reshape(example_slots, SEQ, own_rank)
    input_blocks = input_side.reshape(example_slots, SEQ, RANK)
    example_grad = jnp.einsum(
        "eta,etb->eab", grad_blocks, input_blocks, precision=lax.Precision.HIGHEST
    )
    example_grad = example_grad.reshape(example_slots, own_rank * RANK) / jnp.sqrt(jnp.float32(SEQ))
    live = jnp.arange(example_slots, dtype=jnp.int32) < example_count[0]
    example_grad = jnp.where(live[:, None], example_grad, jnp.zeros_like(example_grad))
    leaf_node = prior_sketch + jnp.dot(fold_map, example_grad, precision=lax.Precision.HIGHEST)
    leaf_weight = lax.psum(jnp.sum(leaf_node * leaf_node), "tensor")
    mix_first = merge_mix[:, :sketch_rows]
    mix_second = merge_mix[:, sketch_rows:]
    depth_count = lax.axis_size("dp").bit_length() - 1
    rank_index = lax.axis_index("dp")
    sketch_node = leaf_node
    sketch_weight = leaf_weight
    for level_index in range(depth_count):
        sibling_node, sibling_weight = from_partner((sketch_node, sketch_weight), "dp", level_index)
        upper_half = rank_index >> level_index & 1
        block_start = rank_index >> level_index + 1 << level_index + 1
        flip_order = child_order[block_start + (1 << level_index) - 1]
        own_first = upper_half == flip_order
        first = jnp.where(own_first, sketch_node, sibling_node)
        second = jnp.where(own_first, sibling_node, sketch_node)
        first_weight = jnp.where(own_first, sketch_weight, sibling_weight)
        second_weight = jnp.where(own_first, sibling_weight, sketch_weight)
        mixture = jnp.dot(mix_first, first, precision=lax.Precision.HIGHEST) + jnp.dot(
            mix_second, second, precision=lax.Precision.HIGHEST
        )
        mix_total = lax.psum(jnp.sum(mixture * mixture), "tensor")
        sketch_weight = first_weight + second_weight
        sketch_node = mixture * jnp.sqrt(sketch_weight / (mix_total + 1e-06))
    gram_part = jnp.dot(sketch_node, sketch_node.T, precision=lax.Precision.HIGHEST)
    product_part = jnp.dot(sketch_node, example_grad.T, precision=lax.Precision.HIGHEST)
    gram, sketch_grad = lax.psum((gram_part, product_part), "tensor")
    damping = jnp.trace(gram) / sketch_rows
    system = gram + damping * jnp.eye(sketch_rows, dtype=jnp.float32)
    factor = jnp.linalg.cholesky(system)
    solved = jax.scipy.linalg.cho_solve((factor, True), sketch_grad)
    preconditioned = example_grad - jnp.dot(solved.T, sketch_node, precision=lax.Precision.HIGHEST)
    return (sketch_node, preconditioned)


def fits_fused(rows, columns, slots, n_dp, n_tp):
    return (
        columns == n_dp * LANES
        and slots == n_tp
        and 2 * RANK == LANES
        and n_dp == 8
        and n_tp == 4
        and rows == 2 * LANES
    )


def step(*args):
    n_dp, n_tp = lax.axis_size("dp"), lax.axis_size("tensor")
    slots = args[0].shape[0] // SEQ
    rows, columns = args[6].shape
    if fits_fused(rows, columns, slots, n_dp, n_tp):
        return fused_body(*args)
    return body(*args)


def solution(mesh):
    in_specs = (
        P("dp", "tensor"),
        P("dp", "tensor"),
        P("tensor", None),
        P("tensor", None),
        P("dp"),
        P(),
        P("dp", "tensor"),
        P(),
        P(),
    )
    out_specs = (P(None, "tensor"), P("dp", "tensor"))
    return jax.shard_map(step, mesh=mesh, in_specs=in_specs, out_specs=out_specs, check_vma=False)
```

```python
import functools

import jax
import jax.numpy as jnp
from jax import lax
from jax.experimental import pallas as pl
from jax.experimental.pallas import tpu as pltpu
from jax.sharding import PartitionSpec as P

RANK = 64
SEQ = 128
LANES = 128
HIGHEST = lax.Precision.HIGHEST
MESH = pl.DeviceIdType.MESH


def newton_plan(rows):
    low, high = 0.999, (rows + 1) * 1.001
    first = 2.0 / (low + high)
    reach, scales = first * low, []
    while 1.0 - reach > 1e-3:
        grown = reach * (2.0 - reach)
        scale = 2.0 / (1.0 + grown)
        scales.append(scale)
        reach = grown * scale
    return first, scales


def dot_high(left, right):
    return jnp.dot(left, right, precision=HIGHEST, preferred_element_type=jnp.float32)


def dot_flip(left, right):
    return lax.dot_general(left, right, (((1,), (1,)), ((), ())), preferred_element_type=jnp.float32)


def halves(value):
    high = value.astype(jnp.bfloat16)
    return high, (value - high.astype(jnp.float32)).astype(jnp.bfloat16)


def dot_halves(left, right):
    (a, b), (c, d) = left, right
    out = jnp.dot(a, c, preferred_element_type=jnp.float32)
    out = out + jnp.dot(a, d, preferred_element_type=jnp.float32)
    return out + jnp.dot(b, c, preferred_element_type=jnp.float32)


def dot_mid(left, right):
    return dot_halves(halves(left), halves(right))


def dot_flip_halves(left, right):
    (a, b), (c, d) = left, right
    return dot_flip(jnp.concatenate([a, a, b], axis=1), jnp.concatenate([c, d, c], axis=1))


def dot_rows_halved(left, right):
    (a, b), (c, d) = left, right
    left = jnp.concatenate([a, a, b], axis=1)
    right = jnp.concatenate([c, d, c], axis=0)
    half = left.shape[0] // 2
    return jnp.concatenate(
        [
            jnp.dot(left[:half], right, preferred_element_type=jnp.float32),
            jnp.dot(left[half:], right, preferred_element_type=jnp.float32),
        ],
        axis=0,
    )


def thirds(value):
    high = value.astype(jnp.bfloat16)
    return (high, *halves(value - high.astype(jnp.float32)))


def dot_thirds(left, right):
    count = left.shape[0]
    stack = jnp.concatenate(thirds(left), axis=0)
    a, b, c = (jnp.dot(stack, part, preferred_element_type=jnp.float32) for part in thirds(right))
    high = a[count : 2 * count] + b[:count]
    low = (a[2 * count :] + b[count : 2 * count]) + c[:count]
    return a[:count] + (high + low)


def stacked(value, order):
    high = value.astype(jnp.bfloat16).astype(jnp.float32)
    both = (high, value - high)
    return jnp.concatenate([both[i] for i in order], axis=0)


def solve(gram, target):
    rows = gram.shape[0]
    eye = lax.broadcasted_iota(jnp.int32, gram.shape, 0) == lax.broadcasted_iota(jnp.int32, gram.shape, 1)
    system = gram + jnp.where(eye, 1.0, 0.0)
    first, scales = newton_plan(rows)
    state, solved, path = first * system, first * target, None
    for index, scale in enumerate(scales):
        factor = jnp.where(eye, 2.0 * scale, 0.0) - scale * state
        factor_halves = halves(factor)
        solved = dot_halves(halves(solved), factor_halves)
        if index < len(scales) - 1:
            state = dot_rows_halved(halves(state), factor_halves)
            if path is None:
                path = factor_halves[0]
            else:
                path = jnp.dot(path, factor_halves[0], preferred_element_type=jnp.float32)
                path = path.astype(jnp.bfloat16)
    rest = (first * (target - dot_thirds(solved, system))).astype(jnp.bfloat16)
    step = jnp.dot(rest, path, preferred_element_type=jnp.float32)
    return solved + dot_halves(halves(step), factor_halves)


def fused_kernel(
    n_dp,
    n_tp,
    act_hbm,
    out_hbm,
    wi_hbm,
    wo_hbm,
    count_ref,
    order_hbm,
    prior_hbm,
    fold_hbm,
    mix_hbm,
    root_out,
    solved_out,
    grads_out,
    tokens,
    weights,
    order_ref,
    prior,
    fold_ref,
    mix_ref,
    pair_in,
    node_send,
    node_recv,
    zsend,
    zmid,
    zrecv,
    full,
    slices_send,
    grads,
    grads_rows,
    grads_all,
    peer_all,
    mix_send,
    mix_recv,
    sums_all,
    root,
    gram_part,
    gram_rs,
    gram_z,
    gram_all,
    load_sem,
    sems,
    root_sems,
    out_sem,
    ready_sem,
):
    f32 = jnp.float32
    me, z = lax.axis_index("dp"), lax.axis_index("tensor")
    rows = prior.shape[0]
    levels = n_dp.bit_length() - 1

    def dp_of(k):
        return lax.rem(me + k, n_dp)

    def tp_of(k):
        return lax.rem(z + k, n_tp)

    width = act_hbm.shape[1]
    near = z + 1 - 2 * lax.rem(z, 2)
    far = z + 2 - 4 * (z // 2)
    diagonal = near + 2 - 4 * (near // 2)
    order = (diagonal, far, near, z)
    used = []

    def load(*pairs):
        for source, target in pairs:
            pltpu.make_async_copy(source, target, load_sem.at[len(used)]).start()
        used.append(None)
        return len(used) - 1

    def drain(ref, sem):
        pltpu.make_async_copy(ref, ref, sem).wait()

    def load_chunk(index, start=0, count=SEQ):
        span = pl.ds(pl.multiple_of(order[index] * SEQ + start, count), count)
        into = tokens.at[index, start : start + count]
        return load((act_hbm.at[span], into.at[:, :width]), (out_hbm.at[span], into.at[:, width:]))

    order_load = load((order_hbm, order_ref))
    weight_load = load((wi_hbm, weights.at[:, :width]), (wo_hbm, weights.at[:, width:]))
    mid = SEQ // 2
    half_loads = [load_chunk(0, start, mid) for start in (0, mid)]
    prior_load = load((prior_hbm, prior))
    mix_load = load((mix_hbm, mix_ref))
    chunk_loads = [None] + [load_chunk(index) for index in range(1, n_tp)]
    fold_load = load((fold_hbm, fold_ref))

    def tile_of(owner):
        return pl.ds(pl.multiple_of(owner * LANES, LANES), LANES)

    barrier = pltpu.get_barrier_semaphore()
    for k in range(1, n_tp):
        pl.semaphore_signal(barrier, inc=1, device_id={"tensor": tp_of(k)}, device_id_type=MESH)
    for k in range(1, n_dp):
        pl.semaphore_signal(barrier, inc=1, device_id={"dp": dp_of(k)}, device_id_type=MESH)

    half = n_dp // 2
    core, chip = lax.rem(me, 2), me // 2
    partner = me + 1 - 2 * core
    chip_x = chip + 1 - 2 * lax.rem(chip, 2)
    chip_y = chip + 2 - 4 * (chip // 2)
    chip_d = half - 1 - chip

    PAIR, NODE, MID, SIDE, SLICE, ROW, PEER, SUM, SCATTER, ALONG, GATHER, MIX = range(12)

    def push(phase, source, target, **device):
        pltpu.make_async_remote_copy(
            src_ref=source,
            dst_ref=target,
            send_sem=sems.at[0, phase],
            recv_sem=sems.at[1, phase],
            device_id=device,
            device_id_type=MESH,
        ).start()

    def received(phase, ref):
        drain(ref, sems.at[1, phase])

    z_peers = (diagonal, far, near)
    dp_peers = [2 * other + side for other in (chip_d, chip_x, chip_y) for side in (core, 1 - core)]
    dp_peers.append(partner)

    def exchange(axis, phase, source, target):
        for other in z_peers if axis == "tensor" else dp_peers:
            push(phase, source(other), target, **{axis: other})

    def exchange_all(phase, source, target):
        for t in (*z_peers, z):
            for d in (*dp_peers, me):
                if t is not z or d is not me:
                    push(phase, source(d, t), target, dp=d, tensor=t)

    def sides_of_rows(index, start, count):
        spans = [slice(start + h * count, start + (h + 1) * count) for h in range(2)]
        right = [dot_flip(tokens[index, span, width:], weights[:, width:]) for span in spans]
        left = [dot_flip(tokens[index, span, :width], weights[:, :width]) for span in spans]
        return [jnp.concatenate(pair, axis=1) for pair in zip(left, right)]

    def sides_of_chunk(index):
        drain(tokens.at[index], load_sem.at[chunk_loads[index]])
        return sides_of_rows(index, 0, mid)

    def sides_of_half(h):
        drain(tokens.at[0, h * mid : (h + 1) * mid], load_sem.at[half_loads[h]])
        zsend[h] = jnp.concatenate(sides_of_rows(0, h * mid, mid // 2), axis=0)

    drain(weights, load_sem.at[weight_load])
    sides_of_half(0)
    pl.semaphore_wait(barrier, n_dp + n_tp - 2)
    push(MID, zsend.at[0], zmid, tensor=near)
    for q in range(half):
        push(PAIR, prior_hbm.at[:, tile_of(2 * q + 1 - core)], pair_in.at[q], dp=partner)
    for k in range(1, n_dp):
        pl.semaphore_signal(ready_sem, inc=1, device_id={"dp": dp_of(k)}, device_id_type=MESH)
    sides_of_half(1)
    push(SIDE, zsend.at[1], zrecv.at[4], tensor=diagonal)
    far_sides = sides_of_chunk(1)
    zsend[3] = far_sides[1]
    push(SIDE, zsend.at[3], zrecv.at[3], tensor=far)
    zsend[4], zsend[5] = sides_of_chunk(2)
    push(SIDE, zsend.at[4:6], zrecv.at[0:2], tensor=near)

    drain(order_ref, load_sem.at[order_load])
    drain(prior, load_sem.at[prior_load])
    drain(mix_ref, load_sem.at[mix_load])
    received(PAIR, pair_in)
    first_mix, second_mix = mix_ref[:, :rows], mix_ref[:, rows:]
    own_first = order_ref[0, 2 * chip] == core
    own_half = [prior[:, tile_of(2 * q + core)] for q in range(half)]
    firsts = [jnp.where(own_first, own_half[q], pair_in[q]) for q in range(half)]
    seconds = [jnp.where(own_first, pair_in[q], own_half[q]) for q in range(half)]
    first_halves, second_halves = halves(first_mix), halves(second_mix)
    mixed = dot_halves(first_halves, halves(jnp.concatenate(firsts, axis=1)))
    mixed = mixed + dot_halves(second_halves, halves(jnp.concatenate(seconds, axis=1)))
    for q in range(half):
        node_send[q] = mixed[:, q * LANES : (q + 1) * LANES]
    for other in (chip_x, chip_y, chip_d):
        push(NODE, node_send.at[other], node_recv.at[chip], dp=2 * other + core)
    node_recv[chip] = node_send[chip]
    received(MID, zmid)
    zsend[2] = far_sides[0] + zmid[...]
    push(SIDE, zsend.at[2], zrecv.at[2], tensor=far)
    own_sides = sides_of_chunk(3)

    drain(fold_ref, load_sem.at[fold_load])
    fold_rows = fold_ref[...]

    def through(value):
        count = value.shape[0]
        both = stacked(value, (0, 1)).astype(jnp.bfloat16)
        high = value.astype(jnp.bfloat16)
        results = []
        for top, bottom in (first_halves, second_halves):
            most = dot_flip(both, top)
            results.append(most[:count] + (most[count:] + dot_flip(high, bottom)))
        return results

    paths = [[jnp.concatenate(through(fold_rows), axis=0)]]
    for level in range(1, levels):
        count = paths[-1][0].shape[0]
        mapped = through(jnp.concatenate(paths[-1], axis=0))
        paths.append([v[i : i + count] for v in mapped for i in range(0, v.shape[0], count)])
    paths = [[stacked(p, (0, 0, 1)).T.astype(jnp.bfloat16) for p in level] for level in paths]
    def total(value):
        return jnp.sum(jnp.sum(value, axis=0, keepdims=True), axis=1, keepdims=True)

    fold_gram = [
        [jnp.sum(fold_rows[e : e + 1] * fold_rows[k : k + 1], axis=1, keepdims=True) for k in range(n_tp)]
        for e in range(n_tp)
    ]
    crossed = dot_halves(halves(fold_rows), halves(prior[...]))
    crossed = [
        jnp.concatenate(
            [crossed[e : e + 1, tile * LANES : (tile + 1) * LANES] for tile in range(n_dp)], axis=0
        )
        for e in range(n_tp)
    ]
    prior_square = jnp.zeros((rows, LANES), f32)
    for tile in range(n_dp):
        part = prior[:, tile * LANES : (tile + 1) * LANES]
        prior_square = prior_square + part * part
    prior_mass = total(prior_square)

    received(SIDE, zrecv)
    sides = jnp.concatenate(
        [
            (own_sides[0] + zrecv[0]) + zrecv[2],
            (own_sides[1] + zrecv[1]) + (zrecv[3] + zrecv[4]),
        ],
        axis=0,
    )
    lane = lax.broadcasted_iota(jnp.int32, sides.shape, 1)
    doubled = jnp.where(lane < RANK, sides, pltpu.roll(sides, RANK, 1))
    product = dot_mid(sides.T, doubled) / jnp.sqrt(f32(SEQ))
    product = jnp.where(z < count_ref[0], product, jnp.zeros_like(product))
    full[...] = product[RANK:]
    even = full[pl.ds(0, RANK // 2, stride=2), :]
    odd = full[pl.ds(1, RANK // 2, stride=2), :]
    lane = lax.broadcasted_iota(jnp.int32, even.shape, 1)
    mine = jnp.where(lane < RANK, even, odd)
    for row in range(n_tp * n_dp):
        grads_rows[row] = mine[row : row + 1]
    for index in range(n_tp):
        slices_send[index] = mine[index * n_dp : (index + 1) * n_dp]
    grads[z] = slices_send[z]
    slot = me * n_tp + z
    grads_all[slot] = grads_rows[z * n_dp + me]
    pl.semaphore_wait(ready_sem, n_dp - 1)
    exchange("tensor", SLICE, lambda t: slices_send.at[t], grads.at[z])
    exchange_all(ROW, lambda d, t: grads_rows.at[t * n_dp + d], grads_all.at[slot])

    flags = [
        [order_ref[0, j * 2 ** (level + 1) + 2**level - 1] == 1 for j in range(n_dp >> (level + 1))]
        for level in range(levels)
    ]

    def pick(flip, lower, upper):
        first = [jnp.where(flip, b, a) for a, b in zip(lower, upper)]
        return first, [jnp.where(flip, a, b) for a, b in zip(lower, upper)]

    received(SLICE, grads.at[: n_tp - 1])
    steps = [grads[e] for e in range(n_tp)]
    growth = jnp.zeros((n_dp, LANES), f32)
    for e, step in enumerate(steps):
        slope = 2.0 * crossed[e]
        for other, weight in zip(steps, fold_gram[e]):
            slope = slope + weight * other
        growth = growth + step * slope
    own_mass = prior_mass + total(growth)

    received(NODE, node_recv.at[: half - 1])
    mixtures = [[[node_recv[j]] for j in range(half)]]
    for level in range(1, levels):
        below = mixtures[-1]
        sides_of = [pick(flags[level][j], below[2 * j], below[2 * j + 1]) for j in range(len(below) // 2)]
        count = len(below[0])
        left = dot_halves(first_halves, halves(jnp.concatenate([v for f, _ in sides_of for v in f], axis=1)))
        right = dot_halves(second_halves, halves(jnp.concatenate([v for _, g in sides_of for v in g], axis=1)))
        mixtures.append(
            [
                [
                    side[:, (j * count + i) * LANES : (j * count + i + 1) * LANES]
                    for side in (left, right)
                    for i in range(count)
                ]
                for j in range(len(sides_of))
            ]
        )

    for index, part in enumerate(mixtures[-1][0]):
        mix_send[index] = part
    push(MIX, mix_send, mix_recv, dp=partner)

    received(ROW, grads_all.at[: n_tp * n_dp - 1])
    push(PEER, grads_all, peer_all, dp=partner)

    def steps_from(rows_of):
        steps_of = [
            [jnp.concatenate([rows_of[r * n_tp + e] for e in range(n_tp)], axis=0)] for r in range(n_dp)
        ]
        return steps_of, jnp.concatenate([step[0] for step in steps_of], axis=0)

    def merge_steps(level, steps_of):
        merged_steps = []
        for j in range(len(steps_of) // 2):
            first, second = pick(flags[level][j], steps_of[2 * j], steps_of[2 * j + 1])
            if level == 0:
                merged_steps.append([jnp.concatenate([first[0], second[0]], axis=0)])
            else:
                merged_steps.append(first + second)
        return merged_steps

    def updates_of(level, merged_steps):
        return [
            jnp.dot(
                path,
                jnp.concatenate([stacked(g[i], (0, 1, 0)) for g in merged_steps], axis=1).astype(jnp.bfloat16),
                preferred_element_type=f32,
            )
            for i, path in enumerate(paths[level])
        ]

    steps_of, every = steps_from(grads_all)
    sums, products, nodes = [], [], []
    for level in range(levels):
        level_products, level_nodes = [], []
        merged_steps = merge_steps(level, steps_of)
        updates = updates_of(level, merged_steps)
        for j in range(len(merged_steps)):
            parts = [
                v + update[:, j * LANES : (j + 1) * LANES]
                for v, update in zip(mixtures[level][j], updates)
            ]
            index_of = {}
            for a in range(len(parts)):
                for b in range(a + 1):
                    index_of[a, b] = n_dp + len(sums)
                    sums.append(total(parts[a] * parts[b]))
            level_products.append(index_of)
            level_nodes.append(parts)
        steps_of = merged_steps
        products.append(level_products)
        nodes = level_nodes
    lane = lax.broadcasted_iota(jnp.int32, (1, LANES), 1)
    packed = jnp.where(lane == me, own_mass, jnp.zeros((1, LANES), f32))
    for index, value in enumerate(sums):
        packed = jnp.where(lane == n_dp + index, value, packed)
    sums_all[slot] = packed
    exchange_all(SUM, lambda d, t: sums_all.at[slot], sums_all.at[slot])
    for e, step in enumerate(steps):
        for tile in range(n_dp):
            grads_out[e : e + 1, tile * LANES : (tile + 1) * LANES] = step[tile : tile + 1]
    received(PEER, peer_all)
    received(MIX, mix_recv)
    steps_of, peer_every = steps_from(peer_all)
    for level in range(levels):
        steps_of = merge_steps(level, steps_of)
    peer_parts = [mix_recv[i] + update for i, update in enumerate(updates_of(levels - 1, steps_of))]
    every_halves = halves(jnp.concatenate([every, peer_every], axis=1))
    received(SUM, sums_all.at[: n_tp * n_dp - 1])
    parts_of = [sums_all[index] for index in range(n_tp * n_dp)]
    while len(parts_of) > 1:
        parts_of = [a + b for a, b in zip(parts_of[0::2], parts_of[1::2])]
    packed = parts_of[0]

    def summed(index):
        return jnp.sum(jnp.where(lane == index, packed, 0.0), axis=1, keepdims=True)

    masses = [summed(index) for index in range(n_dp)]
    scales = [[jnp.ones((1, 1), f32)] for _ in range(n_dp)]
    for level in range(levels):
        new_masses, new_scales = [], []
        for j, products_of in enumerate(products[level]):
            flip = flags[level][j]
            lower, upper = scales[2 * j], scales[2 * j + 1]
            if level == 0:
                coefs = [jnp.ones((1, 1), f32)]
            else:
                coefs = [jnp.where(flip, b, a) for a, b in zip(lower, upper)]
                coefs += [jnp.where(flip, a, b) for a, b in zip(lower, upper)]
            square = jnp.zeros((1, 1), f32)
            for (a, b), index in products_of.items():
                term = coefs[a] * (coefs[b] * summed(index))
                square = square + (term if a == b else 2.0 * term)
            mass = masses[2 * j] + masses[2 * j + 1]
            scale = jnp.sqrt(mass / (jnp.maximum(square, 0.0) + 1e-06))
            trace = scale * scale * square
            new_masses.append(mass)
            new_scales.append([scale * c for c in coefs])
        masses, scales = new_masses, new_scales
    chunks = []
    for parts in (nodes[0], peer_parts):
        chunk = scales[0][0] * parts[0]
        for c, part in zip(scales[0][1:], parts[1:]):
            chunk = chunk + c * part
        chunks.append(chunk)
    root[:, tile_of(me)] = chunks[0]
    root[:, tile_of(partner)] = chunks[1]

    chunk_halves = halves(jnp.concatenate(chunks, axis=1))
    upper_halves, lower_halves = [[v[s] for v in chunk_halves] for s in (slice(0, LANES), slice(LANES, rows))]
    targets = dot_flip_halves(every_halves, chunk_halves)
    unit = rows / trace
    triangle = jnp.concatenate(
        [
            dot_flip_halves(upper_halves, upper_halves),
            dot_flip_halves(lower_halves, upper_halves),
            dot_flip_halves(lower_halves, lower_halves),
        ],
        axis=0,
    )
    own_rows = gram_all.shape[1]
    for r in range(n_dp):
        gram_part[r, :own_rows] = unit * triangle[r * own_rows : (r + 1) * own_rows]
        own = targets[r * n_tp : (r + 1) * n_tp]
        gram_part[r, own_rows:] = unit * jnp.concatenate([own[:, :LANES], own[:, LANES:]], axis=0)
    gram_rs[chip] = gram_part[me]
    for other in (chip_d, chip_x, chip_y):
        push(SCATTER, gram_part.at[2 * other + core], gram_rs.at[chip], dp=2 * other + core)
    dev_x, dev_y, dev_d = (2 * other + core for other in (chip_x, chip_y, chip_d))
    upper, lower = pl.ds(0, rows // 2), pl.ds(rows // 2, rows // 2)

    def relay(index, owner, device, span=slice(None)):
        block_of = root.at[span, tile_of(owner)]
        pltpu.make_async_remote_copy(
            src_ref=block_of,
            dst_ref=block_of,
            send_sem=root_sems.at[5],
            recv_sem=root_sems.at[index],
            device_id={"dp": device},
            device_id_type=MESH,
        ).start()

    def relayed(index, count):
        drain(root.at[:, : count * LANES] if count else root.at[upper, :LANES], root_sems.at[index])

    drain(gram_rs.at[: half - 1], sems.at[0, SCATTER])
    relay(0, me, dev_x)
    relay(1, me, dev_y)
    received(SCATTER, gram_rs.at[: half - 1])
    part = gram_rs[0]
    for index in range(1, half):
        part = part + gram_rs[index]
    gram_z[z] = part
    exchange("tensor", ALONG, lambda t: gram_z.at[z], gram_z.at[z])
    relayed(0, 1)
    relay(2, dev_x, dev_y, upper)
    relay(4, dev_x, partner)
    relayed(1, 1)
    relay(3, dev_y, dev_x, lower)
    relay(4, dev_y, partner)
    received(ALONG, gram_z.at[: n_tp - 1])
    part = gram_z[0]
    for index in range(1, n_tp):
        part = part + gram_z[index]
    gram_all[me] = part[:own_rows]
    target = jnp.concatenate([part[own_rows : own_rows + n_tp], part[own_rows + n_tp :]], axis=1)
    exchange("dp", GATHER, lambda t: gram_all.at[me], gram_all.at[me])
    relayed(2, 0)
    relayed(3, 0)
    relay(4, dev_d, partner)
    for phase, ref in (
        (PAIR, pair_in),
        (NODE, node_recv.at[: half - 1]),
        (MID, zmid),
        (SIDE, zrecv),
        (SLICE, grads.at[: n_tp - 1]),
        (ROW, grads_all.at[: n_tp * n_dp - 1]),
        (SUM, sums_all.at[: n_tp * n_dp - 1]),
        (PEER, peer_all),
        (MIX, mix_recv),
        (ALONG, gram_z.at[: n_tp - 1]),
    ):
        drain(ref, sems.at[0, phase])
    received(GATHER, gram_all.at[: n_dp - 1])
    triangle = jnp.concatenate([gram_all[r] for r in range(n_dp)], axis=0)
    corner = triangle[LANES:rows]
    gram = jnp.concatenate(
        [
            jnp.concatenate([triangle[:LANES], corner.T], axis=1),
            jnp.concatenate([corner, triangle[rows : rows + LANES]], axis=1),
        ],
        axis=0,
    )
    solved_out[...] = solve(gram, target)
    drain(gram_all.at[: n_dp - 1], sems.at[0, GATHER])
    relayed(4, half - 1)
    root_write = pltpu.make_async_copy(root, root_out, out_sem.at[0])
    root_write.start()
    drain(root.at[:, : (n_dp - 2) * LANES], root_sems.at[5])
    root_write.wait()


def last_kernel(root_ref, solved_ref, grads_ref, root_out, pre_out, pre, sem):
    write = pltpu.make_async_copy(root_ref, root_out, sem.at[0])
    write.start()
    pre[...] = grads_ref[...] - dot_mid(solved_ref[...], root_ref[...])
    pre_write = pltpu.make_async_copy(pre, pre_out, sem.at[1])
    pre_write.start()
    write.wait()
    pre_write.wait()


def fused_body(
    activations,
    out_grads,
    input_proj,
    grad_proj,
    example_count,
    child_order,
    prior_sketch,
    fold_map,
    merge_mix,
):
    n_dp, n_tp = lax.axis_size("dp"), lax.axis_size("tensor")
    rows, columns = prior_sketch.shape
    slots = activations.shape[0] // SEQ
    f32, bf16 = jnp.float32, jnp.bfloat16
    width, hidden = activations.shape[1], out_grads.shape[1]
    hbm = pl.BlockSpec(memory_space=pltpu.HBM)
    anywhere = pl.BlockSpec(memory_space=pl.ANY)
    vmem = pl.BlockSpec(memory_space=pltpu.VMEM)
    smem = pl.BlockSpec(memory_space=pltpu.SMEM)
    devices = n_dp * n_tp
    own_rows = 3 * LANES // n_dp
    part_rows = own_rows + 2 * slots
    pin = functools.partial(pltpu.with_memory_space_constraint, memory_space=pltpu.HBM)
    root, solved, grads = pl.pallas_call(
        functools.partial(fused_kernel, n_dp, n_tp),
        out_shape=(
            jax.ShapeDtypeStruct((rows, columns), f32),
            jax.ShapeDtypeStruct((slots, rows), f32),
            jax.ShapeDtypeStruct((slots, columns), f32),
        ),
        in_specs=[hbm, hbm, hbm, hbm, smem, hbm, hbm, hbm, hbm],
        out_specs=(anywhere, vmem, vmem),
        scratch_shapes=[
            pltpu.VMEM((slots, SEQ, width + hidden), bf16),
            pltpu.VMEM((RANK, width + hidden), bf16),
            pltpu.SMEM((1, n_dp), jnp.int32),
            pltpu.VMEM((rows, columns), f32),
            pltpu.VMEM((slots, rows), f32),
            pltpu.VMEM((rows, 2 * rows), f32),
            pltpu.VMEM((n_dp // 2, rows, LANES), f32),
            pltpu.VMEM((n_dp // 2, rows, LANES), f32),
            pltpu.VMEM((n_dp // 2, rows, LANES), f32),
            pltpu.VMEM((6, SEQ // 2, LANES), f32),
            pltpu.VMEM((SEQ // 2, LANES), f32),
            pltpu.VMEM((5, SEQ // 2, LANES), f32),
            pltpu.VMEM((RANK, LANES), f32),
            pltpu.VMEM((n_tp, n_dp, LANES), f32),
            pltpu.VMEM((n_tp, n_dp, LANES), f32),
            pltpu.VMEM((devices, 1, LANES), f32),
            pltpu.VMEM((devices, 1, LANES), f32),
            pltpu.VMEM((devices, 1, LANES), f32),
            pltpu.VMEM((n_dp // 2, rows, LANES), f32),
            pltpu.VMEM((n_dp // 2, rows, LANES), f32),
            pltpu.VMEM((devices, 1, LANES), f32),
            pltpu.VMEM((rows, columns), f32),
            pltpu.VMEM((n_dp, part_rows, LANES), f32),
            pltpu.VMEM((n_dp // 2, part_rows, LANES), f32),
            pltpu.VMEM((n_tp, part_rows, LANES), f32),
            pltpu.VMEM((n_dp, own_rows, LANES), f32),
            pltpu.SemaphoreType.DMA((10,)),
            pltpu.SemaphoreType.DMA((2, 12)),
            pltpu.SemaphoreType.DMA((6,)),
            pltpu.SemaphoreType.DMA((1,)),
            pltpu.SemaphoreType.REGULAR,
        ],
        compiler_params=pltpu.CompilerParams(
            collective_id=0, has_side_effects=True, vmem_limit_bytes=32 * 2**20
        ),
    )(
        pin(activations),
        pin(out_grads),
        pin(input_proj.T),
        pin(grad_proj.T),
        example_count,
        pin(child_order.reshape(1, n_dp)),
        pin(prior_sketch),
        pin(fold_map.T),
        pin(merge_mix),
    )
    return pl.pallas_call(
        last_kernel,
        out_shape=(
            jax.ShapeDtypeStruct((rows, columns), f32),
            jax.ShapeDtypeStruct((slots, columns), f32),
        ),
        in_specs=[vmem] * 3,
        out_specs=(anywhere, anywhere),
        scratch_shapes=[pltpu.VMEM((slots, columns), f32), pltpu.SemaphoreType.DMA((2,))],
        compiler_params=pltpu.CompilerParams(vmem_limit_bytes=16 * 2**20),
    )(root, solved, grads)


def from_partner(value, axis, stride):
    mask = 2**stride
    pairs = [(source, source ^ mask) for source in range(lax.axis_size(axis))]
    return lax.ppermute(value, axis, pairs)


def body(
    activations,
    out_grads,
    input_proj,
    grad_proj,
    example_count,
    child_order,
    prior_sketch,
    fold_map,
    merge_mix,
):
    tensor_count = lax.axis_size("tensor")
    own_rank = RANK // tensor_count
    example_slots = activations.shape[0] // SEQ
    sketch_rows = prior_sketch.shape[0]
    input_part = jnp.dot(activations, input_proj, preferred_element_type=jnp.float32)
    grad_part = jnp.dot(out_grads, grad_proj, preferred_element_type=jnp.float32)
    input_side, grad_side = lax.psum((input_part, grad_part), "tensor")
    grad_own = lax.dynamic_slice_in_dim(grad_side, lax.axis_index("tensor") * own_rank, own_rank, 1)
    grad_blocks = grad_own.reshape(example_slots, SEQ, own_rank)
    input_blocks = input_side.reshape(example_slots, SEQ, RANK)
    example_grad = jnp.einsum(
        "eta,etb->eab", grad_blocks, input_blocks, precision=lax.Precision.HIGHEST
    )
    example_grad = example_grad.reshape(example_slots, own_rank * RANK) / jnp.sqrt(jnp.float32(SEQ))
    live = jnp.arange(example_slots, dtype=jnp.int32) < example_count[0]
    example_grad = jnp.where(live[:, None], example_grad, jnp.zeros_like(example_grad))
    leaf_node = prior_sketch + jnp.dot(fold_map, example_grad, precision=lax.Precision.HIGHEST)
    leaf_weight = lax.psum(jnp.sum(leaf_node * leaf_node), "tensor")
    mix_first = merge_mix[:, :sketch_rows]
    mix_second = merge_mix[:, sketch_rows:]
    depth_count = lax.axis_size("dp").bit_length() - 1
    rank_index = lax.axis_index("dp")
    sketch_node = leaf_node
    sketch_weight = leaf_weight
    for level_index in range(depth_count):
        sibling_node, sibling_weight = from_partner((sketch_node, sketch_weight), "dp", level_index)
        upper_half = rank_index >> level_index & 1
        block_start = rank_index >> level_index + 1 << level_index + 1
        flip_order = child_order[block_start + (1 << level_index) - 1]
        own_first = upper_half == flip_order
        first = jnp.where(own_first, sketch_node, sibling_node)
        second = jnp.where(own_first, sibling_node, sketch_node)
        first_weight = jnp.where(own_first, sketch_weight, sibling_weight)
        second_weight = jnp.where(own_first, sibling_weight, sketch_weight)
        mixture = jnp.dot(mix_first, first, precision=lax.Precision.HIGHEST) + jnp.dot(
            mix_second, second, precision=lax.Precision.HIGHEST
        )
        mix_total = lax.psum(jnp.sum(mixture * mixture), "tensor")
        sketch_weight = first_weight + second_weight
        sketch_node = mixture * jnp.sqrt(sketch_weight / (mix_total + 1e-06))
    gram_part = jnp.dot(sketch_node, sketch_node.T, precision=lax.Precision.HIGHEST)
    product_part = jnp.dot(sketch_node, example_grad.T, precision=lax.Precision.HIGHEST)
    gram, sketch_grad = lax.psum((gram_part, product_part), "tensor")
    damping = jnp.trace(gram) / sketch_rows
    system = gram + damping * jnp.eye(sketch_rows, dtype=jnp.float32)
    factor = jnp.linalg.cholesky(system)
    solved = jax.scipy.linalg.cho_solve((factor, True), sketch_grad)
    preconditioned = example_grad - jnp.dot(solved.T, sketch_node, precision=lax.Precision.HIGHEST)
    return (sketch_node, preconditioned)


def fits_fused(rows, columns, slots, n_dp, n_tp):
    return (
        columns == n_dp * LANES
        and slots == n_tp
        and 2 * RANK == LANES
        and n_dp == 8
        and n_tp == 4
        and rows == 2 * LANES
    )


def step(*args):
    n_dp, n_tp = lax.axis_size("dp"), lax.axis_size("tensor")
    slots = args[0].shape[0] // SEQ
    rows, columns = args[6].shape
    if fits_fused(rows, columns, slots, n_dp, n_tp):
        return fused_body(*args)
    return body(*args)


def solution(mesh):
    in_specs = (
        P("dp", "tensor"),
        P("dp", "tensor"),
        P("tensor", None),
        P("tensor", None),
        P("dp"),
        P(),
        P("dp", "tensor"),
        P(),
        P(),
    )
    out_specs = (P(None, "tensor"), P("dp", "tensor"))
    return jax.shard_map(step, mesh=mesh, in_specs=in_specs, out_specs=out_specs, check_vma=False)
```

```python
import functools

import jax
import jax.numpy as jnp
from jax import lax
from jax.experimental import pallas as pl
from jax.experimental.pallas import tpu as pltpu
from jax.sharding import PartitionSpec as P

RANK = 64
SEQ = 128
LANES = 128
HIGHEST = lax.Precision.HIGHEST
MESH = pl.DeviceIdType.MESH


def newton_plan(rows):
    low, high = 0.999, (rows + 1) * 1.001
    first = 2.0 / (low + high)
    reach, scales = first * low, []
    while 1.0 - reach > 1e-3:
        grown = reach * (2.0 - reach)
        scale = 2.0 / (1.0 + grown)
        scales.append(scale)
        reach = grown * scale
    return first, scales


def dot_high(left, right):
    return jnp.dot(left, right, precision=HIGHEST, preferred_element_type=jnp.float32)


def dot_flip(left, right):
    return lax.dot_general(left, right, (((1,), (1,)), ((), ())), preferred_element_type=jnp.float32)


def halves(value):
    high = value.astype(jnp.bfloat16)
    return high, (value - high.astype(jnp.float32)).astype(jnp.bfloat16)


def dot_halves(left, right):
    (a, b), (c, d) = left, right
    out = jnp.dot(a, c, preferred_element_type=jnp.float32)
    out = out + jnp.dot(a, d, preferred_element_type=jnp.float32)
    return out + jnp.dot(b, c, preferred_element_type=jnp.float32)


def dot_mid(left, right):
    return dot_halves(halves(left), halves(right))


def dot_flip_halves(left, right):
    (a, b), (c, d) = left, right
    return dot_flip(jnp.concatenate([a, a, b], axis=1), jnp.concatenate([c, d, c], axis=1))


def dot_rows_halved(left, right):
    (a, b), (c, d) = left, right
    left = jnp.concatenate([a, a, b], axis=1)
    right = jnp.concatenate([c, d, c], axis=0)
    half = left.shape[0] // 2
    return jnp.concatenate(
        [
            jnp.dot(left[:half], right, preferred_element_type=jnp.float32),
            jnp.dot(left[half:], right, preferred_element_type=jnp.float32),
        ],
        axis=0,
    )


def thirds(value):
    high = value.astype(jnp.bfloat16)
    return (high, *halves(value - high.astype(jnp.float32)))


def dot_thirds(left, right):
    count = left.shape[0]
    stack = jnp.concatenate(thirds(left), axis=0)
    a, b, c = (jnp.dot(stack, part, preferred_element_type=jnp.float32) for part in thirds(right))
    high = a[count : 2 * count] + b[:count]
    low = (a[2 * count :] + b[count : 2 * count]) + c[:count]
    return a[:count] + (high + low)


def stacked(value, order):
    high = value.astype(jnp.bfloat16).astype(jnp.float32)
    both = (high, value - high)
    return jnp.concatenate([both[i] for i in order], axis=0)


def solve(gram, target):
    rows = gram.shape[0]
    eye = lax.broadcasted_iota(jnp.int32, gram.shape, 0) == lax.broadcasted_iota(jnp.int32, gram.shape, 1)
    system = gram + jnp.where(eye, 1.0, 0.0)
    first, scales = newton_plan(rows)
    state, solved, path = first * system, first * target, None
    for index, scale in enumerate(scales):
        factor = jnp.where(eye, 2.0 * scale, 0.0) - scale * state
        factor_halves = halves(factor)
        solved = dot_halves(halves(solved), factor_halves)
        if index < len(scales) - 1:
            state = dot_rows_halved(halves(state), factor_halves)
            if path is None:
                path = factor_halves[0]
            else:
                path = jnp.dot(path, factor_halves[0], preferred_element_type=jnp.float32)
                path = path.astype(jnp.bfloat16)
    rest = (first * (target - dot_thirds(solved, system))).astype(jnp.bfloat16)
    step = jnp.dot(rest, path, preferred_element_type=jnp.float32)
    return solved + dot_halves(halves(step), factor_halves)


def fused_kernel(
    n_dp,
    n_tp,
    act_hbm,
    out_hbm,
    wi_hbm,
    wo_hbm,
    count_ref,
    order_hbm,
    prior_hbm,
    fold_hbm,
    mix_hbm,
    root_out,
    solved_out,
    grads_out,
    tokens,
    weights,
    order_ref,
    prior,
    fold_ref,
    mix_ref,
    pair_in,
    node_send,
    node_recv,
    zsend,
    zmid,
    zrecv,
    full,
    slices_send,
    grads,
    grads_rows,
    grads_all,
    peer_all,
    mix_send,
    mix_recv,
    sums_all,
    root,
    gram_part,
    gram_rs,
    gram_z,
    gram_all,
    load_sem,
    sems,
    root_sems,
    out_sem,
    ready_sem,
):
    f32 = jnp.float32
    me, z = lax.axis_index("dp"), lax.axis_index("tensor")
    rows = prior.shape[0]
    levels = n_dp.bit_length() - 1

    def dp_of(k):
        return lax.rem(me + k, n_dp)

    def tp_of(k):
        return lax.rem(z + k, n_tp)

    width = act_hbm.shape[1]
    near = z + 1 - 2 * lax.rem(z, 2)
    far = z + 2 - 4 * (z // 2)
    diagonal = near + 2 - 4 * (near // 2)
    order = (diagonal, far, near, z)
    used = []

    def load(*pairs):
        for source, target in pairs:
            pltpu.make_async_copy(source, target, load_sem.at[len(used)]).start()
        used.append(None)
        return len(used) - 1

    def drain(ref, sem):
        pltpu.make_async_copy(ref, ref, sem).wait()

    def load_chunk(index, start=0, count=SEQ):
        span = pl.ds(pl.multiple_of(order[index] * SEQ + start, count), count)
        into = tokens.at[index, start : start + count]
        return load((act_hbm.at[span], into.at[:, :width]), (out_hbm.at[span], into.at[:, width:]))

    order_load = load((order_hbm, order_ref))
    weight_load = load((wi_hbm, weights.at[:, :width]), (wo_hbm, weights.at[:, width:]))
    mid = SEQ // 2
    half_loads = [load_chunk(0, start, mid) for start in (0, mid)]
    prior_load = load((prior_hbm, prior))
    mix_load = load((mix_hbm, mix_ref))
    chunk_loads = [None] + [load_chunk(index) for index in range(1, n_tp)]
    fold_load = load((fold_hbm, fold_ref))

    def tile_of(owner):
        return pl.ds(pl.multiple_of(owner * LANES, LANES), LANES)

    barrier = pltpu.get_barrier_semaphore()
    for k in range(1, n_tp):
        pl.semaphore_signal(barrier, inc=1, device_id={"tensor": tp_of(k)}, device_id_type=MESH)
    for k in range(1, n_dp):
        pl.semaphore_signal(barrier, inc=1, device_id={"dp": dp_of(k)}, device_id_type=MESH)

    half = n_dp // 2
    core, chip = lax.rem(me, 2), me // 2
    partner = me + 1 - 2 * core
    chip_x = chip + 1 - 2 * lax.rem(chip, 2)
    chip_y = chip + 2 - 4 * (chip // 2)
    chip_d = half - 1 - chip

    PAIR, NODE, MID, SIDE, SLICE, ROW, PEER, SUM, SCATTER, ALONG, GATHER, MIX = range(12)

    def push(phase, source, target, **device):
        pltpu.make_async_remote_copy(
            src_ref=source,
            dst_ref=target,
            send_sem=sems.at[0, phase],
            recv_sem=sems.at[1, phase],
            device_id=device,
            device_id_type=MESH,
        ).start()

    def received(phase, ref):
        drain(ref, sems.at[1, phase])

    z_peers = (diagonal, far, near)
    dp_peers = [2 * other + side for other in (chip_d, chip_x, chip_y) for side in (core, 1 - core)]
    dp_peers.append(partner)

    def exchange(axis, phase, source, target):
        for other in z_peers if axis == "tensor" else dp_peers:
            push(phase, source(other), target, **{axis: other})

    def exchange_all(phase, source, target):
        for t in (*z_peers, z):
            for d in (*dp_peers, me):
                if t is not z or d is not me:
                    push(phase, source(d, t), target, dp=d, tensor=t)

    def sides_of_rows(index, start, count):
        spans = [slice(start + h * count, start + (h + 1) * count) for h in range(2)]
        right = [dot_flip(tokens[index, span, width:], weights[:, width:]) for span in spans]
        left = [dot_flip(tokens[index, span, :width], weights[:, :width]) for span in spans]
        return [jnp.concatenate(pair, axis=1) for pair in zip(left, right)]

    def sides_of_chunk(index):
        drain(tokens.at[index], load_sem.at[chunk_loads[index]])
        return sides_of_rows(index, 0, mid)

    def sides_of_half(h):
        drain(tokens.at[0, h * mid : (h + 1) * mid], load_sem.at[half_loads[h]])
        zsend[h] = jnp.concatenate(sides_of_rows(0, h * mid, mid // 2), axis=0)

    drain(weights, load_sem.at[weight_load])
    sides_of_half(0)
    pl.semaphore_wait(barrier, n_dp + n_tp - 2)
    push(MID, zsend.at[0], zmid, tensor=near)
    for q in range(half):
        push(PAIR, prior_hbm.at[:, tile_of(2 * q + 1 - core)], pair_in.at[q], dp=partner)
    for k in range(1, n_dp):
        pl.semaphore_signal(ready_sem, inc=1, device_id={"dp": dp_of(k)}, device_id_type=MESH)
    sides_of_half(1)
    push(SIDE, zsend.at[1], zrecv.at[4], tensor=diagonal)
    far_sides = sides_of_chunk(1)
    zsend[3] = far_sides[1]
    push(SIDE, zsend.at[3], zrecv.at[3], tensor=far)
    zsend[4], zsend[5] = sides_of_chunk(2)
    push(SIDE, zsend.at[4:6], zrecv.at[0:2], tensor=near)

    drain(order_ref, load_sem.at[order_load])
    drain(prior, load_sem.at[prior_load])
    drain(mix_ref, load_sem.at[mix_load])
    received(PAIR, pair_in)
    first_mix, second_mix = mix_ref[:, :rows], mix_ref[:, rows:]
    own_first = order_ref[0, 2 * chip] == core
    own_half = [prior[:, tile_of(2 * q + core)] for q in range(half)]
    firsts = [jnp.where(own_first, own_half[q], pair_in[q]) for q in range(half)]
    seconds = [jnp.where(own_first, pair_in[q], own_half[q]) for q in range(half)]
    first_halves, second_halves = halves(first_mix), halves(second_mix)
    mixed = dot_halves(first_halves, halves(jnp.concatenate(firsts, axis=1)))
    mixed = mixed + dot_halves(second_halves, halves(jnp.concatenate(seconds, axis=1)))
    for q in range(half):
        node_send[q] = mixed[:, q * LANES : (q + 1) * LANES]
    for other in (chip_x, chip_y, chip_d):
        push(NODE, node_send.at[other], node_recv.at[chip], dp=2 * other + core)
    node_recv[chip] = node_send[chip]
    received(MID, zmid)
    zsend[2] = far_sides[0] + zmid[...]
    push(SIDE, zsend.at[2], zrecv.at[2], tensor=far)
    own_sides = sides_of_chunk(3)

    drain(fold_ref, load_sem.at[fold_load])
    fold_rows = fold_ref[...]

    def through(value):
        count = value.shape[0]
        both = stacked(value, (0, 1)).astype(jnp.bfloat16)
        high = value.astype(jnp.bfloat16)
        results = []
        for top, bottom in (first_halves, second_halves):
            most = dot_flip(both, top)
            results.append(most[:count] + (most[count:] + dot_flip(high, bottom)))
        return results

    paths = [[jnp.concatenate(through(fold_rows), axis=0)]]
    for level in range(1, levels):
        count = paths[-1][0].shape[0]
        mapped = through(jnp.concatenate(paths[-1], axis=0))
        paths.append([v[i : i + count] for v in mapped for i in range(0, v.shape[0], count)])
    paths = [[stacked(p, (0, 0, 1)).T.astype(jnp.bfloat16) for p in level] for level in paths]
    def total(value):
        return jnp.sum(jnp.sum(value, axis=0, keepdims=True), axis=1, keepdims=True)

    fold_gram = [
        [jnp.sum(fold_rows[e : e + 1] * fold_rows[k : k + 1], axis=1, keepdims=True) for k in range(n_tp)]
        for e in range(n_tp)
    ]
    crossed = dot_halves(halves(fold_rows), halves(prior[...]))
    crossed = [
        jnp.concatenate(
            [crossed[e : e + 1, tile * LANES : (tile + 1) * LANES] for tile in range(n_dp)], axis=0
        )
        for e in range(n_tp)
    ]
    prior_square = jnp.zeros((rows, LANES), f32)
    for tile in range(n_dp):
        part = prior[:, tile * LANES : (tile + 1) * LANES]
        prior_square = prior_square + part * part
    prior_mass = total(prior_square)

    received(SIDE, zrecv)
    sides = jnp.concatenate(
        [
            (own_sides[0] + zrecv[0]) + zrecv[2],
            (own_sides[1] + zrecv[1]) + (zrecv[3] + zrecv[4]),
        ],
        axis=0,
    )
    lane = lax.broadcasted_iota(jnp.int32, sides.shape, 1)
    doubled = jnp.where(lane < RANK, sides, pltpu.roll(sides, RANK, 1))
    product = dot_mid(sides.T[RANK:], doubled) / jnp.sqrt(f32(SEQ))
    product = jnp.where(z < count_ref[0], product, jnp.zeros_like(product))
    full[...] = product
    even = full[pl.ds(0, RANK // 2, stride=2), :]
    odd = full[pl.ds(1, RANK // 2, stride=2), :]
    lane = lax.broadcasted_iota(jnp.int32, even.shape, 1)
    mine = jnp.where(lane < RANK, even, odd)
    for row in range(n_tp * n_dp):
        grads_rows[row] = mine[row : row + 1]
    for index in range(n_tp):
        slices_send[index] = mine[index * n_dp : (index + 1) * n_dp]
    grads[z] = slices_send[z]
    slot = me * n_tp + z
    grads_all[slot] = grads_rows[z * n_dp + me]
    pl.semaphore_wait(ready_sem, n_dp - 1)
    exchange("tensor", SLICE, lambda t: slices_send.at[t], grads.at[z])
    exchange_all(ROW, lambda d, t: grads_rows.at[t * n_dp + d], grads_all.at[slot])

    flags = [
        [order_ref[0, j * 2 ** (level + 1) + 2**level - 1] == 1 for j in range(n_dp >> (level + 1))]
        for level in range(levels)
    ]

    def pick(flip, lower, upper):
        first = [jnp.where(flip, b, a) for a, b in zip(lower, upper)]
        return first, [jnp.where(flip, a, b) for a, b in zip(lower, upper)]

    received(SLICE, grads.at[: n_tp - 1])
    steps = [grads[e] for e in range(n_tp)]
    growth = jnp.zeros((n_dp, LANES), f32)
    for e, step in enumerate(steps):
        slope = 2.0 * crossed[e]
        for other, weight in zip(steps, fold_gram[e]):
            slope = slope + weight * other
        growth = growth + step * slope
    own_mass = prior_mass + total(growth)

    received(NODE, node_recv.at[: half - 1])
    mixtures = [[[node_recv[j]] for j in range(half)]]
    for level in range(1, levels):
        below = mixtures[-1]
        sides_of = [pick(flags[level][j], below[2 * j], below[2 * j + 1]) for j in range(len(below) // 2)]
        count = len(below[0])
        left = dot_halves(first_halves, halves(jnp.concatenate([v for f, _ in sides_of for v in f], axis=1)))
        right = dot_halves(second_halves, halves(jnp.concatenate([v for _, g in sides_of for v in g], axis=1)))
        mixtures.append(
            [
                [
                    side[:, (j * count + i) * LANES : (j * count + i + 1) * LANES]
                    for side in (left, right)
                    for i in range(count)
                ]
                for j in range(len(sides_of))
            ]
        )

    for index, part in enumerate(mixtures[-1][0]):
        mix_send[index] = part
    push(MIX, mix_send, mix_recv, dp=partner)

    received(ROW, grads_all.at[: n_tp * n_dp - 1])
    push(PEER, grads_all, peer_all, dp=partner)

    def steps_from(rows_of):
        steps_of = [
            [jnp.concatenate([rows_of[r * n_tp + e] for e in range(n_tp)], axis=0)] for r in range(n_dp)
        ]
        return steps_of, jnp.concatenate([step[0] for step in steps_of], axis=0)

    def merge_steps(level, steps_of):
        merged_steps = []
        for j in range(len(steps_of) // 2):
            first, second = pick(flags[level][j], steps_of[2 * j], steps_of[2 * j + 1])
            if level == 0:
                merged_steps.append([jnp.concatenate([first[0], second[0]], axis=0)])
            else:
                merged_steps.append(first + second)
        return merged_steps

    def updates_of(level, merged_steps):
        return [
            jnp.dot(
                path,
                jnp.concatenate([stacked(g[i], (0, 1, 0)) for g in merged_steps], axis=1).astype(jnp.bfloat16),
                preferred_element_type=f32,
            )
            for i, path in enumerate(paths[level])
        ]

    steps_of, every = steps_from(grads_all)
    sums, products, nodes = [], [], []
    for level in range(levels):
        level_products, level_nodes = [], []
        merged_steps = merge_steps(level, steps_of)
        updates = updates_of(level, merged_steps)
        for j in range(len(merged_steps)):
            parts = [
                v + update[:, j * LANES : (j + 1) * LANES]
                for v, update in zip(mixtures[level][j], updates)
            ]
            index_of = {}
            for a in range(len(parts)):
                for b in range(a + 1):
                    index_of[a, b] = n_dp + len(sums)
                    sums.append(total(parts[a] * parts[b]))
            level_products.append(index_of)
            level_nodes.append(parts)
        steps_of = merged_steps
        products.append(level_products)
        nodes = level_nodes
    lane = lax.broadcasted_iota(jnp.int32, (1, LANES), 1)
    packed = jnp.where(lane == me, own_mass, jnp.zeros((1, LANES), f32))
    for index, value in enumerate(sums):
        packed = jnp.where(lane == n_dp + index, value, packed)
    sums_all[slot] = packed
    exchange_all(SUM, lambda d, t: sums_all.at[slot], sums_all.at[slot])
    for e, step in enumerate(steps):
        for tile in range(n_dp):
            grads_out[e : e + 1, tile * LANES : (tile + 1) * LANES] = step[tile : tile + 1]
    received(PEER, peer_all)
    received(MIX, mix_recv)
    steps_of, peer_every = steps_from(peer_all)
    for level in range(levels):
        steps_of = merge_steps(level, steps_of)
    peer_parts = [mix_recv[i] + update for i, update in enumerate(updates_of(levels - 1, steps_of))]
    every_halves = halves(jnp.concatenate([every, peer_every], axis=1))
    received(SUM, sums_all.at[: n_tp * n_dp - 1])
    parts_of = [sums_all[index] for index in range(n_tp * n_dp)]
    while len(parts_of) > 1:
        parts_of = [a + b for a, b in zip(parts_of[0::2], parts_of[1::2])]
    packed = parts_of[0]

    def summed(index):
        return jnp.sum(jnp.where(lane == index, packed, 0.0), axis=1, keepdims=True)

    masses = [summed(index) for index in range(n_dp)]
    scales = [[jnp.ones((1, 1), f32)] for _ in range(n_dp)]
    for level in range(levels):
        new_masses, new_scales = [], []
        for j, products_of in enumerate(products[level]):
            flip = flags[level][j]
            lower, upper = scales[2 * j], scales[2 * j + 1]
            if level == 0:
                coefs = [jnp.ones((1, 1), f32)]
            else:
                coefs = [jnp.where(flip, b, a) for a, b in zip(lower, upper)]
                coefs += [jnp.where(flip, a, b) for a, b in zip(lower, upper)]
            square = jnp.zeros((1, 1), f32)
            for (a, b), index in products_of.items():
                term = coefs[a] * (coefs[b] * summed(index))
                square = square + (term if a == b else 2.0 * term)
            mass = masses[2 * j] + masses[2 * j + 1]
            scale = jnp.sqrt(mass / (jnp.maximum(square, 0.0) + 1e-06))
            trace = scale * scale * square
            new_masses.append(mass)
            new_scales.append([scale * c for c in coefs])
        masses, scales = new_masses, new_scales
    chunks = []
    for parts in (nodes[0], peer_parts):
        chunk = scales[0][0] * parts[0]
        for c, part in zip(scales[0][1:], parts[1:]):
            chunk = chunk + c * part
        chunks.append(chunk)
    root[:, tile_of(me)] = chunks[0]
    root[:, tile_of(partner)] = chunks[1]

    chunk_halves = halves(jnp.concatenate(chunks, axis=1))
    upper_halves, lower_halves = [[v[s] for v in chunk_halves] for s in (slice(0, LANES), slice(LANES, rows))]
    below = dot_flip_halves(
        [jnp.concatenate(pair, axis=0) for pair in zip(lower_halves, every_halves)], chunk_halves
    )
    targets = below[LANES:]
    unit = rows / trace
    triangle = jnp.concatenate(
        [
            dot_flip_halves(upper_halves, upper_halves),
            below[:LANES, :LANES],
            below[:LANES, LANES:],
        ],
        axis=0,
    )
    own_rows = gram_all.shape[1]
    for r in range(n_dp):
        gram_part[r, :own_rows] = unit * triangle[r * own_rows : (r + 1) * own_rows]
        own = targets[r * n_tp : (r + 1) * n_tp]
        gram_part[r, own_rows:] = unit * jnp.concatenate([own[:, :LANES], own[:, LANES:]], axis=0)
    gram_rs[chip] = gram_part[me]
    for other in (chip_d, chip_x, chip_y):
        push(SCATTER, gram_part.at[2 * other + core], gram_rs.at[chip], dp=2 * other + core)
    dev_x, dev_y, dev_d = (2 * other + core for other in (chip_x, chip_y, chip_d))
    upper, lower = pl.ds(0, rows // 2), pl.ds(rows // 2, rows // 2)

    def relay(index, owner, device, span=slice(None)):
        block_of = root.at[span, tile_of(owner)]
        pltpu.make_async_remote_copy(
            src_ref=block_of,
            dst_ref=block_of,
            send_sem=root_sems.at[5],
            recv_sem=root_sems.at[index],
            device_id={"dp": device},
            device_id_type=MESH,
        ).start()

    def relayed(index, count):
        drain(root.at[:, : count * LANES] if count else root.at[upper, :LANES], root_sems.at[index])

    drain(gram_rs.at[: half - 1], sems.at[0, SCATTER])
    relay(0, me, dev_x)
    relay(1, me, dev_y)
    received(SCATTER, gram_rs.at[: half - 1])
    part = gram_rs[0]
    for index in range(1, half):
        part = part + gram_rs[index]
    gram_z[z] = part
    exchange("tensor", ALONG, lambda t: gram_z.at[z], gram_z.at[z])
    relayed(0, 1)
    relay(2, dev_x, dev_y, upper)
    relay(4, dev_x, partner)
    relayed(1, 1)
    relay(3, dev_y, dev_x, lower)
    relay(4, dev_y, partner)
    received(ALONG, gram_z.at[: n_tp - 1])
    part = gram_z[0]
    for index in range(1, n_tp):
        part = part + gram_z[index]
    gram_all[me] = part[:own_rows]
    target = jnp.concatenate([part[own_rows : own_rows + n_tp], part[own_rows + n_tp :]], axis=1)
    exchange("dp", GATHER, lambda t: gram_all.at[me], gram_all.at[me])
    relayed(2, 0)
    relayed(3, 0)
    relay(4, dev_d, partner)
    for phase, ref in (
        (PAIR, pair_in),
        (NODE, node_recv.at[: half - 1]),
        (MID, zmid),
        (SIDE, zrecv),
        (SLICE, grads.at[: n_tp - 1]),
        (ROW, grads_all.at[: n_tp * n_dp - 1]),
        (SUM, sums_all.at[: n_tp * n_dp - 1]),
        (PEER, peer_all),
        (MIX, mix_recv),
        (ALONG, gram_z.at[: n_tp - 1]),
    ):
        drain(ref, sems.at[0, phase])
    received(GATHER, gram_all.at[: n_dp - 1])
    triangle = jnp.concatenate([gram_all[r] for r in range(n_dp)], axis=0)
    corner = triangle[LANES:rows]
    gram = jnp.concatenate(
        [
            jnp.concatenate([triangle[:LANES], corner.T], axis=1),
            jnp.concatenate([corner, triangle[rows : rows + LANES]], axis=1),
        ],
        axis=0,
    )
    solved_out[...] = solve(gram, target)
    drain(gram_all.at[: n_dp - 1], sems.at[0, GATHER])
    relayed(4, half - 1)
    root_write = pltpu.make_async_copy(root, root_out, out_sem.at[0])
    root_write.start()
    drain(root.at[:, : (n_dp - 2) * LANES], root_sems.at[5])
    root_write.wait()


def last_kernel(root_ref, solved_ref, grads_ref, root_out, pre_out, pre, sem):
    write = pltpu.make_async_copy(root_ref, root_out, sem.at[0])
    write.start()
    pre[...] = grads_ref[...] - dot_mid(solved_ref[...], root_ref[...])
    pre_write = pltpu.make_async_copy(pre, pre_out, sem.at[1])
    pre_write.start()
    write.wait()
    pre_write.wait()


def fused_body(
    activations,
    out_grads,
    input_proj,
    grad_proj,
    example_count,
    child_order,
    prior_sketch,
    fold_map,
    merge_mix,
):
    n_dp, n_tp = lax.axis_size("dp"), lax.axis_size("tensor")
    rows, columns = prior_sketch.shape
    slots = activations.shape[0] // SEQ
    f32, bf16 = jnp.float32, jnp.bfloat16
    width, hidden = activations.shape[1], out_grads.shape[1]
    hbm = pl.BlockSpec(memory_space=pltpu.HBM)
    anywhere = pl.BlockSpec(memory_space=pl.ANY)
    vmem = pl.BlockSpec(memory_space=pltpu.VMEM)
    smem = pl.BlockSpec(memory_space=pltpu.SMEM)
    devices = n_dp * n_tp
    own_rows = 3 * LANES // n_dp
    part_rows = own_rows + 2 * slots
    pin = functools.partial(pltpu.with_memory_space_constraint, memory_space=pltpu.HBM)
    root, solved, grads = pl.pallas_call(
        functools.partial(fused_kernel, n_dp, n_tp),
        out_shape=(
            jax.ShapeDtypeStruct((rows, columns), f32),
            jax.ShapeDtypeStruct((slots, rows), f32),
            jax.ShapeDtypeStruct((slots, columns), f32),
        ),
        in_specs=[hbm, hbm, hbm, hbm, smem, hbm, hbm, hbm, hbm],
        out_specs=(anywhere, vmem, vmem),
        scratch_shapes=[
            pltpu.VMEM((slots, SEQ, width + hidden), bf16),
            pltpu.VMEM((RANK, width + hidden), bf16),
            pltpu.SMEM((1, n_dp), jnp.int32),
            pltpu.VMEM((rows, columns), f32),
            pltpu.VMEM((slots, rows), f32),
            pltpu.VMEM((rows, 2 * rows), f32),
            pltpu.VMEM((n_dp // 2, rows, LANES), f32),
            pltpu.VMEM((n_dp // 2, rows, LANES), f32),
            pltpu.VMEM((n_dp // 2, rows, LANES), f32),
            pltpu.VMEM((6, SEQ // 2, LANES), f32),
            pltpu.VMEM((SEQ // 2, LANES), f32),
            pltpu.VMEM((5, SEQ // 2, LANES), f32),
            pltpu.VMEM((RANK, LANES), f32),
            pltpu.VMEM((n_tp, n_dp, LANES), f32),
            pltpu.VMEM((n_tp, n_dp, LANES), f32),
            pltpu.VMEM((devices, 1, LANES), f32),
            pltpu.VMEM((devices, 1, LANES), f32),
            pltpu.VMEM((devices, 1, LANES), f32),
            pltpu.VMEM((n_dp // 2, rows, LANES), f32),
            pltpu.VMEM((n_dp // 2, rows, LANES), f32),
            pltpu.VMEM((devices, 1, LANES), f32),
            pltpu.VMEM((rows, columns), f32),
            pltpu.VMEM((n_dp, part_rows, LANES), f32),
            pltpu.VMEM((n_dp // 2, part_rows, LANES), f32),
            pltpu.VMEM((n_tp, part_rows, LANES), f32),
            pltpu.VMEM((n_dp, own_rows, LANES), f32),
            pltpu.SemaphoreType.DMA((10,)),
            pltpu.SemaphoreType.DMA((2, 12)),
            pltpu.SemaphoreType.DMA((6,)),
            pltpu.SemaphoreType.DMA((1,)),
            pltpu.SemaphoreType.REGULAR,
        ],
        compiler_params=pltpu.CompilerParams(
            collective_id=0, has_side_effects=True, vmem_limit_bytes=32 * 2**20
        ),
    )(
        pin(activations),
        pin(out_grads),
        pin(input_proj.T),
        pin(grad_proj.T),
        example_count,
        pin(child_order.reshape(1, n_dp)),
        pin(prior_sketch),
        pin(fold_map.T),
        pin(merge_mix),
    )
    return pl.pallas_call(
        last_kernel,
        out_shape=(
            jax.ShapeDtypeStruct((rows, columns), f32),
            jax.ShapeDtypeStruct((slots, columns), f32),
        ),
        in_specs=[vmem] * 3,
        out_specs=(anywhere, anywhere),
        scratch_shapes=[pltpu.VMEM((slots, columns), f32), pltpu.SemaphoreType.DMA((2,))],
        compiler_params=pltpu.CompilerParams(vmem_limit_bytes=16 * 2**20),
    )(root, solved, grads)


def from_partner(value, axis, stride):
    mask = 2**stride
    pairs = [(source, source ^ mask) for source in range(lax.axis_size(axis))]
    return lax.ppermute(value, axis, pairs)


def body(
    activations,
    out_grads,
    input_proj,
    grad_proj,
    example_count,
    child_order,
    prior_sketch,
    fold_map,
    merge_mix,
):
    tensor_count = lax.axis_size("tensor")
    own_rank = RANK // tensor_count
    example_slots = activations.shape[0] // SEQ
    sketch_rows = prior_sketch.shape[0]
    input_part = jnp.dot(activations, input_proj, preferred_element_type=jnp.float32)
    grad_part = jnp.dot(out_grads, grad_proj, preferred_element_type=jnp.float32)
    input_side, grad_side = lax.psum((input_part, grad_part), "tensor")
    grad_own = lax.dynamic_slice_in_dim(grad_side, lax.axis_index("tensor") * own_rank, own_rank, 1)
    grad_blocks = grad_own.reshape(example_slots, SEQ, own_rank)
    input_blocks = input_side.reshape(example_slots, SEQ, RANK)
    example_grad = jnp.einsum(
        "eta,etb->eab", grad_blocks, input_blocks, precision=lax.Precision.HIGHEST
    )
    example_grad = example_grad.reshape(example_slots, own_rank * RANK) / jnp.sqrt(jnp.float32(SEQ))
    live = jnp.arange(example_slots, dtype=jnp.int32) < example_count[0]
    example_grad = jnp.where(live[:, None], example_grad, jnp.zeros_like(example_grad))
    leaf_node = prior_sketch + jnp.dot(fold_map, example_grad, precision=lax.Precision.HIGHEST)
    leaf_weight = lax.psum(jnp.sum(leaf_node * leaf_node), "tensor")
    mix_first = merge_mix[:, :sketch_rows]
    mix_second = merge_mix[:, sketch_rows:]
    depth_count = lax.axis_size("dp").bit_length() - 1
    rank_index = lax.axis_index("dp")
    sketch_node = leaf_node
    sketch_weight = leaf_weight
    for level_index in range(depth_count):
        sibling_node, sibling_weight = from_partner((sketch_node, sketch_weight), "dp", level_index)
        upper_half = rank_index >> level_index & 1
        block_start = rank_index >> level_index + 1 << level_index + 1
        flip_order = child_order[block_start + (1 << level_index) - 1]
        own_first = upper_half == flip_order
        first = jnp.where(own_first, sketch_node, sibling_node)
        second = jnp.where(own_first, sibling_node, sketch_node)
        first_weight = jnp.where(own_first, sketch_weight, sibling_weight)
        second_weight = jnp.where(own_first, sibling_weight, sketch_weight)
        mixture = jnp.dot(mix_first, first, precision=lax.Precision.HIGHEST) + jnp.dot(
            mix_second, second, precision=lax.Precision.HIGHEST
        )
        mix_total = lax.psum(jnp.sum(mixture * mixture), "tensor")
        sketch_weight = first_weight + second_weight
        sketch_node = mixture * jnp.sqrt(sketch_weight / (mix_total + 1e-06))
    gram_part = jnp.dot(sketch_node, sketch_node.T, precision=lax.Precision.HIGHEST)
    product_part = jnp.dot(sketch_node, example_grad.T, precision=lax.Precision.HIGHEST)
    gram, sketch_grad = lax.psum((gram_part, product_part), "tensor")
    damping = jnp.trace(gram) / sketch_rows
    system = gram + damping * jnp.eye(sketch_rows, dtype=jnp.float32)
    factor = jnp.linalg.cholesky(system)
    solved = jax.scipy.linalg.cho_solve((factor, True), sketch_grad)
    preconditioned = example_grad - jnp.dot(solved.T, sketch_node, precision=lax.Precision.HIGHEST)
    return (sketch_node, preconditioned)


def fits_fused(rows, columns, slots, n_dp, n_tp):
    return (
        columns == n_dp * LANES
        and slots == n_tp
        and 2 * RANK == LANES
        and n_dp == 8
        and n_tp == 4
        and rows == 2 * LANES
    )


def step(*args):
    n_dp, n_tp = lax.axis_size("dp"), lax.axis_size("tensor")
    slots = args[0].shape[0] // SEQ
    rows, columns = args[6].shape
    if fits_fused(rows, columns, slots, n_dp, n_tp):
        return fused_body(*args)
    return body(*args)


def solution(mesh):
    in_specs = (
        P("dp", "tensor"),
        P("dp", "tensor"),
        P("tensor", None),
        P("tensor", None),
        P("dp"),
        P(),
        P("dp", "tensor"),
        P(),
        P(),
    )
    out_specs = (P(None, "tensor"), P("dp", "tensor"))
    return jax.shard_map(step, mesh=mesh, in_specs=in_specs, out_specs=out_specs, check_vma=False)
```

```python
import functools

import jax
import jax.numpy as jnp
from jax import lax
from jax.experimental import pallas as pl
from jax.experimental.pallas import tpu as pltpu
from jax.sharding import PartitionSpec as P

RANK = 64
SEQ = 128
LANES = 128
HIGHEST = lax.Precision.HIGHEST
MESH = pl.DeviceIdType.MESH


def newton_plan(rows):
    low, high = 0.999, (rows + 1) * 1.001
    first = 2.0 / (low + high)
    reach, scales = first * low, []
    while 1.0 - reach > 1e-3:
        grown = reach * (2.0 - reach)
        scale = 2.0 / (1.0 + grown)
        scales.append(scale)
        reach = grown * scale
    return first, scales


def dot_high(left, right):
    return jnp.dot(left, right, precision=HIGHEST, preferred_element_type=jnp.float32)


def dot_flip(left, right):
    return lax.dot_general(left, right, (((1,), (1,)), ((), ())), preferred_element_type=jnp.float32)


def halves(value):
    high = value.astype(jnp.bfloat16)
    return high, (value - high.astype(jnp.float32)).astype(jnp.bfloat16)


def dot_halves(left, right):
    (a, b), (c, d) = left, right
    out = jnp.dot(a, c, preferred_element_type=jnp.float32)
    out = out + jnp.dot(a, d, preferred_element_type=jnp.float32)
    return out + jnp.dot(b, c, preferred_element_type=jnp.float32)


def dot_mid(left, right):
    return dot_halves(halves(left), halves(right))


def dot_flip_halves(left, right):
    (a, b), (c, d) = left, right
    return dot_flip(jnp.concatenate([a, a, b], axis=1), jnp.concatenate([c, d, c], axis=1))


def dot_rows_halved(left, right):
    (a, b), (c, d) = left, right
    left = jnp.concatenate([a, a, b], axis=1)
    right = jnp.concatenate([c, d, c], axis=0)
    half = left.shape[0] // 2
    return jnp.concatenate(
        [
            jnp.dot(left[:half], right, preferred_element_type=jnp.float32),
            jnp.dot(left[half:], right, preferred_element_type=jnp.float32),
        ],
        axis=0,
    )


def thirds(value):
    high = value.astype(jnp.bfloat16)
    return (high, *halves(value - high.astype(jnp.float32)))


def dot_thirds(left, right):
    count = left.shape[0]
    stack = jnp.concatenate(thirds(left), axis=0)
    a, b, c = (jnp.dot(stack, part, preferred_element_type=jnp.float32) for part in thirds(right))
    high = a[count : 2 * count] + b[:count]
    low = (a[2 * count :] + b[count : 2 * count]) + c[:count]
    return a[:count] + (high + low)


def stacked(value, order):
    high = value.astype(jnp.bfloat16).astype(jnp.float32)
    both = (high, value - high)
    return jnp.concatenate([both[i] for i in order], axis=0)


def solve(gram, target):
    rows = gram.shape[0]
    eye = lax.broadcasted_iota(jnp.int32, gram.shape, 0) == lax.broadcasted_iota(jnp.int32, gram.shape, 1)
    system = gram + jnp.where(eye, 1.0, 0.0)
    first, scales = newton_plan(rows)
    state, solved, path = first * system, first * target, None
    for index, scale in enumerate(scales):
        factor = jnp.where(eye, 2.0 * scale, 0.0) - scale * state
        factor_halves = halves(factor)
        solved = dot_halves(halves(solved), factor_halves)
        if index < len(scales) - 1:
            state = dot_rows_halved(halves(state), factor_halves)
            if path is None:
                path = factor_halves[0]
            else:
                path = jnp.dot(path, factor_halves[0], preferred_element_type=jnp.float32)
                path = path.astype(jnp.bfloat16)
    rest = (first * (target - dot_thirds(solved, system))).astype(jnp.bfloat16)
    step = jnp.dot(rest, path, preferred_element_type=jnp.float32)
    return solved + dot_halves(halves(step), factor_halves)


def fused_kernel(
    n_dp,
    n_tp,
    act_hbm,
    out_hbm,
    wi_hbm,
    wo_hbm,
    count_ref,
    order_hbm,
    prior_hbm,
    fold_hbm,
    mix_hbm,
    root_out,
    solved_out,
    grads_out,
    tokens,
    weights,
    order_ref,
    prior,
    fold_ref,
    mix_ref,
    pair_in,
    node_send,
    node_recv,
    zsend,
    zmid,
    zrecv,
    full,
    slices_send,
    grads,
    grads_rows,
    grads_all,
    peer_all,
    mix_send,
    mix_recv,
    sums_all,
    root,
    gram_part,
    gram_rs,
    gram_z,
    gram_all,
    sent,
    load_sem,
    sems,
    send_sems,
    root_sems,
    out_sem,
    ready_sem,
):
    f32 = jnp.float32
    me, z = lax.axis_index("dp"), lax.axis_index("tensor")
    rows = prior.shape[0]
    levels = n_dp.bit_length() - 1

    def dp_of(k):
        return lax.rem(me + k, n_dp)

    def tp_of(k):
        return lax.rem(z + k, n_tp)

    width = act_hbm.shape[1]
    near = z + 1 - 2 * lax.rem(z, 2)
    far = z + 2 - 4 * (z // 2)
    diagonal = near + 2 - 4 * (near // 2)
    order = (diagonal, far, near, z)
    used = []

    def load(*pairs):
        for source, target in pairs:
            pltpu.make_async_copy(source, target, load_sem.at[len(used)]).start()
        used.append(None)
        return len(used) - 1

    def drain(ref, sem):
        pltpu.make_async_copy(ref, ref, sem).wait()

    def load_chunk(index, start=0, count=SEQ):
        span = pl.ds(pl.multiple_of(order[index] * SEQ + start, count), count)
        into = tokens.at[index, start : start + count]
        return load((act_hbm.at[span], into.at[:, :width]), (out_hbm.at[span], into.at[:, width:]))

    order_load = load((order_hbm, order_ref))
    weight_load = load((wi_hbm, weights.at[:, :width]), (wo_hbm, weights.at[:, width:]))
    mid = SEQ // 2
    half_loads = [load_chunk(0, start, mid) for start in (0, mid)]
    prior_load = load((prior_hbm, prior))
    mix_load = load((mix_hbm, mix_ref))
    chunk_loads = [None] + [load_chunk(index) for index in range(1, n_tp)]
    fold_load = load((fold_hbm, fold_ref))

    def tile_of(owner):
        return pl.ds(pl.multiple_of(owner * LANES, LANES), LANES)

    barrier = pltpu.get_barrier_semaphore()
    for k in range(1, n_tp):
        pl.semaphore_signal(barrier, inc=1, device_id={"tensor": tp_of(k)}, device_id_type=MESH)
    for k in range(1, n_dp):
        pl.semaphore_signal(barrier, inc=1, device_id={"dp": dp_of(k)}, device_id_type=MESH)

    half = n_dp // 2
    core, chip = lax.rem(me, 2), me // 2
    partner = me + 1 - 2 * core
    chip_x = chip + 1 - 2 * lax.rem(chip, 2)
    chip_y = chip + 2 - 4 * (chip // 2)
    chip_d = half - 1 - chip

    PAIR, NODE, MID, SIDE, SLICE, ROW, PEER, SUM, SCATTER, ALONG, GATHER, MIX = range(12)

    def push(phase, source, target, **device):
        pltpu.make_async_remote_copy(
            src_ref=source,
            dst_ref=target,
            send_sem=send_sems.at[{SCATTER: 1, GATHER: 2}.get(phase, 0)],
            recv_sem=sems.at[phase],
            device_id=device,
            device_id_type=MESH,
        ).start()

    def received(phase, ref):
        drain(ref, sems.at[phase])

    z_peers = (diagonal, far, near)
    dp_peers = [2 * other + side for other in (chip_d, chip_x, chip_y) for side in (core, 1 - core)]
    dp_peers.append(partner)

    def exchange(axis, phase, source, target):
        for other in z_peers if axis == "tensor" else dp_peers:
            push(phase, source(other), target, **{axis: other})

    def exchange_all(phase, source, target):
        for t in (*z_peers, z):
            for d in (*dp_peers, me):
                if t is not z or d is not me:
                    push(phase, source(d, t), target, dp=d, tensor=t)

    def sides_of_rows(index, start, count):
        spans = [slice(start + h * count, start + (h + 1) * count) for h in range(2)]
        right = [dot_flip(tokens[index, span, width:], weights[:, width:]) for span in spans]
        left = [dot_flip(tokens[index, span, :width], weights[:, :width]) for span in spans]
        return [jnp.concatenate(pair, axis=1) for pair in zip(left, right)]

    def sides_of_chunk(index):
        drain(tokens.at[index], load_sem.at[chunk_loads[index]])
        return sides_of_rows(index, 0, mid)

    def sides_of_half(h):
        drain(tokens.at[0, h * mid : (h + 1) * mid], load_sem.at[half_loads[h]])
        zsend[h] = jnp.concatenate(sides_of_rows(0, h * mid, mid // 2), axis=0)

    drain(weights, load_sem.at[weight_load])
    sides_of_half(0)
    pl.semaphore_wait(barrier, n_dp + n_tp - 2)
    push(MID, zsend.at[0], zmid, tensor=near)
    for q in range(half):
        push(PAIR, prior_hbm.at[:, tile_of(2 * q + 1 - core)], pair_in.at[q], dp=partner)
    for k in range(1, n_dp):
        pl.semaphore_signal(ready_sem, inc=1, device_id={"dp": dp_of(k)}, device_id_type=MESH)
    sides_of_half(1)
    push(SIDE, zsend.at[1], zrecv.at[4], tensor=diagonal)
    far_sides = sides_of_chunk(1)
    zsend[3] = far_sides[1]
    push(SIDE, zsend.at[3], zrecv.at[3], tensor=far)
    zsend[4], zsend[5] = sides_of_chunk(2)
    push(SIDE, zsend.at[4:6], zrecv.at[0:2], tensor=near)

    drain(order_ref, load_sem.at[order_load])
    drain(prior, load_sem.at[prior_load])
    drain(mix_ref, load_sem.at[mix_load])
    received(PAIR, pair_in)
    first_mix, second_mix = mix_ref[:, :rows], mix_ref[:, rows:]
    own_first = order_ref[0, 2 * chip] == core
    own_half = [prior[:, tile_of(2 * q + core)] for q in range(half)]
    firsts = [jnp.where(own_first, own_half[q], pair_in[q]) for q in range(half)]
    seconds = [jnp.where(own_first, pair_in[q], own_half[q]) for q in range(half)]
    first_halves, second_halves = halves(first_mix), halves(second_mix)
    mixed = dot_halves(first_halves, halves(jnp.concatenate(firsts, axis=1)))
    mixed = mixed + dot_halves(second_halves, halves(jnp.concatenate(seconds, axis=1)))
    for q in range(half):
        node_send[q] = mixed[:, q * LANES : (q + 1) * LANES]
    for other in (chip_x, chip_y, chip_d):
        push(NODE, node_send.at[other], node_recv.at[chip], dp=2 * other + core)
    node_recv[chip] = node_send[chip]
    received(MID, zmid)
    zsend[2] = far_sides[0] + zmid[...]
    push(SIDE, zsend.at[2], zrecv.at[2], tensor=far)
    own_sides = sides_of_chunk(3)

    drain(fold_ref, load_sem.at[fold_load])
    fold_rows = fold_ref[...]

    def through(value):
        count = value.shape[0]
        both = stacked(value, (0, 1)).astype(jnp.bfloat16)
        high = value.astype(jnp.bfloat16)
        results = []
        for top, bottom in (first_halves, second_halves):
            most = dot_flip(both, top)
            results.append(most[:count] + (most[count:] + dot_flip(high, bottom)))
        return results

    paths = [[jnp.concatenate(through(fold_rows), axis=0)]]
    for level in range(1, levels):
        count = paths[-1][0].shape[0]
        mapped = through(jnp.concatenate(paths[-1], axis=0))
        paths.append([v[i : i + count] for v in mapped for i in range(0, v.shape[0], count)])
    paths = [[stacked(p, (0, 0, 1)).T.astype(jnp.bfloat16) for p in level] for level in paths]
    def total(value):
        return jnp.sum(jnp.sum(value, axis=0, keepdims=True), axis=1, keepdims=True)

    fold_gram = [
        [jnp.sum(fold_rows[e : e + 1] * fold_rows[k : k + 1], axis=1, keepdims=True) for k in range(n_tp)]
        for e in range(n_tp)
    ]
    crossed = dot_halves(halves(fold_rows), halves(prior[...]))
    crossed = [
        jnp.concatenate(
            [crossed[e : e + 1, tile * LANES : (tile + 1) * LANES] for tile in range(n_dp)], axis=0
        )
        for e in range(n_tp)
    ]
    prior_square = jnp.zeros((rows, LANES), f32)
    for tile in range(n_dp):
        part = prior[:, tile * LANES : (tile + 1) * LANES]
        prior_square = prior_square + part * part
    prior_mass = total(prior_square)

    received(SIDE, zrecv)
    sides = jnp.concatenate(
        [
            (own_sides[0] + zrecv[0]) + zrecv[2],
            (own_sides[1] + zrecv[1]) + (zrecv[3] + zrecv[4]),
        ],
        axis=0,
    )
    lane = lax.broadcasted_iota(jnp.int32, sides.shape, 1)
    doubled = jnp.where(lane < RANK, sides, pltpu.roll(sides, RANK, 1))
    product = dot_mid(sides.T[RANK:], doubled) / jnp.sqrt(f32(SEQ))
    product = jnp.where(z < count_ref[0], product, jnp.zeros_like(product))
    full[...] = product
    even = full[pl.ds(0, RANK // 2, stride=2), :]
    odd = full[pl.ds(1, RANK // 2, stride=2), :]
    lane = lax.broadcasted_iota(jnp.int32, even.shape, 1)
    mine = jnp.where(lane < RANK, even, odd)
    for row in range(n_tp * n_dp):
        grads_rows[row] = mine[row : row + 1]
    for index in range(n_tp):
        slices_send[index] = mine[index * n_dp : (index + 1) * n_dp]
    grads[z] = slices_send[z]
    slot = me * n_tp + z
    grads_all[slot] = grads_rows[z * n_dp + me]
    pl.semaphore_wait(ready_sem, n_dp - 1)
    exchange("tensor", SLICE, lambda t: slices_send.at[t], grads.at[z])
    exchange_all(ROW, lambda d, t: grads_rows.at[t * n_dp + d], grads_all.at[slot])

    flags = [
        [order_ref[0, j * 2 ** (level + 1) + 2**level - 1] == 1 for j in range(n_dp >> (level + 1))]
        for level in range(levels)
    ]

    def pick(flip, lower, upper):
        first = [jnp.where(flip, b, a) for a, b in zip(lower, upper)]
        return first, [jnp.where(flip, a, b) for a, b in zip(lower, upper)]

    received(SLICE, grads.at[: n_tp - 1])
    steps = [grads[e] for e in range(n_tp)]
    growth = jnp.zeros((n_dp, LANES), f32)
    for e, step in enumerate(steps):
        slope = 2.0 * crossed[e]
        for other, weight in zip(steps, fold_gram[e]):
            slope = slope + weight * other
        growth = growth + step * slope
    own_mass = prior_mass + total(growth)

    received(NODE, node_recv.at[: half - 1])
    mixtures = [[[node_recv[j]] for j in range(half)]]
    for level in range(1, levels):
        below = mixtures[-1]
        sides_of = [pick(flags[level][j], below[2 * j], below[2 * j + 1]) for j in range(len(below) // 2)]
        count = len(below[0])
        left = dot_halves(first_halves, halves(jnp.concatenate([v for f, _ in sides_of for v in f], axis=1)))
        right = dot_halves(second_halves, halves(jnp.concatenate([v for _, g in sides_of for v in g], axis=1)))
        mixtures.append(
            [
                [
                    side[:, (j * count + i) * LANES : (j * count + i + 1) * LANES]
                    for side in (left, right)
                    for i in range(count)
                ]
                for j in range(len(sides_of))
            ]
        )

    for index, part in enumerate(mixtures[-1][0]):
        mix_send[index] = part
    push(MIX, mix_send, mix_recv, dp=partner)

    received(ROW, grads_all.at[: n_tp * n_dp - 1])
    push(PEER, grads_all, peer_all, dp=partner)

    def steps_from(rows_of):
        steps_of = [
            [jnp.concatenate([rows_of[r * n_tp + e] for e in range(n_tp)], axis=0)] for r in range(n_dp)
        ]
        return steps_of, jnp.concatenate([step[0] for step in steps_of], axis=0)

    def merge_steps(level, steps_of):
        merged_steps = []
        for j in range(len(steps_of) // 2):
            first, second = pick(flags[level][j], steps_of[2 * j], steps_of[2 * j + 1])
            if level == 0:
                merged_steps.append([jnp.concatenate([first[0], second[0]], axis=0)])
            else:
                merged_steps.append(first + second)
        return merged_steps

    def updates_of(level, merged_steps):
        return [
            jnp.dot(
                path,
                jnp.concatenate([stacked(g[i], (0, 1, 0)) for g in merged_steps], axis=1).astype(jnp.bfloat16),
                preferred_element_type=f32,
            )
            for i, path in enumerate(paths[level])
        ]

    steps_of, every = steps_from(grads_all)
    sums, products, nodes = [], [], []
    for level in range(levels):
        level_products, level_nodes = [], []
        merged_steps = merge_steps(level, steps_of)
        updates = updates_of(level, merged_steps)
        for j in range(len(merged_steps)):
            parts = [
                v + update[:, j * LANES : (j + 1) * LANES]
                for v, update in zip(mixtures[level][j], updates)
            ]
            index_of = {}
            for a in range(len(parts)):
                for b in range(a + 1):
                    index_of[a, b] = n_dp + len(sums)
                    sums.append(total(parts[a] * parts[b]))
            level_products.append(index_of)
            level_nodes.append(parts)
        steps_of = merged_steps
        products.append(level_products)
        nodes = level_nodes
    lane = lax.broadcasted_iota(jnp.int32, (1, LANES), 1)
    packed = jnp.where(lane == me, own_mass, jnp.zeros((1, LANES), f32))
    for index, value in enumerate(sums):
        packed = jnp.where(lane == n_dp + index, value, packed)
    sums_all[slot] = packed
    exchange_all(SUM, lambda d, t: sums_all.at[slot], sums_all.at[slot])
    for e, step in enumerate(steps):
        for tile in range(n_dp):
            grads_out[e : e + 1, tile * LANES : (tile + 1) * LANES] = step[tile : tile + 1]
    received(PEER, peer_all)
    received(MIX, mix_recv)
    steps_of, peer_every = steps_from(peer_all)
    for level in range(levels):
        steps_of = merge_steps(level, steps_of)
    peer_parts = [mix_recv[i] + update for i, update in enumerate(updates_of(levels - 1, steps_of))]
    every_halves = halves(jnp.concatenate([every, peer_every], axis=1))
    received(SUM, sums_all.at[: n_tp * n_dp - 1])
    parts_of = [sums_all[index] for index in range(n_tp * n_dp)]
    while len(parts_of) > 1:
        parts_of = [a + b for a, b in zip(parts_of[0::2], parts_of[1::2])]
    packed = parts_of[0]

    def summed(index):
        return jnp.sum(jnp.where(lane == index, packed, 0.0), axis=1, keepdims=True)

    masses = [summed(index) for index in range(n_dp)]
    scales = [[jnp.ones((1, 1), f32)] for _ in range(n_dp)]
    for level in range(levels):
        new_masses, new_scales = [], []
        for j, products_of in enumerate(products[level]):
            flip = flags[level][j]
            lower, upper = scales[2 * j], scales[2 * j + 1]
            if level == 0:
                coefs = [jnp.ones((1, 1), f32)]
            else:
                coefs = [jnp.where(flip, b, a) for a, b in zip(lower, upper)]
                coefs += [jnp.where(flip, a, b) for a, b in zip(lower, upper)]
            square = jnp.zeros((1, 1), f32)
            for (a, b), index in products_of.items():
                term = coefs[a] * (coefs[b] * summed(index))
                square = square + (term if a == b else 2.0 * term)
            mass = masses[2 * j] + masses[2 * j + 1]
            scale = jnp.sqrt(mass / (jnp.maximum(square, 0.0) + 1e-06))
            trace = scale * scale * square
            new_masses.append(mass)
            new_scales.append([scale * c for c in coefs])
        masses, scales = new_masses, new_scales
    chunks = []
    for parts in (nodes[0], peer_parts):
        chunk = scales[0][0] * parts[0]
        for c, part in zip(scales[0][1:], parts[1:]):
            chunk = chunk + c * part
        chunks.append(chunk)
    root[:, tile_of(me)] = chunks[0]
    root[:, tile_of(partner)] = chunks[1]

    chunk_halves = halves(jnp.concatenate(chunks, axis=1))
    upper_halves, lower_halves = [[v[s] for v in chunk_halves] for s in (slice(0, LANES), slice(LANES, rows))]
    below = dot_flip_halves(
        [jnp.concatenate(pair, axis=0) for pair in zip(lower_halves, every_halves)], chunk_halves
    )
    targets = below[LANES:]
    unit = rows / trace
    triangle = jnp.concatenate(
        [
            dot_flip_halves(upper_halves, upper_halves),
            below[:LANES, :LANES],
            below[:LANES, LANES:],
        ],
        axis=0,
    )
    own_rows = gram_all.shape[1]
    for r in range(n_dp):
        gram_part[r, :own_rows] = unit * triangle[r * own_rows : (r + 1) * own_rows]
        own = targets[r * n_tp : (r + 1) * n_tp]
        gram_part[r, own_rows:] = unit * jnp.concatenate([own[:, :LANES], own[:, LANES:]], axis=0)
    gram_rs[chip] = gram_part[me]
    for other in (chip_d, chip_x, chip_y):
        push(SCATTER, gram_part.at[2 * other + core], gram_rs.at[chip], dp=2 * other + core)
    dev_x, dev_y, dev_d = (2 * other + core for other in (chip_x, chip_y, chip_d))
    upper, lower = pl.ds(0, rows // 2), pl.ds(rows // 2, rows // 2)

    def relay(index, owner, device, span=slice(None)):
        block_of = root.at[span, tile_of(owner)]
        pltpu.make_async_remote_copy(
            src_ref=block_of,
            dst_ref=block_of,
            send_sem=root_sems.at[5],
            recv_sem=root_sems.at[index],
            device_id={"dp": device},
            device_id_type=MESH,
        ).start()

    def relayed(index, count):
        drain(root.at[:, : count * LANES] if count else root.at[upper, :LANES], root_sems.at[index])

    drain(gram_rs.at[: half - 1], send_sems.at[1])
    relay(0, me, dev_x)
    relay(1, me, dev_y)
    received(SCATTER, gram_rs.at[: half - 1])
    part = gram_rs[0]
    for index in range(1, half):
        part = part + gram_rs[index]
    gram_z[z] = part
    exchange("tensor", ALONG, lambda t: gram_z.at[z], gram_z.at[z])
    relayed(0, 1)
    relay(2, dev_x, dev_y, upper)
    relay(4, dev_x, partner)
    relayed(1, 1)
    relay(3, dev_y, dev_x, lower)
    relay(4, dev_y, partner)
    received(ALONG, gram_z.at[: n_tp - 1])
    part = gram_z[0]
    for index in range(1, n_tp):
        part = part + gram_z[index]
    gram_all[me] = part[:own_rows]
    target = jnp.concatenate([part[own_rows : own_rows + n_tp], part[own_rows + n_tp :]], axis=1)
    exchange("dp", GATHER, lambda t: gram_all.at[me], gram_all.at[me])
    relayed(2, 0)
    relayed(3, 0)
    relay(4, dev_d, partner)
    drain(sent, send_sems.at[0])
    received(GATHER, gram_all.at[: n_dp - 1])
    triangle = jnp.concatenate([gram_all[r] for r in range(n_dp)], axis=0)
    corner = triangle[LANES:rows]
    gram = jnp.concatenate(
        [
            jnp.concatenate([triangle[:LANES], corner.T], axis=1),
            jnp.concatenate([corner, triangle[rows : rows + LANES]], axis=1),
        ],
        axis=0,
    )
    solved_out[...] = solve(gram, target)
    drain(gram_all.at[: n_dp - 1], send_sems.at[2])
    relayed(4, half - 1)
    root_write = pltpu.make_async_copy(root, root_out, out_sem.at[0])
    root_write.start()
    drain(root.at[:, : (n_dp - 2) * LANES], root_sems.at[5])
    root_write.wait()


def last_kernel(root_ref, solved_ref, grads_ref, root_out, pre_out, pre, sem):
    write = pltpu.make_async_copy(root_ref, root_out, sem.at[0])
    write.start()
    pre[...] = grads_ref[...] - dot_mid(solved_ref[...], root_ref[...])
    pre_write = pltpu.make_async_copy(pre, pre_out, sem.at[1])
    pre_write.start()
    write.wait()
    pre_write.wait()


def fused_body(
    activations,
    out_grads,
    input_proj,
    grad_proj,
    example_count,
    child_order,
    prior_sketch,
    fold_map,
    merge_mix,
):
    n_dp, n_tp = lax.axis_size("dp"), lax.axis_size("tensor")
    rows, columns = prior_sketch.shape
    slots = activations.shape[0] // SEQ
    f32, bf16 = jnp.float32, jnp.bfloat16
    width, hidden = activations.shape[1], out_grads.shape[1]
    hbm = pl.BlockSpec(memory_space=pltpu.HBM)
    anywhere = pl.BlockSpec(memory_space=pl.ANY)
    vmem = pl.BlockSpec(memory_space=pltpu.VMEM)
    smem = pl.BlockSpec(memory_space=pltpu.SMEM)
    devices = n_dp * n_tp
    own_rows = 3 * LANES // n_dp
    part_rows = own_rows + 2 * slots
    whole = (3 * (n_dp // 2) - 1) * rows + 3 * SEQ
    sent_rows = whole + (n_tp - 1) * (n_dp + part_rows) + 3 * devices - 2
    pin = functools.partial(pltpu.with_memory_space_constraint, memory_space=pltpu.HBM)
    root, solved, grads = pl.pallas_call(
        functools.partial(fused_kernel, n_dp, n_tp),
        out_shape=(
            jax.ShapeDtypeStruct((rows, columns), f32),
            jax.ShapeDtypeStruct((slots, rows), f32),
            jax.ShapeDtypeStruct((slots, columns), f32),
        ),
        in_specs=[hbm, hbm, hbm, hbm, smem, hbm, hbm, hbm, hbm],
        out_specs=(anywhere, vmem, vmem),
        scratch_shapes=[
            pltpu.VMEM((slots, SEQ, width + hidden), bf16),
            pltpu.VMEM((RANK, width + hidden), bf16),
            pltpu.SMEM((1, n_dp), jnp.int32),
            pltpu.VMEM((rows, columns), f32),
            pltpu.VMEM((slots, rows), f32),
            pltpu.VMEM((rows, 2 * rows), f32),
            pltpu.VMEM((n_dp // 2, rows, LANES), f32),
            pltpu.VMEM((n_dp // 2, rows, LANES), f32),
            pltpu.VMEM((n_dp // 2, rows, LANES), f32),
            pltpu.VMEM((6, SEQ // 2, LANES), f32),
            pltpu.VMEM((SEQ // 2, LANES), f32),
            pltpu.VMEM((5, SEQ // 2, LANES), f32),
            pltpu.VMEM((RANK, LANES), f32),
            pltpu.VMEM((n_tp, n_dp, LANES), f32),
            pltpu.VMEM((n_tp, n_dp, LANES), f32),
            pltpu.VMEM((devices, 1, LANES), f32),
            pltpu.VMEM((devices, 1, LANES), f32),
            pltpu.VMEM((devices, 1, LANES), f32),
            pltpu.VMEM((n_dp // 2, rows, LANES), f32),
            pltpu.VMEM((n_dp // 2, rows, LANES), f32),
            pltpu.VMEM((devices, 1, LANES), f32),
            pltpu.VMEM((rows, columns), f32),
            pltpu.VMEM((n_dp, part_rows, LANES), f32),
            pltpu.VMEM((n_dp // 2, part_rows, LANES), f32),
            pltpu.VMEM((n_tp, part_rows, LANES), f32),
            pltpu.VMEM((n_dp, own_rows, LANES), f32),
            pltpu.VMEM((sent_rows, 1, LANES), f32),
            pltpu.SemaphoreType.DMA((10,)),
            pltpu.SemaphoreType.DMA((12,)),
            pltpu.SemaphoreType.DMA((3,)),
            pltpu.SemaphoreType.DMA((6,)),
            pltpu.SemaphoreType.DMA((1,)),
            pltpu.SemaphoreType.REGULAR,
        ],
        compiler_params=pltpu.CompilerParams(
            collective_id=0, has_side_effects=True, vmem_limit_bytes=32 * 2**20
        ),
    )(
        pin(activations),
        pin(out_grads),
        pin(input_proj.T),
        pin(grad_proj.T),
        example_count,
        pin(child_order.reshape(1, n_dp)),
        pin(prior_sketch),
        pin(fold_map.T),
        pin(merge_mix),
    )
    return pl.pallas_call(
        last_kernel,
        out_shape=(
            jax.ShapeDtypeStruct((rows, columns), f32),
            jax.ShapeDtypeStruct((slots, columns), f32),
        ),
        in_specs=[vmem] * 3,
        out_specs=(anywhere, anywhere),
        scratch_shapes=[pltpu.VMEM((slots, columns), f32), pltpu.SemaphoreType.DMA((2,))],
        compiler_params=pltpu.CompilerParams(vmem_limit_bytes=16 * 2**20),
    )(root, solved, grads)


def from_partner(value, axis, stride):
    mask = 2**stride
    pairs = [(source, source ^ mask) for source in range(lax.axis_size(axis))]
    return lax.ppermute(value, axis, pairs)


def body(
    activations,
    out_grads,
    input_proj,
    grad_proj,
    example_count,
    child_order,
    prior_sketch,
    fold_map,
    merge_mix,
):
    tensor_count = lax.axis_size("tensor")
    own_rank = RANK // tensor_count
    example_slots = activations.shape[0] // SEQ
    sketch_rows = prior_sketch.shape[0]
    input_part = jnp.dot(activations, input_proj, preferred_element_type=jnp.float32)
    grad_part = jnp.dot(out_grads, grad_proj, preferred_element_type=jnp.float32)
    input_side, grad_side = lax.psum((input_part, grad_part), "tensor")
    grad_own = lax.dynamic_slice_in_dim(grad_side, lax.axis_index("tensor") * own_rank, own_rank, 1)
    grad_blocks = grad_own.reshape(example_slots, SEQ, own_rank)
    input_blocks = input_side.reshape(example_slots, SEQ, RANK)
    example_grad = jnp.einsum(
        "eta,etb->eab", grad_blocks, input_blocks, precision=lax.Precision.HIGHEST
    )
    example_grad = example_grad.reshape(example_slots, own_rank * RANK) / jnp.sqrt(jnp.float32(SEQ))
    live = jnp.arange(example_slots, dtype=jnp.int32) < example_count[0]
    example_grad = jnp.where(live[:, None], example_grad, jnp.zeros_like(example_grad))
    leaf_node = prior_sketch + jnp.dot(fold_map, example_grad, precision=lax.Precision.HIGHEST)
    leaf_weight = lax.psum(jnp.sum(leaf_node * leaf_node), "tensor")
    mix_first = merge_mix[:, :sketch_rows]
    mix_second = merge_mix[:, sketch_rows:]
    depth_count = lax.axis_size("dp").bit_length() - 1
    rank_index = lax.axis_index("dp")
    sketch_node = leaf_node
    sketch_weight = leaf_weight
    for level_index in range(depth_count):
        sibling_node, sibling_weight = from_partner((sketch_node, sketch_weight), "dp", level_index)
        upper_half = rank_index >> level_index & 1
        block_start = rank_index >> level_index + 1 << level_index + 1
        flip_order = child_order[block_start + (1 << level_index) - 1]
        own_first = upper_half == flip_order
        first = jnp.where(own_first, sketch_node, sibling_node)
        second = jnp.where(own_first, sibling_node, sketch_node)
        first_weight = jnp.where(own_first, sketch_weight, sibling_weight)
        second_weight = jnp.where(own_first, sibling_weight, sketch_weight)
        mixture = jnp.dot(mix_first, first, precision=lax.Precision.HIGHEST) + jnp.dot(
            mix_second, second, precision=lax.Precision.HIGHEST
        )
        mix_total = lax.psum(jnp.sum(mixture * mixture), "tensor")
        sketch_weight = first_weight + second_weight
        sketch_node = mixture * jnp.sqrt(sketch_weight / (mix_total + 1e-06))
    gram_part = jnp.dot(sketch_node, sketch_node.T, precision=lax.Precision.HIGHEST)
    product_part = jnp.dot(sketch_node, example_grad.T, precision=lax.Precision.HIGHEST)
    gram, sketch_grad = lax.psum((gram_part, product_part), "tensor")
    damping = jnp.trace(gram) / sketch_rows
    system = gram + damping * jnp.eye(sketch_rows, dtype=jnp.float32)
    factor = jnp.linalg.cholesky(system)
    solved = jax.scipy.linalg.cho_solve((factor, True), sketch_grad)
    preconditioned = example_grad - jnp.dot(solved.T, sketch_node, precision=lax.Precision.HIGHEST)
    return (sketch_node, preconditioned)


def fits_fused(rows, columns, slots, n_dp, n_tp):
    return (
        columns == n_dp * LANES
        and slots == n_tp
        and 2 * RANK == LANES
        and n_dp == 8
        and n_tp == 4
        and rows == 2 * LANES
    )


def step(*args):
    n_dp, n_tp = lax.axis_size("dp"), lax.axis_size("tensor")
    slots = args[0].shape[0] // SEQ
    rows, columns = args[6].shape
    if fits_fused(rows, columns, slots, n_dp, n_tp):
        return fused_body(*args)
    return body(*args)


def solution(mesh):
    in_specs = (
        P("dp", "tensor"),
        P("dp", "tensor"),
        P("tensor", None),
        P("tensor", None),
        P("dp"),
        P(),
        P("dp", "tensor"),
        P(),
        P(),
    )
    out_specs = (P(None, "tensor"), P("dp", "tensor"))
    return jax.shard_map(step, mesh=mesh, in_specs=in_specs, out_specs=out_specs, check_vma=False)
```
